256 devices in a mesh: dp: 16 (over z_lo, x, core), frame: 16 (over y, z_hi).
Axes of the slice: x: 4, y: 4, z: 8 (z_hi: 4, z_lo: 2; z = z_hi * 2 + z_lo), core: 2. Of those that a mesh axis runs over, the one named last changes fastest.
Arguments:
- clips: bfloat16 [16, 32, 16, 32, 320], P('dp', 'frame'), may hold values from -15 to 15
- cotangent: bfloat16 [16, 32, 16, 32, 320], P('dp', 'frame'), may hold values from -6 to 6
- spatial_weight: bfloat16 [3, 3, 320, 320], replicated, may hold values from -0.109375 to 0.109375
- temporal_weight: bfloat16 [3, 320, 320], replicated, may hold values from -0.1875 to 0.1875
- gain_one: float32 [320], replicated, may hold values from 0.1 to 1.9
- gain_two: float32 [320], replicated, may hold values from 0.1 to 1.9
Outputs:
- output: bfloat16 [16, 32, 16, 32, 320], P('dp', 'frame')
- input_grad: bfloat16 [16, 32, 16, 32, 320], P('dp', 'frame')
- spatial_grad: bfloat16 [3, 3, 320, 320], replicated
- temporal_grad: bfloat16 [3, 320, 320], replicated
The draws below stay inside these ranges and needn't reach their ends.
All inputs are finite; a program needn't handle non-finite values.
Results may differ from the reference program's by a relative error of at most 0.0035.
The reference program's roundings to bfloat16 on the way (of `acts`, `hidden`, `mixed`, `temporal`, `mixed_grad` and `hidden_low`) count: a program that leaves them out, or rounds other values in their place, can miss the bound.
Values may be sent and summed in bfloat16 or wider, within the bound.
No kernel may reach another device: no remote copies, remote signals or barrier semaphores. Data moves between devices by JAX's collectives and lax.ppermute only.
A program may use at most 64 MiB of HBM per device.

```python
import jax
import jax.numpy as jnp
from jax import lax

CHANNELS = 320
GROUPS = 32
COLUMNS = 32
FRAMES = 32
ROWS = 16
CLIPS = 16


def draw_clips(key, part):
    first, second = jax.random.split(key, 2)
    shape = (CLIPS, FRAMES, ROWS, COLUMNS, CHANNELS)
    frame_scale = 0.6 + 1.2 * jnp.arange(FRAMES, dtype=jnp.float32) / max(FRAMES - 1, 1)
    channel_scale = jnp.exp(jax.random.uniform(second, (CHANNELS,), jnp.float32, -0.7, 0.7))
    base = jnp.clip(jax.random.normal(first, shape, jnp.float32), -4.0, 4.0)
    return (base * frame_scale[None, :, None, None, None] * channel_scale).astype(jnp.bfloat16)


def shard_levels(rng, dims, cuts, least, high):
    level = 1.0
    for position, shards_of in cuts:
        steps = jax.random.uniform(jax.random.fold_in(jax.random.fold_in(rng, 6), position), (shards_of,), jnp.float32, least / len(cuts), high / len(cuts))
        level = level * jnp.repeat(jnp.exp(steps), dims[position] // shards_of).reshape((-1,) + (1,) * (len(dims) - 1 - position))
    return level


def bell_draw(stream_key, shape, spread, bound, shards=(), kind=jnp.bfloat16):
    entries = jax.random.normal(stream_key, shape, jnp.float32) * spread
    if len(shards) > 0:
        entries = shard_levels(stream_key, shape, shards, -0.22, 0.18) * entries
    return jnp.clip(entries, min=-bound, max=bound).astype(kind)


def setup_inputs(seed: int = 0) -> dict:
    keys = jax.random.split(jax.random.key(seed), 7)
    return {
        "clips": draw_clips(jax.random.fold_in(keys[6], 71), 0),
        "cotangent": bell_draw(keys[1], (CLIPS, FRAMES, ROWS, COLUMNS, CHANNELS), 1.0, 6.0, ((0, 16), (1, 16))),
        "spatial_weight": bell_draw(keys[2], (3, 3, CHANNELS, CHANNELS), (9 * CHANNELS) ** -0.5, 0.109375),
        "temporal_weight": bell_draw(keys[3], (3, CHANNELS, CHANNELS), (3 * CHANNELS) ** -0.5, 0.1875),
        "gain_one": jnp.clip(1.0 + 0.18 * jax.random.normal(keys[4], (CHANNELS,), jnp.float32), 0.1, 1.9),
        "gain_two": jnp.clip(1.0 + 0.18 * jax.random.normal(keys[5], (CHANNELS,), jnp.float32), 0.1, 1.9),
    }


epsilon = 1e-05

def silu_slope(value):
    sigma = jax.nn.sigmoid(value)
    return sigma * (1.0 + value * (1.0 - sigma))

def group_view(value, groups):
    return value.reshape(value.shape[:-1] + (groups, value.shape[-1] // groups))

def spatial_conv(acts, weight):
    height, width = (acts.shape[1], acts.shape[2])
    padded = jnp.pad(acts, ((0, 0), (1, 1), (1, 1), (0, 0)))
    total = jnp.zeros(acts.shape[:-1] + (weight.shape[-1],), jnp.float32)
    for row_tap in range(3):
        for col_tap in range(3):
            window = padded[:, row_tap:row_tap + height, col_tap:col_tap + width, :]
            total = total + jnp.dot(window, weight[row_tap, col_tap], preferred_element_type=jnp.float32)
    return total

def spatial_back(grads, acts, weight):
    height, width, chans = (acts.shape[1], acts.shape[2], acts.shape[3])
    padded = jnp.pad(acts, ((0, 0), (1, 1), (1, 1), (0, 0)))
    grad_pad = jnp.pad(grads, ((0, 0), (1, 1), (1, 1), (0, 0)))
    flat_grads = grads.reshape(-1, grads.shape[-1])
    acts_grad = jnp.zeros(acts.shape, jnp.float32)
    pieces = []
    for row_tap in range(3):
        for col_tap in range(3):
            moved = grad_pad[:, 2 - row_tap:2 - row_tap + height, 2 - col_tap:2 - col_tap + width, :]
            acts_grad = acts_grad + jnp.dot(moved, weight[row_tap, col_tap].T, preferred_element_type=jnp.float32)
            window = padded[:, row_tap:row_tap + height, col_tap:col_tap + width, :].reshape(-1, chans)
            pieces.append(jnp.dot(window.T, flat_grads, preferred_element_type=jnp.float32))
    return (acts_grad, jnp.stack(pieces).reshape(3, 3, chans, -1))

def temporal_conv(padded, weight):
    length = padded.shape[0] - 2
    total = jnp.zeros((length,) + padded.shape[1:-1] + (weight.shape[-1],), jnp.float32)
    for frame_tap in range(3):
        total = total + jnp.dot(padded[frame_tap:frame_tap + length], weight[frame_tap], preferred_element_type=jnp.float32)
    return total

def temporal_back(grad_pad, padded, weight):
    length = padded.shape[0] - 2
    chans = padded.shape[-1]
    grads = grad_pad[1:1 + length].reshape(-1, grad_pad.shape[-1])
    mixed_grad = jnp.zeros((length,) + padded.shape[1:], jnp.float32)
    pieces = []
    for frame_tap in range(3):
        moved = grad_pad[2 - frame_tap:2 - frame_tap + length]
        mixed_grad = mixed_grad + jnp.dot(moved, weight[frame_tap].T, preferred_element_type=jnp.float32)
        window = padded[frame_tap:frame_tap + length].reshape(-1, chans)
        pieces.append(jnp.dot(window.T, grads, preferred_element_type=jnp.float32))
    return (mixed_grad, jnp.stack(pieces))

def frame_pad(value):
    return jnp.pad(value, ((1, 1), (0, 0), (0, 0), (0, 0)))

def clip_pass(single, single_grad, spatial_weight, temporal_weight, gain_one, gain_two):
    groups = GROUPS
    inputs = single.astype(jnp.float32)
    view_one = group_view(inputs, groups)
    mean_one = lax.optimization_barrier(jnp.mean(view_one, axis=(1, 2, 4), keepdims=True))
    var_one = lax.optimization_barrier(jnp.mean(view_one * view_one, axis=(1, 2, 4), keepdims=True)) - mean_one * mean_one
    inv_one = lax.rsqrt(var_one + epsilon)
    hat_one = ((view_one - mean_one) * inv_one).reshape(inputs.shape)
    pre_one = hat_one * gain_one
    acts = jax.nn.silu(pre_one).astype(jnp.bfloat16)
    hidden = (inputs + spatial_conv(acts, spatial_weight)).astype(jnp.bfloat16)
    hidden_full = hidden.astype(jnp.float32)
    view_two = group_view(hidden_full, groups)
    mean_two = lax.optimization_barrier(jnp.mean(view_two, axis=(0, 1, 2, 4), keepdims=True))
    var_two = lax.optimization_barrier(jnp.mean(view_two * view_two, axis=(0, 1, 2, 4), keepdims=True)) - mean_two * mean_two
    inv_two = lax.rsqrt(var_two + epsilon)
    hat_two = ((view_two - mean_two) * inv_two).reshape(inputs.shape)
    pre_two = hat_two * gain_two
    mixed = jax.nn.silu(pre_two).astype(jnp.bfloat16)
    mixed_pad = frame_pad(mixed)
    temporal = temporal_conv(mixed_pad, temporal_weight).astype(jnp.bfloat16)
    output = (hidden_full + temporal.astype(jnp.float32)).astype(jnp.bfloat16)
    mixed_grad, temporal_sum = temporal_back(frame_pad(single_grad), mixed_pad, temporal_weight)
    mixed_grad = mixed_grad.astype(jnp.bfloat16)
    dhat_two = mixed_grad.astype(jnp.float32) * silu_slope(pre_two) * gain_two
    grad_view = group_view(dhat_two, groups)
    hat_view = group_view(hat_two, groups)
    first = lax.optimization_barrier(jnp.mean(grad_view, axis=(0, 1, 2, 4), keepdims=True))
    second = lax.optimization_barrier(jnp.mean(grad_view * hat_view, axis=(0, 1, 2, 4), keepdims=True))
    hidden_grad = single_grad.astype(jnp.float32) + (inv_two * (grad_view - first - hat_view * second)).reshape(inputs.shape)
    hidden_low = hidden_grad.astype(jnp.bfloat16)
    acts_grad, spatial_sum = spatial_back(hidden_low, acts, spatial_weight)
    dhat_one = acts_grad * silu_slope(pre_one) * gain_one
    grad_one = group_view(dhat_one, groups)
    hat_onev = group_view(hat_one, groups)
    first_one = lax.optimization_barrier(jnp.mean(grad_one, axis=(1, 2, 4), keepdims=True))
    second_one = lax.optimization_barrier(jnp.mean(grad_one * hat_onev, axis=(1, 2, 4), keepdims=True))
    input_grad = (hidden_grad + (inv_one * (grad_one - first_one - hat_onev * second_one)).reshape(inputs.shape)).astype(jnp.bfloat16)
    return (output, input_grad, spatial_sum, temporal_sum)

def reference(clips, cotangent, spatial_weight, temporal_weight, gain_one, gain_two):
    chans = clips.shape[-1]

    def advance(carry, pair):
        output, input_grad, spatial_sum, temporal_sum = clip_pass(pair[0], pair[1], spatial_weight, temporal_weight, gain_one, gain_two)
        return ((carry[0] + spatial_sum, carry[1] + temporal_sum), (output, input_grad))
    start = (jnp.zeros((3, 3, chans, chans), jnp.float32), jnp.zeros((3, chans, chans), jnp.float32))
    totals, results = lax.scan(advance, start, (clips, cotangent))
    return (results[0], results[1], totals[0].astype(jnp.bfloat16), totals[1].astype(jnp.bfloat16))
```

```python
import jax
import jax.numpy as jnp
from jax import lax
from jax.sharding import Mesh, PartitionSpec as P

GROUPS = 32


epsilon = 1e-05

DP = ("zl", "x", "c")
FRAME = ("y", "zh")
PLANE = ("x", "y")
LINE = ("zl", "zh")


def silu_slope(value):
    sigma = jax.nn.sigmoid(value)
    return sigma * (1.0 + value * (1.0 - sigma))


def group_view(value, groups):
    return value.reshape(value.shape[:-1] + (groups, value.shape[-1] // groups))


def spatial_conv(acts, weight):
    height, width = (acts.shape[1], acts.shape[2])
    padded = jnp.pad(acts, ((0, 0), (1, 1), (1, 1), (0, 0)))
    total = jnp.zeros(acts.shape[:-1] + (weight.shape[-1],), jnp.float32)
    for row_tap in range(3):
        for col_tap in range(3):
            window = padded[:, row_tap : row_tap + height, col_tap : col_tap + width, :]
            total = total + jnp.dot(
                window, weight[row_tap, col_tap], preferred_element_type=jnp.float32
            )
    return total


def spatial_back(grads, acts, weight):
    height, width, chans = (acts.shape[1], acts.shape[2], acts.shape[3])
    padded = jnp.pad(acts, ((0, 0), (1, 1), (1, 1), (0, 0)))
    grad_pad = jnp.pad(grads, ((0, 0), (1, 1), (1, 1), (0, 0)))
    flat_grads = grads.reshape(-1, grads.shape[-1])
    acts_grad = jnp.zeros(acts.shape, jnp.float32)
    pieces = []
    for row_tap in range(3):
        for col_tap in range(3):
            moved = grad_pad[
                :, 2 - row_tap : 2 - row_tap + height, 2 - col_tap : 2 - col_tap + width, :
            ]
            acts_grad = acts_grad + jnp.dot(
                moved, weight[row_tap, col_tap].T, preferred_element_type=jnp.float32
            )
            window = padded[:, row_tap : row_tap + height, col_tap : col_tap + width, :].reshape(
                -1, chans
            )
            pieces.append(jnp.dot(window.T, flat_grads, preferred_element_type=jnp.float32))
    return (acts_grad, pieces)


def temporal_conv(padded, weight):
    length = padded.shape[0] - 2
    total = jnp.zeros((length,) + padded.shape[1:-1] + (weight.shape[-1],), jnp.float32)
    for frame_tap in range(3):
        total = total + jnp.dot(
            padded[frame_tap : frame_tap + length],
            weight[frame_tap],
            preferred_element_type=jnp.float32,
        )
    return total


def temporal_back(grad_pad, padded, weight):
    length = padded.shape[0] - 2
    chans = padded.shape[-1]
    grads = grad_pad[1 : 1 + length].reshape(-1, grad_pad.shape[-1])
    mixed_grad = jnp.zeros((length,) + padded.shape[1:], jnp.float32)
    pieces = []
    for frame_tap in range(3):
        moved = grad_pad[2 - frame_tap : 2 - frame_tap + length]
        mixed_grad = mixed_grad + jnp.dot(
            moved, weight[frame_tap].T, preferred_element_type=jnp.float32
        )
        window = padded[frame_tap : frame_tap + length].reshape(-1, chans)
        pieces.append(jnp.dot(window.T, grads, preferred_element_type=jnp.float32))
    return (mixed_grad, pieces)


def neighbours(value):
    size = lax.axis_size(FRAME)
    before = lax.ppermute(value[1], FRAME, [(i, i + 1) for i in range(size - 1)])
    after = lax.ppermute(value[0], FRAME, [(i + 1, i) for i in range(size - 1)])
    return before, after


def frame_total(first, second):
    size = lax.axis_size(FRAME)
    packed = jnp.concatenate([first, second])[None, None]
    spread = jnp.broadcast_to(packed, (size, 1, packed.shape[-1]))
    total = jnp.sum(lax.all_to_all(spread, FRAME, 0, 0), axis=(0, 1))
    return total[: first.shape[0]], total[first.shape[0] :]


def everyone_total(value):
    core = lax.axis_index("c")
    rows, width = value.shape
    half = width // 2
    left, right = value[:, :half], value[:, half:]
    keep = jnp.where(core == 0, left, right)
    give = jnp.where(core == 0, right, left)
    value = keep + lax.ppermute(give, "c", [(0, 1), (1, 0)])
    plane = lax.axis_size(PLANE)
    line = lax.axis_size(LINE)
    value = value.reshape(plane, rows // plane, half)
    value = jnp.pad(value, ((0, 0), (0, 64 - rows // plane), (0, 0)))
    value = jnp.sum(lax.all_to_all(value, PLANE, 0, 0), axis=0)
    value = value.reshape(line, 64 // line, half)
    value = jnp.sum(lax.all_to_all(value, LINE, 0, 0), axis=0)
    value = value.astype(jnp.bfloat16)
    value = jnp.broadcast_to(value[None], (line,) + value.shape)
    value = lax.all_to_all(value, LINE, 0, 0).reshape(64, half)
    value = jnp.broadcast_to(value[None], (plane,) + value.shape)
    value = lax.all_to_all(value, PLANE, 0, 0)
    other = lax.ppermute(value, "c", [(0, 1), (1, 0)])
    left = jnp.where(core == 0, value, other)
    right = jnp.where(core == 0, other, value)
    both = jnp.concatenate([left, right], axis=-1)
    return both[:, : rows // plane].reshape(rows, width)


def on_device(clips, cotangent, spatial_weight, temporal_weight, gain_one, gain_two):
    groups = GROUPS
    single = clips[0]
    single_grad = cotangent[0]
    chans = single.shape[-1]
    place = lax.axis_index(FRAME)
    grad_before, grad_after = neighbours(single_grad)
    inputs = single.astype(jnp.float32)
    view_one = group_view(inputs, groups)
    mean_one = jnp.mean(view_one, axis=(1, 2, 4), keepdims=True)
    var_one = jnp.mean(view_one * view_one, axis=(1, 2, 4), keepdims=True) - mean_one * mean_one
    inv_one = lax.rsqrt(var_one + epsilon)
    hat_one = ((view_one - mean_one) * inv_one).reshape(inputs.shape)
    pre_one = hat_one * gain_one
    acts = jax.nn.silu(pre_one).astype(jnp.bfloat16)
    hidden = (inputs + spatial_conv(acts, spatial_weight)).astype(jnp.bfloat16)
    hidden_before, hidden_after = neighbours(hidden)
    hidden_full = hidden.astype(jnp.float32)
    view_two = group_view(hidden_full, groups)
    count = (
        view_two.shape[0]
        * lax.axis_size(FRAME)
        * view_two.shape[1]
        * view_two.shape[2]
        * view_two.shape[4]
    )
    local_sums = jnp.sum(view_two, axis=(0, 1, 2, 4))
    local_squares = jnp.sum(view_two * view_two, axis=(0, 1, 2, 4))
    total_sums, total_squares = frame_total(local_sums, local_squares)
    mean_two = (total_sums / count)[:, None]
    var_two = (total_squares / count)[:, None] - mean_two * mean_two
    inv_two = lax.rsqrt(var_two + epsilon)

    def normal_two(value):
        view = group_view(value.astype(jnp.float32), groups)
        hat = ((view - mean_two) * inv_two).reshape(value.shape)
        return hat, hat * gain_two

    hat_two, pre_two = normal_two(hidden)
    mixed = jax.nn.silu(pre_two).astype(jnp.bfloat16)
    mixed_before = jax.nn.silu(normal_two(hidden_before)[1]).astype(jnp.bfloat16)
    mixed_after = jax.nn.silu(normal_two(hidden_after)[1]).astype(jnp.bfloat16)
    mixed_before = jnp.where(place > 0, mixed_before, jnp.zeros_like(mixed_before))
    mixed_after = jnp.where(
        place < lax.axis_size(FRAME) - 1, mixed_after, jnp.zeros_like(mixed_after)
    )
    mixed_pad = jnp.concatenate([mixed_before[None], mixed, mixed_after[None]])
    grad_pad = jnp.concatenate([grad_before[None], single_grad, grad_after[None]])
    temporal = temporal_conv(mixed_pad, temporal_weight).astype(jnp.bfloat16)
    mixed_grad, temporal_pieces = temporal_back(grad_pad, mixed_pad, temporal_weight)
    mixed_grad = mixed_grad.astype(jnp.bfloat16)
    output = (hidden_full + temporal.astype(jnp.float32)).astype(jnp.bfloat16)
    dhat_two = mixed_grad.astype(jnp.float32) * silu_slope(pre_two) * gain_two
    grad_view = group_view(dhat_two, groups)
    hat_view = group_view(hat_two, groups)
    local_first = jnp.sum(grad_view, axis=(0, 1, 2, 4))
    local_second = jnp.sum(grad_view * hat_view, axis=(0, 1, 2, 4))
    total_first, total_second = frame_total(local_first, local_second)
    first = (total_first / count)[:, None]
    second = (total_second / count)[:, None]
    hidden_grad = single_grad.astype(jnp.float32) + (
        inv_two * (grad_view - first - hat_view * second)
    ).reshape(inputs.shape)
    hidden_low = hidden_grad.astype(jnp.bfloat16)
    acts_grad, spatial_pieces = spatial_back(hidden_low, acts, spatial_weight)
    pieces = [jnp.stack(spatial_pieces[3 * i : 3 * i + 3]) for i in range(3)]
    pieces.append(jnp.stack(temporal_pieces))
    halves = [
        jnp.concatenate([p[..., at : at + chans // 2] for p in pieces], axis=-1)
        for at in (0, chans // 2)
    ]
    packed = jnp.concatenate(halves, axis=-1).reshape(3 * chans, 4 * chans)
    totals = everyone_total(packed)
    totals = totals.reshape(3, chans, 2, 4, chans // 2).transpose(3, 0, 1, 2, 4)
    totals = totals.reshape(4, 3, chans, chans)
    dhat_one = acts_grad * silu_slope(pre_one) * gain_one
    grad_one = group_view(dhat_one, groups)
    hat_onev = group_view(hat_one, groups)
    first_one = jnp.mean(grad_one, axis=(1, 2, 4), keepdims=True)
    second_one = jnp.mean(grad_one * hat_onev, axis=(1, 2, 4), keepdims=True)
    input_grad = (
        hidden_grad
        + (inv_one * (grad_one - first_one - hat_onev * second_one)).reshape(inputs.shape)
    ).astype(jnp.bfloat16)
    return output[None], input_grad[None], totals[:3], totals[3]


def solution(mesh):
    fine = Mesh(mesh.devices.reshape(2, 4, 2, 4, 4), ("zl", "x", "c", "y", "zh"))
    return jax.shard_map(
        on_device,
        mesh=fine,
        in_specs=(P(DP, FRAME), P(DP, FRAME), P(), P(), P(), P()),
        out_specs=(P(DP, FRAME), P(DP, FRAME), P(), P()),
        check_vma=False,
    )
```

```python
import functools

import jax
import jax.numpy as jnp
from jax import lax
from jax.experimental import pallas as pl
from jax.experimental.pallas import tpu as pltpu
from jax.sharding import Mesh, PartitionSpec as P

epsilon = 1e-05

GROUPS = 32
DP = ("zl", "x", "c")
FRAME = ("y", "zh")
PLANE = ("x", "y")
LINE = ("zl", "zh")

C = 320
W = 32
PAD = 384
HALF = C // 2
PIX = 512
ROWS = 2 * PIX
STEP = 128
F32 = jnp.float32
BF16 = jnp.bfloat16

PARAMS = pltpu.CompilerParams(vmem_limit_bytes=56 * 1024 * 1024)


def call(body, out, scratch=(), flops=0):
    return pl.pallas_call(
        body,
        out_shape=out,
        scratch_shapes=list(scratch),
        compiler_params=PARAMS,
        cost_estimate=pl.CostEstimate(flops=flops, transcendentals=0, bytes_accessed=8_000_000),
    )


def shape(dims, kind):
    return jax.ShapeDtypeStruct(dims, kind)


def at(step, size=STEP):
    return pl.ds(pl.multiple_of(step * size, size), size)


def group_sum(rows):
    per = C // GROUPS
    one = lax.broadcasted_iota(jnp.int32, (C, C), 0) * 6554 >> 16
    two = lax.broadcasted_iota(jnp.int32, (C, C), 1) * 6554 >> 16
    assert per == 10
    same = jnp.where(one == two, 1.0, 0.0).astype(F32)
    return jnp.dot(rows, same, precision=lax.Precision.HIGHEST, preferred_element_type=F32)


def fold(value):
    return jnp.sum(value.reshape(value.shape[0] // 8, 8, value.shape[1]), axis=0)


def column(width):
    return lax.broadcasted_iota(jnp.int32, (STEP, width), 0) & (W - 1)


def four(*sums):
    return jnp.concatenate([jnp.sum(s, axis=0, keepdims=True) for s in sums] + [jnp.zeros((8 - len(sums), C), F32)])


def sigmoid(value):
    return 1.0 / (1.0 + jnp.exp(-value))


def forward_body(x_ref, w_ref, gain_ref, h0_ref, h1_ref, acts_ref, stat_ref, sums_ref, wf, x3, y):
    for i in range(3):
        for j in range(3):
            wf[C * j : C * (j + 1), PAD * i : PAD * i + C] = w_ref[3 * i + j]
    zero = jnp.zeros((8, C), F32)

    def moments(step, carry):
        value = x_ref[at(step), :].astype(F32)
        return carry[0] + fold(value), carry[1] + fold(value * value)

    half = PIX // STEP
    s0, q0 = lax.fori_loop(0, half, moments, (zero, zero))
    s1, q1 = lax.fori_loop(half, 2 * half, moments, (zero, zero))
    grouped = group_sum(four(s0, q0, s1, q1)) * (1.0 / (PIX * C // GROUPS))
    stats = []
    for f in range(2):
        mean = grouped[2 * f : 2 * f + 1]
        var = grouped[2 * f + 1 : 2 * f + 2] - mean * mean
        stats += [mean, lax.rsqrt(var + epsilon)]
    stat_ref[...] = jnp.concatenate(stats + [jnp.zeros((4, C), F32)])
    gain = gain_ref[...]
    edge = column(C)

    def activate(step, mean, scale):
        value = x_ref[at(step), :].astype(F32)
        pre = (value - mean) * scale * gain
        act = pre / (1.0 + jnp.exp(-pre))
        low = act.astype(BF16)
        acts_ref[at(step), :] = low
        act = low.astype(F32)
        x3[at(step), 0:C] = jnp.where(edge == 0, 0.0, pltpu.roll(act, 1, 0)).astype(BF16)
        x3[at(step), C : 2 * C] = low
        x3[at(step), 2 * C : 3 * C] = jnp.where(
            edge == W - 1, 0.0, pltpu.roll(act, STEP - 1, 0)
        ).astype(BF16)

    total = (zero, zero)
    for f in range(2):
        mean, scale = stats[2 * f], stats[2 * f + 1]

        def act_step(step, carry, mean=mean, scale=scale):
            activate(step, mean, scale)
            return carry

        lax.fori_loop(f * half, (f + 1) * half, act_step, 0)
        y[f, 0:W, :] = jnp.zeros((W, 3 * PAD), F32)
        y[f, W + PIX : 2 * W + PIX, :] = jnp.zeros((W, 3 * PAD), F32)
        y[f, W : W + PIX, :] = jnp.dot(
            x3[f * PIX : (f + 1) * PIX, :], wf[...], preferred_element_type=F32
        )

        h_ref = (h0_ref, h1_ref)[f]

        def finish(step, carry, f=f, h_ref=h_ref):
            base = pl.multiple_of(step * STEP, STEP)
            conv = (
                y[f, pl.ds(base, STEP), 0:C]
                + y[f, pl.ds(base + W, STEP), PAD : PAD + C]
                + y[f, pl.ds(base + 2 * W, STEP), 2 * PAD : 2 * PAD + C]
            )
            value = x_ref[pl.ds(base + f * PIX, STEP), :].astype(F32)
            low = (value + conv).astype(BF16)
            h_ref[pl.ds(base, STEP), :] = low
            value = low.astype(F32)
            return carry[0] + fold(value), carry[1] + fold(value * value)

        total = lax.fori_loop(0, half, finish, total)
    spread(total, sums_ref)


def spread(total, sums_ref):
    first = jnp.sum(total[0], axis=0, keepdims=True)
    second = jnp.sum(total[1], axis=0, keepdims=True)
    both = jnp.concatenate([first, second])
    for k in range(sums_ref.shape[0]):
        sums_ref[k] = both


def forward(x, weight, gain, peers):
    return call(
        forward_body,
        (
            shape((PIX, C), BF16),
            shape((PIX, C), BF16),
            shape((ROWS, C), BF16),
            shape((8, C), F32),
            shape((peers, 2, C), F32),
        ),
        (
            pltpu.VMEM((3 * C, 3 * PAD), BF16),
            pltpu.VMEM((ROWS, 3 * C), BF16),
            pltpu.VMEM((2, PIX + 2 * W, 3 * PAD), F32),
        ),
        flops=2_500_000_000,
    )(x, weight, gain)


def times_transposed(a, b):
    return lax.dot_general(a, b, (((1,), (1,)), ((), ())), preferred_element_type=F32)


def mixed_grad_body(before_ref, cot_ref, after_ref, w_ref, out_ref):
    for f in range(2):
        last = cot_ref[0:PIX, :] if f else before_ref[...]
        here = cot_ref[f * PIX : (f + 1) * PIX, :]
        later = after_ref[...] if f else cot_ref[PIX:ROWS, :]
        total = times_transposed(later, w_ref[0])
        total = total + times_transposed(here, w_ref[1])
        total = total + times_transposed(last, w_ref[2])
        out_ref[f * PIX : (f + 1) * PIX, :] = total.astype(BF16)


def mixed_gradient(before, cot, after, weight):
    return call(mixed_grad_body, shape((ROWS, C), BF16), flops=1_500_000_000)(
        before, cot, after, weight
    )


def clip_stats(sums_ref, count):
    total = jnp.sum(sums_ref[...], axis=0)
    grouped = group_sum(jnp.concatenate([total, jnp.zeros((6, C), F32)])) * (1.0 / count)
    return grouped[0:1], grouped[1:2]


def slope_body(count, sums_ref, h0_ref, h1_ref, grad_ref, gain_ref, dhat_ref, stat_ref, out_ref):
    mean, square = clip_stats(sums_ref, count)
    scale = lax.rsqrt(square - mean * mean + epsilon)
    stat_ref[...] = jnp.concatenate([mean, scale, jnp.zeros((6, C), F32)])
    gain = gain_ref[...]
    zero = jnp.zeros((8, C), F32)
    total = (zero, zero)
    for f, h_ref in enumerate((h0_ref, h1_ref)):

        def step_body(step, carry, f=f, h_ref=h_ref):
            base = pl.multiple_of(step * STEP, STEP)
            hat = (h_ref[pl.ds(base, STEP), :].astype(F32) - mean) * scale
            pre = hat * gain
            s = sigmoid(pre)
            slope = s * (1.0 + pre * (1.0 - s))
            dhat = grad_ref[pl.ds(base + f * PIX, STEP), :].astype(F32) * slope * gain
            dhat_ref[pl.ds(base + f * PIX, STEP), :] = dhat
            return carry[0] + fold(dhat), carry[1] + fold(dhat * hat)

        total = lax.fori_loop(0, PIX // STEP, step_body, total)
    spread(total, out_ref)


def slopes(sums, h0, h1, grad, gain, count):
    return call(
        functools.partial(slope_body, count),
        (shape((ROWS, C), F32), shape((8, C), F32), shape(sums.shape, F32)),
    )(sums, h0, h1, grad, gain)


def temporal_body(
    place_ref, hb_ref, h0_ref, h1_ref, ha_ref, cot_ref, w_ref, stat_ref, gain_ref,
    out_ref, keep_ref, give_ref, mx, mxt,
):
    mean, scale = stat_ref[0:1, :], stat_ref[1:2, :]
    gain = gain_ref[...]
    live = (place_ref[1], None, None, place_ref[2])
    for n, h_ref in enumerate((hb_ref, h0_ref, h1_ref, ha_ref)):

        def step_body(step, carry, n=n, h_ref=h_ref):
            base = pl.multiple_of(step * STEP, STEP)
            pre = (h_ref[pl.ds(base, STEP), :].astype(F32) - mean) * scale * gain
            act = pre / (1.0 + jnp.exp(-pre))
            if live[n] is not None:
                act = jnp.where(live[n] != 0, act, 0.0)
            act = act.astype(BF16)
            mx[pl.ds(base + n * PIX, STEP), :] = act
            return carry

        lax.fori_loop(0, PIX // STEP, step_body, 0)
    for n in range(4 * PIX // STEP):
        mxt[:, n * STEP : (n + 1) * STEP] = mx[n * STEP : (n + 1) * STEP, :].T
    for f, h_ref in enumerate((h0_ref, h1_ref)):
        total = None
        for k in range(3):
            part = jnp.dot(
                mx[(f + k) * PIX : (f + k + 1) * PIX, :], w_ref[k], preferred_element_type=F32
            )
            total = part if total is None else total + part
        low = total.astype(BF16).astype(F32)
        out_ref[f * PIX : (f + 1) * PIX, :] = (h_ref[...].astype(F32) + low).astype(BF16)
    core = place_ref[0]
    for k in range(3):
        part = jnp.dot(
            mxt[:, k * PIX : k * PIX + ROWS], cot_ref[...], preferred_element_type=F32
        )
        left, right = part[:, 0:HALF], part[:, HALF:C]
        keep_ref[k * C : (k + 1) * C, 0:HALF] = jnp.where(core == 0, left, right)
        give_ref[k * C : (k + 1) * C, 0:HALF] = jnp.where(core == 0, right, left)


SMEM = pl.BlockSpec(memory_space=pltpu.SMEM)
VMEM = pl.BlockSpec(memory_space=pltpu.VMEM)


def call_with_place(body, operands, out, scratch=(), flops=0):
    return pl.pallas_call(
        body,
        out_shape=out,
        in_specs=[SMEM] + [VMEM] * operands,
        scratch_shapes=list(scratch),
        compiler_params=PARAMS,
        cost_estimate=pl.CostEstimate(flops=flops, transcendentals=0, bytes_accessed=8_000_000),
    )


def temporal(place, before, h0, h1, after, cot, weight, stat, gain):
    return call_with_place(
        temporal_body,
        8,
        (shape((ROWS, C), BF16), shape((3 * C, 256), F32), shape((3 * C, 256), F32)),
        (pltpu.VMEM((4 * PIX, C), BF16), pltpu.VMEM((C, 4 * PIX), BF16)),
        flops=3_000_000_000,
    )(place, before, h0, h1, after, cot, weight, stat, gain)


def turned_body(acts_ref, out_ref):
    lane = lax.broadcasted_iota(jnp.int32, (C, STEP), 1) & (W - 1)
    for step in range(ROWS // STEP):
        turned = acts_ref[step * STEP : (step + 1) * STEP, :].astype(F32).T
        where = slice(step * STEP, (step + 1) * STEP)
        out_ref[0:C, where] = jnp.where(lane == 0, 0.0, pltpu.roll(turned, 1, 1)).astype(BF16)
        out_ref[C : 2 * C, where] = turned.astype(BF16)
        out_ref[2 * C : 3 * C, where] = jnp.where(
            lane == W - 1, 0.0, pltpu.roll(turned, STEP - 1, 1)
        ).astype(BF16)


def turned(acts):
    return call(turned_body, shape((3 * C, ROWS), BF16), flops=500_000_000)(acts)


def hidden_grad_body(
    count, place_ref, sums_ref, stat_ref, dhat_ref, h0_ref, h1_ref, cot_ref,
    grad_ref, low_ref, keep_ref, give_ref,
):
    first, second = clip_stats(sums_ref, count)
    mean, scale = stat_ref[0:1, :], stat_ref[1:2, :]
    core = place_ref[0]
    for f, h_ref in enumerate((h0_ref, h1_ref)):

        def step_body(step, carry, f=f, h_ref=h_ref):
            base = pl.multiple_of(step * STEP, STEP)
            here = pl.ds(base + f * PIX, STEP)
            hat = (h_ref[pl.ds(base, STEP), :].astype(F32) - mean) * scale
            grad = cot_ref[here, :].astype(F32) + scale * (dhat_ref[here, :] - first - hat * second)
            grad_ref[here, :] = grad
            low = grad.astype(BF16)
            low_ref[here, :] = low
            left, right = grad[:, 0:HALF], grad[:, HALF:C]
            keep_ref[here, :] = jnp.where(core == 0, left, right).astype(BF16)
            give_ref[here, :] = jnp.where(core == 0, right, left).astype(BF16)
            return carry

        lax.fori_loop(0, PIX // STEP, step_body, 0)


def hidden_gradient(place, sums, stat, dhat, h0, h1, cot, count):
    return call_with_place(
        functools.partial(hidden_grad_body, count),
        7 - 1,
        (
            shape((ROWS, C), F32),
            shape((ROWS, C), BF16),
            shape((ROWS, HALF), BF16),
            shape((ROWS, HALF), BF16),
        ),
    )(place, sums, stat, dhat, h0, h1, cot)


def row_taps(value):
    none = jnp.zeros((W, value.shape[1]), value.dtype)
    return (
        jnp.concatenate([value[W:], none]),
        value,
        jnp.concatenate([none, value[: PIX - W]]),
    )


def weight_grad_body(
    mine_turned_ref, other_turned_ref, mine_ref, other_ref, keep_ref, got_ref, out_ref, rhs
):
    total = None
    for n, (ref, turned_ref) in enumerate(
        ((mine_ref, mine_turned_ref), (other_ref, other_turned_ref))
    ):
        for f in range(2):
            where = slice(f * PIX, (f + 1) * PIX)
            for i, tap in enumerate(row_taps(ref[where, :])):
                rhs[n, where, i * HALF : (i + 1) * HALF] = tap
        part = jnp.dot(turned_ref[...], rhs[n], preferred_element_type=F32)
        total = part if total is None else total + part
    out_ref[0 : 3 * C, 0 : 3 * HALF] = total
    out_ref[0 : 3 * C, 3 * HALF : 4 * HALF] = keep_ref[:, 0:HALF] + got_ref[:, 0:HALF]
    out_ref[3 * C :, :] = jnp.zeros((1024 - 3 * C, 4 * HALF), F32)


def weight_gradients(mine_turned, other_turned, mine, other, keep, got):
    return call(
        weight_grad_body,
        shape((1024, 4 * HALF), F32),
        (pltpu.VMEM((2, ROWS, 3 * HALF), BF16),),
        flops=2_500_000_000,
    )(mine_turned, other_turned, mine, other, keep, got)


def input_grad_body(low_ref, grad_ref, x_ref, stat_ref, gain_ref, w_ref, out_ref, wb, rows, z, dh):
    for j in range(3):
        for i in range(3):
            wb[PAD * j : PAD * j + C, C * i : C * (i + 1)] = w_ref[3 * i + j]
        wb[PAD * j + C : PAD * (j + 1), :] = jnp.zeros((PAD - C, 3 * C), BF16)
    gain = gain_ref[...]
    edge = column(C)
    half = PIX // STEP
    for f in range(2):
        mean, scale = stat_ref[2 * f : 2 * f + 1, :], stat_ref[2 * f + 1 : 2 * f + 2, :]
        for i, tap in enumerate(row_taps(low_ref[f * PIX : (f + 1) * PIX, :])):
            rows[:, i * C : (i + 1) * C] = tap
        z[...] = times_transposed(rows[...], wb[...])

        def step_body(step, carry, f=f, mean=mean, scale=scale):
            base = pl.multiple_of(step * STEP, STEP)
            here = pl.ds(base, STEP)
            right = jnp.where(edge == W - 1, 0.0, pltpu.roll(z[here, 0:C], STEP - 1, 0))
            left = jnp.where(edge == 0, 0.0, pltpu.roll(z[here, 2 * PAD : 2 * PAD + C], 1, 0))
            acts_grad = right + z[here, PAD : PAD + C] + left
            hat = (x_ref[pl.ds(base + f * PIX, STEP), :].astype(F32) - mean) * scale
            pre = hat * gain
            s = sigmoid(pre)
            dhat = acts_grad * (s * (1.0 + pre * (1.0 - s))) * gain
            dh[here, :] = dhat
            return carry[0] + fold(dhat), carry[1] + fold(dhat * hat)

        zero = jnp.zeros((8, C), F32)
        sums = lax.fori_loop(0, half, step_body, (zero, zero))
        grouped = group_sum(four(*sums)) * (1.0 / (PIX * C // GROUPS))
        first, second = grouped[0:1], grouped[1:2]

        def last_body(step, carry, f=f, mean=mean, scale=scale, first=first, second=second):
            base = pl.multiple_of(step * STEP, STEP)
            there = pl.ds(base + f * PIX, STEP)
            hat = (x_ref[there, :].astype(F32) - mean) * scale
            value = grad_ref[there, :] + scale * (dh[pl.ds(base, STEP), :] - first - hat * second)
            out_ref[there, :] = value.astype(BF16)
            return carry

        lax.fori_loop(0, half, last_body, 0)


def input_gradient(low, grad, x, stat, gain, weight):
    return call(
        input_grad_body,
        shape((ROWS, C), BF16),
        (
            pltpu.VMEM((3 * PAD, 3 * C), BF16),
            pltpu.VMEM((PIX, 3 * C), BF16),
            pltpu.VMEM((PIX, 3 * PAD), F32),
            pltpu.VMEM((PIX, C), F32),
        ),
        flops=2_500_000_000,
    )(low, grad, x, stat, gain, weight)


def unpack_body(place_ref, mine_ref, other_ref, spatial_ref, temporal_ref):
    core = place_ref[0]
    for j in range(3):
        here = slice(j * C, (j + 1) * C)
        mine, other = mine_ref[here, :], other_ref[here, :]
        left = jnp.where(core == 0, mine, other)
        right = jnp.where(core == 0, other, mine)
        for i in range(4):
            lanes = slice(i * HALF, (i + 1) * HALF)
            if i < 3:
                spatial_ref[3 * i + j, :, 0:HALF] = left[:, lanes]
                spatial_ref[3 * i + j, :, HALF:C] = right[:, lanes]
            else:
                temporal_ref[j, :, 0:HALF] = left[:, lanes]
                temporal_ref[j, :, HALF:C] = right[:, lanes]


def unpack(place, mine, other):
    return call_with_place(
        unpack_body, 2, (shape((9, C, C), BF16), shape((3, C, C), BF16))
    )(place, mine, other)


def neighbours(first, second):
    size = lax.axis_size(FRAME)
    before = lax.ppermute(second, FRAME, [(i, i + 1) for i in range(size - 1)])
    after = lax.ppermute(first, FRAME, [(i + 1, i) for i in range(size - 1)])
    return before, after


def swap_cores(value):
    return lax.ppermute(value, "c", [(0, 1), (1, 0)])


def everyone_total(value, beside):
    plane, line = lax.axis_size(PLANE), lax.axis_size(LINE)
    width = value.shape[1]
    value = value.reshape(plane, 1024 // plane, width)
    value = lax.all_to_all(value, PLANE, 0, 0)
    value, beside = lax.optimization_barrier((value, beside))
    value = jnp.sum(value, axis=0)
    value = value.reshape(line, 1024 // plane // line, width)
    value = jnp.sum(lax.all_to_all(value, LINE, 0, 0), axis=0).astype(BF16)
    value = jnp.broadcast_to(value[None], (line,) + value.shape)
    value = lax.all_to_all(value, LINE, 0, 0).reshape(1024 // plane, width)
    value = jnp.broadcast_to(value[None], (plane,) + value.shape)
    return lax.all_to_all(value, PLANE, 0, 0).reshape(1024, width), beside


def on_device(clips, cotangent, spatial_weight, temporal_weight, gain_one, gain_two):
    size = lax.axis_size(FRAME)
    place = lax.axis_index(FRAME)
    place = jnp.stack(
        [lax.axis_index("c"), (place > 0).astype(jnp.int32), (place < size - 1).astype(jnp.int32)]
    )
    count = float(size * ROWS * C // GROUPS)
    x = clips.reshape(ROWS, C)
    cot = cotangent.reshape(ROWS, C)
    spatial_weight = spatial_weight.reshape(9, C, C)
    gain_one = gain_one.reshape(1, C)
    gain_two = gain_two.reshape(1, C)
    cot_before, cot_after = neighbours(cot[:PIX], cot[PIX:])
    h0, h1, acts, stat_one, sums = forward(x, spatial_weight, gain_one, size)
    sums = lax.all_to_all(sums, FRAME, 0, 0)
    before, after = neighbours(h0, h1)
    mine_turned = turned(acts)
    mixed_grad = mixed_gradient(cot_before, cot, cot_after, temporal_weight)
    sums, mine_turned, mixed_grad = lax.optimization_barrier((sums, mine_turned, mixed_grad))
    other_turned = swap_cores(mine_turned)
    dhat, stat_two, sums = slopes(sums, h0, h1, mixed_grad, gain_two, count)
    sums = lax.all_to_all(sums, FRAME, 0, 0)
    output, temporal_keep, temporal_give = temporal(
        place, before, h0, h1, after, cot, temporal_weight, stat_two, gain_two
    )
    sums, temporal_give, other_turned = lax.optimization_barrier(
        (sums, temporal_give, other_turned)
    )
    temporal_got = swap_cores(temporal_give)
    grad, low, low_keep, low_give = hidden_gradient(
        place, sums, stat_two, dhat, h0, h1, cot, count
    )
    low_got = swap_cores(low_give)
    packed = weight_gradients(
        mine_turned, other_turned, low_keep, low_got, temporal_keep, temporal_got
    )
    packed, low = lax.optimization_barrier((packed, low))
    input_grad = input_gradient(low, grad, x, stat_one, gain_one, spatial_weight)
    mine, input_grad = everyone_total(packed, input_grad)
    other = swap_cores(mine)
    spatial_grad, temporal_grad = unpack(place, mine, other)
    return (
        output.reshape(clips.shape),
        input_grad.reshape(clips.shape),
        spatial_grad.reshape(3, 3, C, C),
        temporal_grad,
    )


def solution(mesh):
    fine = Mesh(mesh.devices.reshape(2, 4, 2, 4, 4), ("zl", "x", "c", "y", "zh"))
    return jax.shard_map(
        on_device,
        mesh=fine,
        in_specs=(P(DP, FRAME), P(DP, FRAME), P(), P(), P(), P()),
        out_specs=(P(DP, FRAME), P(DP, FRAME), P(), P()),
        check_vma=False,
    )
```

```python
import functools

import jax
import jax.numpy as jnp
from jax import lax
from jax.experimental import pallas as pl
from jax.experimental.pallas import tpu as pltpu
from jax.sharding import Mesh, PartitionSpec as P

epsilon = 1e-05

GROUPS = 32
DP = ("zl", "x", "c")
FRAME = ("y", "zh")
PLANE = ("x", "y")
LINE = ("zl", "zh")

C = 320
W = 32
PAD = 384
HALF = C // 2
PIX = 512
ROWS = 2 * PIX
STEP = 128
F32 = jnp.float32
BF16 = jnp.bfloat16

MIB = 1024 * 1024


def call(body, out, scratch=(), flops=0, limit=12):
    return pl.pallas_call(
        body,
        out_shape=out,
        scratch_shapes=list(scratch),
        compiler_params=pltpu.CompilerParams(vmem_limit_bytes=limit * MIB),
        cost_estimate=pl.CostEstimate(flops=flops, transcendentals=0, bytes_accessed=8_000_000),
    )


def shape(dims, kind):
    return jax.ShapeDtypeStruct(dims, kind)


def at(step, size=STEP):
    return pl.ds(pl.multiple_of(step * size, size), size)


def group_sum(rows):
    per = C // GROUPS
    one = lax.broadcasted_iota(jnp.int32, (C, C), 0) * 6554 >> 16
    two = lax.broadcasted_iota(jnp.int32, (C, C), 1) * 6554 >> 16
    assert per == 10
    same = jnp.where(one == two, 1.0, 0.0).astype(F32)
    return jnp.dot(rows, same, precision=lax.Precision.HIGHEST, preferred_element_type=F32)


def fold(value):
    return jnp.sum(value.reshape(value.shape[0] // 8, 8, value.shape[1]), axis=0)


def column(width):
    return lax.broadcasted_iota(jnp.int32, (STEP, width), 0) & (W - 1)


def four(*sums):
    return jnp.concatenate([jnp.sum(s, axis=0, keepdims=True) for s in sums] + [jnp.zeros((8 - len(sums), C), F32)])


def sigmoid(value):
    return 1.0 / (1.0 + jnp.exp(-value))


def forward_body(x_ref, w_ref, gain_ref, h0_ref, h1_ref, turned_ref, stat_ref, sums_ref, wf, x3, y):
    for i in range(3):
        for j in range(3):
            wf[C * j : C * (j + 1), PAD * i : PAD * i + C] = w_ref[3 * i + j]
    zero = jnp.zeros((8, C), F32)

    def moments(step, carry):
        value = x_ref[at(step), :].astype(F32)
        return carry[0] + fold(value), carry[1] + fold(value * value)

    half = PIX // STEP
    s0, q0 = lax.fori_loop(0, half, moments, (zero, zero))
    s1, q1 = lax.fori_loop(half, 2 * half, moments, (zero, zero))
    grouped = group_sum(four(s0, q0, s1, q1)) * (1.0 / (PIX * C // GROUPS))
    stats = []
    for f in range(2):
        mean = grouped[2 * f : 2 * f + 1]
        var = grouped[2 * f + 1 : 2 * f + 2] - mean * mean
        stats += [mean, lax.rsqrt(var + epsilon)]
    stat_ref[...] = jnp.concatenate(stats + [jnp.zeros((4, C), F32)])
    gain = gain_ref[...].reshape(1, C)
    edge = column(C)

    def activate(step, mean, scale):
        value = x_ref[at(step), :].astype(F32)
        pre = (value - mean) * scale * gain
        act = pre / (1.0 + jnp.exp(-pre))
        low = act.astype(BF16)
        act = low.astype(F32)
        x3[at(step), 0:C] = jnp.where(edge == 0, 0.0, pltpu.roll(act, 1, 0)).astype(BF16)
        x3[at(step), C : 2 * C] = low
        x3[at(step), 2 * C : 3 * C] = jnp.where(
            edge == W - 1, 0.0, pltpu.roll(act, STEP - 1, 0)
        ).astype(BF16)

    total = (zero, zero)
    for f in range(2):
        mean, scale = stats[2 * f], stats[2 * f + 1]

        def act_step(step, carry, mean=mean, scale=scale):
            activate(step, mean, scale)
            return carry

        lax.fori_loop(f * half, (f + 1) * half, act_step, 0)
        y[f, 0:W, :] = jnp.zeros((W, 3 * PAD), F32)
        y[f, W + PIX : 2 * W + PIX, :] = jnp.zeros((W, 3 * PAD), F32)
        y[f, W : W + PIX, :] = jnp.dot(
            x3[f * PIX : (f + 1) * PIX, :], wf[...], preferred_element_type=F32
        )

        turn(x3[f * PIX : (f + 1) * PIX, C : 2 * C], turned_ref, f * PIX)
        h_ref = (h0_ref, h1_ref)[f]

        def finish(step, carry, f=f, h_ref=h_ref):
            base = pl.multiple_of(step * STEP, STEP)
            conv = (
                y[f, pl.ds(base, STEP), 0:C]
                + y[f, pl.ds(base + W, STEP), PAD : PAD + C]
                + y[f, pl.ds(base + 2 * W, STEP), 2 * PAD : 2 * PAD + C]
            )
            value = x_ref[pl.ds(base + f * PIX, STEP), :].astype(F32)
            low = (value + conv).astype(BF16)
            h_ref[pl.ds(base, STEP), :] = low
            value = low.astype(F32)
            return carry[0] + fold(value), carry[1] + fold(value * value)

        total = lax.fori_loop(0, half, finish, total)
    spread(total, sums_ref)


def spread(total, sums_ref):
    first = jnp.sum(total[0], axis=0, keepdims=True)
    second = jnp.sum(total[1], axis=0, keepdims=True)
    both = jnp.concatenate([first, second])
    for k in range(sums_ref.shape[0]):
        sums_ref[k] = both


def turn(acts, out_ref, base):
    rows = lax.broadcasted_iota(jnp.int32, (C, C), 0)
    same = jnp.where(rows == lax.broadcasted_iota(jnp.int32, (C, C), 1), 1.0, 0.0).astype(BF16)
    lane = lax.broadcasted_iota(jnp.int32, (C, STEP), 1) & (W - 1)
    moved = times_transposed(same, acts)
    for step in range(PIX // STEP):
        part = moved[:, step * STEP : (step + 1) * STEP]
        where = slice(base + step * STEP, base + (step + 1) * STEP)
        out_ref[0:C, where] = jnp.where(lane == 0, 0.0, pltpu.roll(part, 1, 1)).astype(BF16)
        out_ref[C : 2 * C, where] = part.astype(BF16)
        out_ref[2 * C : 3 * C, where] = jnp.where(
            lane == W - 1, 0.0, pltpu.roll(part, STEP - 1, 1)
        ).astype(BF16)


def forward(x, weight, gain, peers):
    return call(
        forward_body,
        (
            shape((PIX, C), BF16),
            shape((PIX, C), BF16),
            shape((3 * C, ROWS), BF16),
            shape((8, C), F32),
            shape((peers, 2, C), F32),
        ),
        (
            pltpu.VMEM((3 * C, 3 * PAD), BF16),
            pltpu.VMEM((ROWS, 3 * C), BF16),
            pltpu.VMEM((2, PIX + 2 * W, 3 * PAD), F32),
        ),
        flops=2_500_000_000,
        limit=20,
    )(x, weight, gain)


def times_transposed(a, b):
    return lax.dot_general(a, b, (((1,), (1,)), ((), ())), preferred_element_type=F32)


def mixed_grad_body(before_ref, cot_ref, after_ref, w_ref, out_ref):
    for f in range(2):
        last = cot_ref[0:PIX, :] if f else before_ref[...]
        here = cot_ref[f * PIX : (f + 1) * PIX, :]
        later = after_ref[...] if f else cot_ref[PIX:ROWS, :]
        total = times_transposed(later, w_ref[0])
        total = total + times_transposed(here, w_ref[1])
        total = total + times_transposed(last, w_ref[2])
        out_ref[f * PIX : (f + 1) * PIX, :] = total.astype(BF16)


def mixed_gradient(before, cot, after, weight):
    return call(mixed_grad_body, shape((ROWS, C), BF16), flops=1_500_000_000)(
        before, cot, after, weight
    )


def clip_stats(sums_ref, count):
    total = jnp.sum(sums_ref[...], axis=0)
    grouped = group_sum(jnp.concatenate([total, jnp.zeros((6, C), F32)])) * (1.0 / count)
    return grouped[0:1], grouped[1:2]


def slope_body(
    count, sums_ref, h0_ref, h1_ref, grad_ref, cot_ref, gain_ref, part_ref, stat_ref, out_ref
):
    mean, square = clip_stats(sums_ref, count)
    scale = lax.rsqrt(square - mean * mean + epsilon)
    stat_ref[...] = jnp.concatenate([mean, scale, jnp.zeros((6, C), F32)])
    gain = gain_ref[...].reshape(1, C)
    zero = jnp.zeros((8, C), F32)
    total = (zero, zero)
    for f, h_ref in enumerate((h0_ref, h1_ref)):

        def step_body(step, carry, f=f, h_ref=h_ref):
            base = pl.multiple_of(step * STEP, STEP)
            hat = (h_ref[pl.ds(base, STEP), :].astype(F32) - mean) * scale
            pre = hat * gain
            s = sigmoid(pre)
            slope = s * (1.0 + pre * (1.0 - s))
            dhat = grad_ref[pl.ds(base + f * PIX, STEP), :].astype(F32) * slope * gain
            there = pl.ds(base + f * PIX, STEP)
            part_ref[there, :] = cot_ref[there, :].astype(F32) + scale * dhat
            return carry[0] + fold(dhat), carry[1] + fold(dhat * hat)

        total = lax.fori_loop(0, PIX // STEP, step_body, total)
    spread(total, out_ref)


def slopes(sums, h0, h1, grad, cot, gain, count):
    return call(
        functools.partial(slope_body, count),
        (shape((ROWS, C), F32), shape((8, C), F32), shape(sums.shape, F32)),
    )(sums, h0, h1, grad, cot, gain)


def mixed_body(
    hb_ref, h0_ref, h1_ref, ha_ref, cot_ref, stat_ref, gain_ref, mx_ref, keep_ref, give_ref, turned
):
    mean, scale = stat_ref[0:1, :], stat_ref[1:2, :]
    gain = gain_ref[...].reshape(1, C)
    place = lax.axis_index(FRAME)
    live = (place > 0, None, None, place < lax.axis_size(FRAME) - 1)
    for n, h_ref in enumerate((hb_ref, h0_ref, h1_ref, ha_ref)):

        def step_body(step, carry, n=n, h_ref=h_ref):
            base = pl.multiple_of(step * STEP, STEP)
            pre = (h_ref[pl.ds(base, STEP), :].astype(F32) - mean) * scale * gain
            act = pre / (1.0 + jnp.exp(-pre))
            if live[n] is not None:
                act = jnp.where(live[n], act, 0.0)
            mx_ref[pl.ds(base + n * PIX, STEP), :] = act.astype(BF16)
            return carry

        lax.fori_loop(0, PIX // STEP, step_body, 0)
    for n in range(4 * PIX // STEP):
        where = slice(n * STEP, (n + 1) * STEP)
        turned[:, where] = mx_ref[where, :].T
    core = lax.axis_index("c")
    for k in range(3):
        part = jnp.dot(
            turned[:, k * PIX : k * PIX + ROWS], cot_ref[...], preferred_element_type=F32
        )
        left, right = part[:, 0:HALF], part[:, HALF:C]
        keep_ref[k * C : (k + 1) * C, 0:HALF] = jnp.where(core == 0, left, right)
        give_ref[k * C : (k + 1) * C, 0:HALF] = jnp.where(core == 0, right, left)


def mixed_frames(before, h0, h1, after, cot, stat, gain):
    return call(
        mixed_body,
        (shape((4 * PIX, C), BF16), shape((3 * C, 256), F32), shape((3 * C, 256), F32)),
        (pltpu.VMEM((C, 4 * PIX), BF16),),
        flops=1_500_000_000,
    )(before, h0, h1, after, cot, stat, gain)


def temporal_body(mx_ref, h0_ref, h1_ref, w_ref, out_ref):
    for f, h_ref in enumerate((h0_ref, h1_ref)):
        total = None
        for k in range(3):
            part = jnp.dot(
                mx_ref[(f + k) * PIX : (f + k + 1) * PIX, :],
                w_ref[k],
                preferred_element_type=F32,
            )
            total = part if total is None else total + part
        low = total.astype(BF16).astype(F32)
        out_ref[f * PIX : (f + 1) * PIX, :] = (h_ref[...].astype(F32) + low).astype(BF16)


def temporal(mixed, h0, h1, weight):
    return call(temporal_body, shape((ROWS, C), BF16), flops=1_500_000_000)(mixed, h0, h1, weight)


def whole_grad(part_ref, h_ref, stat_ref, sums, base, f):
    mean, scale = stat_ref[0:1, :], stat_ref[1:2, :]
    hat = (h_ref[pl.ds(base, STEP), :].astype(F32) - mean) * scale
    return part_ref[pl.ds(base + f * PIX, STEP), :] - scale * (sums[0] + hat * sums[1])


def hidden_grad_body(
    count, sums_ref, stat_ref, part_ref, h0_ref, h1_ref, keep_ref, give_ref, total_ref
):
    sums = clip_stats(sums_ref, count)
    total_ref[...] = jnp.concatenate([*sums, jnp.zeros((6, C), F32)])
    core = lax.axis_index("c")
    for f, h_ref in enumerate((h0_ref, h1_ref)):

        def step_body(step, carry, f=f, h_ref=h_ref):
            base = pl.multiple_of(step * STEP, STEP)
            here = pl.ds(base + f * PIX, STEP)
            grad = whole_grad(part_ref, h_ref, stat_ref, sums, base, f)
            left, right = grad[:, 0:HALF], grad[:, HALF:C]
            keep_ref[here, :] = jnp.where(core == 0, left, right).astype(BF16)
            give_ref[here, :] = jnp.where(core == 0, right, left).astype(BF16)
            return carry

        lax.fori_loop(0, PIX // STEP, step_body, 0)


def hidden_gradient(sums, stat, part, h0, h1, count):
    return call(
        functools.partial(hidden_grad_body, count),
        (shape((ROWS, HALF), BF16), shape((ROWS, HALF), BF16), shape((8, C), F32)),
    )(sums, stat, part, h0, h1)


def row_taps(value):
    none = jnp.zeros((W, value.shape[1]), value.dtype)
    return (
        jnp.concatenate([value[W:], none]),
        value,
        jnp.concatenate([none, value[: PIX - W]]),
    )


def weight_grad_body(
    mine_turned_ref, other_turned_ref, mine_ref, other_ref, keep_ref, got_ref, out_ref, rhs
):
    total = None
    for n, (ref, turned_ref) in enumerate(
        ((mine_ref, mine_turned_ref), (other_ref, other_turned_ref))
    ):
        for f in range(2):
            where = slice(f * PIX, (f + 1) * PIX)
            for i, tap in enumerate(row_taps(ref[where, :])):
                rhs[n, where, i * HALF : (i + 1) * HALF] = tap
        part = jnp.dot(turned_ref[...], rhs[n], preferred_element_type=F32)
        total = part if total is None else total + part
    out_ref[0 : 3 * C, 0 : 3 * HALF] = total.astype(BF16)
    kept = keep_ref[:, 0:HALF] + got_ref[:, 0:HALF]
    out_ref[0 : 3 * C, 3 * HALF : 4 * HALF] = kept.astype(BF16)
    out_ref[3 * C :, :] = jnp.zeros((1024 - 3 * C, 4 * HALF), BF16)


def weight_gradients(mine_turned, other_turned, mine, other, keep, got):
    return call(
        weight_grad_body,
        shape((1024, 4 * HALF), BF16),
        (pltpu.VMEM((2, ROWS, 3 * HALF), BF16),),
        flops=2_500_000_000,
    )(mine_turned, other_turned, mine, other, keep, got)


def input_grad_body(
    part_ref, h0_ref, h1_ref, clip_ref, total_ref, x_ref, stat_ref, gain_ref, w_ref,
    out_ref, wb, rows, z, dh, grads, lows,
):
    clip_sums = total_ref[0:1, :], total_ref[1:2, :]
    for j in range(3):
        for i in range(3):
            wb[PAD * j : PAD * j + C, C * i : C * (i + 1)] = w_ref[3 * i + j]
        wb[PAD * j + C : PAD * (j + 1), :] = jnp.zeros((PAD - C, 3 * C), BF16)
    gain = gain_ref[...].reshape(1, C)
    edge = column(C)
    half = PIX // STEP
    for f in range(2):
        mean, scale = stat_ref[2 * f : 2 * f + 1, :], stat_ref[2 * f + 1 : 2 * f + 2, :]
        h_ref = (h0_ref, h1_ref)[f]

        def grad_body(step, carry, f=f, h_ref=h_ref):
            base = pl.multiple_of(step * STEP, STEP)
            grad = whole_grad(part_ref, h_ref, clip_ref, clip_sums, base, f)
            grads[pl.ds(base, STEP), :] = grad
            lows[pl.ds(base, STEP), :] = grad.astype(BF16)
            return carry

        lax.fori_loop(0, half, grad_body, 0)
        for i, tap in enumerate(row_taps(lows[...])):
            rows[:, i * C : (i + 1) * C] = tap
        z[...] = times_transposed(rows[...], wb[...])

        def step_body(step, carry, f=f, mean=mean, scale=scale):
            base = pl.multiple_of(step * STEP, STEP)
            here = pl.ds(base, STEP)
            right = jnp.where(edge == W - 1, 0.0, pltpu.roll(z[here, 0:C], STEP - 1, 0))
            left = jnp.where(edge == 0, 0.0, pltpu.roll(z[here, 2 * PAD : 2 * PAD + C], 1, 0))
            acts_grad = right + z[here, PAD : PAD + C] + left
            hat = (x_ref[pl.ds(base + f * PIX, STEP), :].astype(F32) - mean) * scale
            pre = hat * gain
            s = sigmoid(pre)
            dhat = acts_grad * (s * (1.0 + pre * (1.0 - s))) * gain
            dh[here, :] = dhat
            return carry[0] + fold(dhat), carry[1] + fold(dhat * hat)

        zero = jnp.zeros((8, C), F32)
        sums = lax.fori_loop(0, half, step_body, (zero, zero))
        grouped = group_sum(four(*sums)) * (1.0 / (PIX * C // GROUPS))
        first, second = grouped[0:1], grouped[1:2]

        def last_body(step, carry, f=f, mean=mean, scale=scale, first=first, second=second):
            base = pl.multiple_of(step * STEP, STEP)
            there = pl.ds(base + f * PIX, STEP)
            hat = (x_ref[there, :].astype(F32) - mean) * scale
            here = pl.ds(base, STEP)
            value = grads[here, :] + scale * (dh[here, :] - first - hat * second)
            out_ref[there, :] = value.astype(BF16)
            return carry

        lax.fori_loop(0, half, last_body, 0)


def input_gradient(part, h0, h1, clip_stat, total, x, stat, gain, weight):
    return call(
        input_grad_body,
        shape((ROWS, C), BF16),
        (
            pltpu.VMEM((3 * PAD, 3 * C), BF16),
            pltpu.VMEM((PIX, 3 * C), BF16),
            pltpu.VMEM((PIX, 3 * PAD), F32),
            pltpu.VMEM((PIX, C), F32),
            pltpu.VMEM((PIX, C), F32),
            pltpu.VMEM((PIX, C), BF16),
        ),
        flops=2_500_000_000,
        limit=16,
    )(part, h0, h1, clip_stat, total, x, stat, gain, weight)


def unpack_body(mine_ref, other_ref, spatial_ref, temporal_ref):
    core = lax.axis_index("c")
    for j in range(3):
        here = slice(j * C, (j + 1) * C)
        mine, other = mine_ref[here, :], other_ref[here, :]
        left = jnp.where(core == 0, mine, other)
        right = jnp.where(core == 0, other, mine)
        for i in range(4):
            lanes = slice(i * HALF, (i + 1) * HALF)
            if i < 3:
                spatial_ref[3 * i + j, :, 0:HALF] = left[:, lanes]
                spatial_ref[3 * i + j, :, HALF:C] = right[:, lanes]
            else:
                temporal_ref[j, :, 0:HALF] = left[:, lanes]
                temporal_ref[j, :, HALF:C] = right[:, lanes]


def unpack(mine, other):
    return call(unpack_body, (shape((9, C, C), BF16), shape((3, C, C), BF16)))(mine, other)


def neighbours(first, second):
    size = lax.axis_size(FRAME)
    before = lax.ppermute(second, FRAME, [(i, i + 1) for i in range(size - 1)])
    after = lax.ppermute(first, FRAME, [(i + 1, i) for i in range(size - 1)])
    return before, after


def swap_cores(value):
    return lax.ppermute(value, "c", [(0, 1), (1, 0)])


def everyone_total(value):
    plane = lax.axis_size(PLANE)
    value = value.reshape(plane, 1024 // plane, value.shape[1])
    return lax.all_to_all(value, PLANE, 0, 0)


def everyone_share(value):
    plane, line = lax.axis_size(PLANE), lax.axis_size(LINE)
    width = value.shape[2]
    value = jnp.sum(value.astype(F32), axis=0)
    value = value.reshape(line, 1024 // plane // line, width)
    value = jnp.sum(lax.all_to_all(value, LINE, 0, 0), axis=0).astype(BF16)
    value = jnp.broadcast_to(value[None], (line,) + value.shape)
    value = lax.all_to_all(value, LINE, 0, 0).reshape(1024 // plane, width)
    value = jnp.broadcast_to(value[None], (plane,) + value.shape)
    return lax.all_to_all(value, PLANE, 0, 0).reshape(1024, width)


def on_device(clips, cotangent, spatial_weight, temporal_weight, gain_one, gain_two):
    size = lax.axis_size(FRAME)
    count = float(size * ROWS * C // GROUPS)
    x = clips.reshape(ROWS, C)
    cot = cotangent.reshape(ROWS, C)
    spatial_weight = spatial_weight.reshape(9, C, C)
    barrier = lax.optimization_barrier
    cot_before, cot_after = neighbours(cot[:PIX], cot[PIX:])
    h0, h1, mine_turned, stat_one, sums = forward(x, spatial_weight, gain_one, size)
    before, after = neighbours(h0, h1)
    sums = lax.all_to_all(sums, FRAME, 0, 0)
    mixed_grad = mixed_gradient(cot_before, cot, cot_after, temporal_weight)
    sums, mixed_grad = barrier((sums, mixed_grad))
    part, clip_stat, sums = slopes(sums, h0, h1, mixed_grad, cot, gain_two, count)
    sums, before, after = barrier((sums, before, after))
    sums = lax.all_to_all(sums, FRAME, 0, 0)
    other_turned = swap_cores(mine_turned)
    mixed, temporal_keep, temporal_give = mixed_frames(
        before, h0, h1, after, cot, clip_stat, gain_two
    )
    sums, temporal_give, other_turned = barrier((sums, temporal_give, other_turned))
    temporal_got = swap_cores(temporal_give)
    low_keep, low_give, total = hidden_gradient(sums, clip_stat, part, h0, h1, count)
    low_got = swap_cores(low_give)
    packed = weight_gradients(
        mine_turned, other_turned, low_keep, low_got, temporal_keep, temporal_got
    )
    packed, mixed, part = barrier((packed, mixed, part))
    output = temporal(mixed, h0, h1, temporal_weight)
    input_grad = input_gradient(
        part, h0, h1, clip_stat, total, x, stat_one, gain_one, spatial_weight
    )
    shares = everyone_total(packed)
    shares, output, input_grad = barrier((shares, output, input_grad))
    mine = everyone_share(shares)
    other = swap_cores(mine)
    spatial_grad, temporal_grad = unpack(mine, other)
    return (
        output.reshape(clips.shape),
        input_grad.reshape(clips.shape),
        spatial_grad.reshape(3, 3, C, C),
        temporal_grad,
    )


def solution(mesh):
    fine = Mesh(mesh.devices.reshape(2, 4, 2, 4, 4), ("zl", "x", "c", "y", "zh"))
    return jax.shard_map(
        on_device,
        mesh=fine,
        in_specs=(P(DP, FRAME), P(DP, FRAME), P(), P(), P(), P()),
        out_specs=(P(DP, FRAME), P(DP, FRAME), P(), P()),
        check_vma=False,
    )
```

```python
import functools

import jax
import jax.numpy as jnp
from jax import lax
from jax.experimental import pallas as pl
from jax.experimental.pallas import tpu as pltpu
from jax.sharding import Mesh, PartitionSpec as P

epsilon = 1e-05

GROUPS = 32
DP = ("zl", "x", "c")
FRAME = ("y", "zh")
PLANE = ("x", "y")
LINE = ("zl", "zh")

C = 320
W = 32
PAD = 384
HALF = C // 2
PIX = 512
ROWS = 2 * PIX
STEP = 128
F32 = jnp.float32
BF16 = jnp.bfloat16

MIB = 1024 * 1024


def call(body, out, scratch=(), flops=0, limit=12):
    return pl.pallas_call(
        body,
        out_shape=out,
        scratch_shapes=list(scratch),
        compiler_params=pltpu.CompilerParams(vmem_limit_bytes=limit * MIB),
        cost_estimate=pl.CostEstimate(flops=flops, transcendentals=0, bytes_accessed=8_000_000),
    )


def shape(dims, kind):
    return jax.ShapeDtypeStruct(dims, kind)


def inner(dims, kind):
    return pltpu.VMEM(dims, kind)


def at(step, size=STEP):
    return pl.ds(pl.multiple_of(step * size, size), size)


def group_sum(rows):
    per = C // GROUPS
    one = lax.broadcasted_iota(jnp.int32, (C, C), 0) * 6554 >> 16
    two = lax.broadcasted_iota(jnp.int32, (C, C), 1) * 6554 >> 16
    assert per == 10
    same = jnp.where(one == two, 1.0, 0.0).astype(F32)
    return jnp.dot(rows, same, precision=lax.Precision.HIGHEST, preferred_element_type=F32)


def fold(value):
    return jnp.sum(value.reshape(value.shape[0] // 8, 8, value.shape[1]), axis=0)


def column(width):
    return lax.broadcasted_iota(jnp.int32, (STEP, width), 0) & (W - 1)


def four(*sums):
    return jnp.concatenate([jnp.sum(s, axis=0, keepdims=True) for s in sums] + [jnp.zeros((8 - len(sums), C), F32)])


def sigmoid(value):
    return 1.0 / (1.0 + jnp.exp(-value))


def forward_body(x_ref, w_ref, gain_ref, h0_ref, h1_ref, turned_ref, stat_ref, sums_ref, wf, x3, y):
    for i in range(3):
        for j in range(3):
            wf[C * j : C * (j + 1), PAD * i : PAD * i + C] = w_ref[3 * i + j]
    zero = jnp.zeros((8, C), F32)

    def moments(step, carry):
        value = x_ref[at(step), :].astype(F32)
        return carry[0] + fold(value), carry[1] + fold(value * value)

    half = PIX // STEP
    s0, q0 = lax.fori_loop(0, half, moments, (zero, zero))
    s1, q1 = lax.fori_loop(half, 2 * half, moments, (zero, zero))
    grouped = group_sum(four(s0, q0, s1, q1)) * (1.0 / (PIX * C // GROUPS))
    stats = []
    for f in range(2):
        mean = grouped[2 * f : 2 * f + 1]
        var = grouped[2 * f + 1 : 2 * f + 2] - mean * mean
        stats += [mean, lax.rsqrt(var + epsilon)]
    stat_ref[...] = jnp.concatenate(stats + [jnp.zeros((4, C), F32)])
    gain = gain_ref[...].reshape(1, C)
    edge = column(C)

    def activate(step, mean, scale):
        value = x_ref[at(step), :].astype(F32)
        pre = (value - mean) * scale * gain
        act = pre / (1.0 + jnp.exp(-pre))
        low = act.astype(BF16)
        act = low.astype(F32)
        x3[at(step), 0:C] = jnp.where(edge == 0, 0.0, pltpu.roll(act, 1, 0)).astype(BF16)
        x3[at(step), C : 2 * C] = low
        x3[at(step), 2 * C : 3 * C] = jnp.where(
            edge == W - 1, 0.0, pltpu.roll(act, STEP - 1, 0)
        ).astype(BF16)

    total = (zero, zero)
    for f in range(2):
        mean, scale = stats[2 * f], stats[2 * f + 1]

        def act_step(step, carry, mean=mean, scale=scale):
            activate(step, mean, scale)
            return carry

        lax.fori_loop(f * half, (f + 1) * half, act_step, 0)
        y[f, 0:W, :] = jnp.zeros((W, 3 * PAD), F32)
        y[f, W + PIX : 2 * W + PIX, :] = jnp.zeros((W, 3 * PAD), F32)
        y[f, W : W + PIX, :] = jnp.dot(
            x3[f * PIX : (f + 1) * PIX, :], wf[...], preferred_element_type=F32
        )

        turn(x3[f * PIX : (f + 1) * PIX, C : 2 * C], turned_ref, f * PIX)
        h_ref = (h0_ref, h1_ref)[f]

        def finish(step, carry, f=f, h_ref=h_ref):
            base = pl.multiple_of(step * STEP, STEP)
            conv = (
                y[f, pl.ds(base, STEP), 0:C]
                + y[f, pl.ds(base + W, STEP), PAD : PAD + C]
                + y[f, pl.ds(base + 2 * W, STEP), 2 * PAD : 2 * PAD + C]
            )
            value = x_ref[pl.ds(base + f * PIX, STEP), :].astype(F32)
            low = (value + conv).astype(BF16)
            h_ref[pl.ds(base, STEP), :] = low
            value = low.astype(F32)
            return carry[0] + fold(value), carry[1] + fold(value * value)

        total = lax.fori_loop(0, half, finish, total)
    spread(total, sums_ref)


def spread(total, sums_ref):
    first = jnp.sum(total[0], axis=0, keepdims=True)
    second = jnp.sum(total[1], axis=0, keepdims=True)
    both = jnp.concatenate([first, second])
    for k in range(sums_ref.shape[0]):
        sums_ref[k] = both


def turn(acts, out_ref, base):
    rows = lax.broadcasted_iota(jnp.int32, (C, C), 0)
    same = jnp.where(rows == lax.broadcasted_iota(jnp.int32, (C, C), 1), 1.0, 0.0).astype(BF16)
    lane = lax.broadcasted_iota(jnp.int32, (C, STEP), 1) & (W - 1)
    moved = times_transposed(same, acts)
    for step in range(PIX // STEP):
        part = moved[:, step * STEP : (step + 1) * STEP]
        where = slice(base + step * STEP, base + (step + 1) * STEP)
        out_ref[0:C, where] = jnp.where(lane == 0, 0.0, pltpu.roll(part, 1, 1)).astype(BF16)
        out_ref[C : 2 * C, where] = part.astype(BF16)
        out_ref[2 * C : 3 * C, where] = jnp.where(
            lane == W - 1, 0.0, pltpu.roll(part, STEP - 1, 1)
        ).astype(BF16)


def forward(x, weight, gain, peers):
    return call(
        forward_body,
        (
            shape((PIX, C), BF16),
            shape((PIX, C), BF16),
            shape((3 * C, ROWS), BF16),
            shape((8, C), F32),
            shape((peers, 2, C), F32),
        ),
        (
            pltpu.VMEM((3 * C, 3 * PAD), BF16),
            pltpu.VMEM((ROWS, 3 * C), BF16),
            pltpu.VMEM((2, PIX + 2 * W, 3 * PAD), F32),
        ),
        flops=2_500_000_000,
        limit=20,
    )(x, weight, gain)


def times_transposed(a, b):
    return lax.dot_general(a, b, (((1,), (1,)), ((), ())), preferred_element_type=F32)


def mixed_grad_body(before_ref, cot_ref, after_ref, w_ref, out_ref):
    for f in range(2):
        last = cot_ref[0:PIX, :] if f else before_ref[...]
        here = cot_ref[f * PIX : (f + 1) * PIX, :]
        later = after_ref[...] if f else cot_ref[PIX:ROWS, :]
        total = times_transposed(later, w_ref[0])
        total = total + times_transposed(here, w_ref[1])
        total = total + times_transposed(last, w_ref[2])
        out_ref[f * PIX : (f + 1) * PIX, :] = total.astype(BF16)


def mixed_gradient(before, cot, after, weight):
    return call(mixed_grad_body, shape((ROWS, C), BF16), flops=1_500_000_000)(
        before, cot, after, weight
    )


def clip_stats(sums_ref, count):
    total = jnp.sum(sums_ref[...], axis=0)
    grouped = group_sum(jnp.concatenate([total, jnp.zeros((6, C), F32)])) * (1.0 / count)
    return grouped[0:1], grouped[1:2]


def slope_body(
    count, sums_ref, h0_ref, h1_ref, grad_ref, cot_ref, gain_ref, part_ref, stat_ref, out_ref
):
    mean, square = clip_stats(sums_ref, count)
    scale = lax.rsqrt(square - mean * mean + epsilon)
    stat_ref[...] = jnp.concatenate([mean, scale, jnp.zeros((6, C), F32)])
    gain = gain_ref[...].reshape(1, C)
    zero = jnp.zeros((8, C), F32)
    total = (zero, zero)
    for f, h_ref in enumerate((h0_ref, h1_ref)):

        def step_body(step, carry, f=f, h_ref=h_ref):
            base = pl.multiple_of(step * STEP, STEP)
            hat = (h_ref[pl.ds(base, STEP), :].astype(F32) - mean) * scale
            pre = hat * gain
            s = sigmoid(pre)
            slope = s * (1.0 + pre * (1.0 - s))
            dhat = grad_ref[pl.ds(base + f * PIX, STEP), :].astype(F32) * slope * gain
            there = pl.ds(base + f * PIX, STEP)
            part_ref[there, :] = cot_ref[there, :].astype(F32) + scale * dhat
            return carry[0] + fold(dhat), carry[1] + fold(dhat * hat)

        total = lax.fori_loop(0, PIX // STEP, step_body, total)
    spread(total, out_ref)


def slopes(sums, h0, h1, grad, cot, gain, count):
    return call(
        functools.partial(slope_body, count),
        (shape((ROWS, C), F32), shape((8, C), F32), shape(sums.shape, F32)),
    )(sums, h0, h1, grad, cot, gain)


def mixed_body(
    hb_ref, h0_ref, h1_ref, ha_ref, cot_ref, stat_ref, gain_ref, mx_ref, keep_ref, give_ref, turned
):
    mean, scale = stat_ref[0:1, :], stat_ref[1:2, :]
    gain = gain_ref[...].reshape(1, C)
    place = lax.axis_index(FRAME)
    live = (place > 0, None, None, place < lax.axis_size(FRAME) - 1)
    for n, h_ref in enumerate((hb_ref, h0_ref, h1_ref, ha_ref)):

        def step_body(step, carry, n=n, h_ref=h_ref):
            base = pl.multiple_of(step * STEP, STEP)
            pre = (h_ref[pl.ds(base, STEP), :].astype(F32) - mean) * scale * gain
            act = pre / (1.0 + jnp.exp(-pre))
            if live[n] is not None:
                act = jnp.where(live[n], act, 0.0)
            mx_ref[pl.ds(base + n * PIX, STEP), :] = act.astype(BF16)
            return carry

        lax.fori_loop(0, PIX // STEP, step_body, 0)
    for n in range(4 * PIX // STEP):
        where = slice(n * STEP, (n + 1) * STEP)
        turned[:, where] = mx_ref[where, :].T
    core = lax.axis_index("c")
    for k in range(3):
        part = jnp.dot(
            turned[:, k * PIX : k * PIX + ROWS], cot_ref[...], preferred_element_type=F32
        )
        left, right = part[:, 0:HALF], part[:, HALF:C]
        keep_ref[k * C : (k + 1) * C, 0:HALF] = jnp.where(core == 0, left, right)
        give_ref[k * C : (k + 1) * C, 0:HALF] = jnp.where(core == 0, right, left)


def mixed_frames(before, h0, h1, after, cot, stat, gain):
    return call(
        mixed_body,
        (shape((4 * PIX, C), BF16), shape((3 * C, 256), F32), shape((3 * C, 256), F32)),
        (pltpu.VMEM((C, 4 * PIX), BF16),),
        flops=1_500_000_000,
    )(before, h0, h1, after, cot, stat, gain)


def temporal_body(mx_ref, h0_ref, h1_ref, w_ref, out_ref):
    for f, h_ref in enumerate((h0_ref, h1_ref)):
        total = None
        for k in range(3):
            part = jnp.dot(
                mx_ref[(f + k) * PIX : (f + k + 1) * PIX, :],
                w_ref[k],
                preferred_element_type=F32,
            )
            total = part if total is None else total + part
        low = total.astype(BF16).astype(F32)
        out_ref[f * PIX : (f + 1) * PIX, :] = (h_ref[...].astype(F32) + low).astype(BF16)


def temporal(mixed, h0, h1, weight):
    return call(temporal_body, shape((ROWS, C), BF16), flops=1_500_000_000)(mixed, h0, h1, weight)


def whole_grad(part_ref, h_ref, stat_ref, sums, base, f):
    mean, scale = stat_ref[0:1, :], stat_ref[1:2, :]
    hat = (h_ref[pl.ds(base, STEP), :].astype(F32) - mean) * scale
    return part_ref[pl.ds(base + f * PIX, STEP), :] - scale * (sums[0] + hat * sums[1])


def hidden_grad_body(
    count, sums_ref, stat_ref, part_ref, h0_ref, h1_ref, keep_ref, give_ref, total_ref
):
    sums = clip_stats(sums_ref, count)
    total_ref[...] = jnp.concatenate([*sums, jnp.zeros((6, C), F32)])
    core = lax.axis_index("c")
    for f, h_ref in enumerate((h0_ref, h1_ref)):

        def step_body(step, carry, f=f, h_ref=h_ref):
            base = pl.multiple_of(step * STEP, STEP)
            here = pl.ds(base + f * PIX, STEP)
            grad = whole_grad(part_ref, h_ref, stat_ref, sums, base, f)
            left, right = grad[:, 0:HALF], grad[:, HALF:C]
            keep_ref[here, :] = jnp.where(core == 0, left, right).astype(BF16)
            give_ref[here, :] = jnp.where(core == 0, right, left).astype(BF16)
            return carry

        lax.fori_loop(0, PIX // STEP, step_body, 0)


def hidden_gradient(sums, stat, part, h0, h1, count):
    return call(
        functools.partial(hidden_grad_body, count),
        (shape((ROWS, HALF), BF16), shape((ROWS, HALF), BF16), shape((8, C), F32)),
    )(sums, stat, part, h0, h1)


def row_taps(value):
    none = jnp.zeros((W, value.shape[1]), value.dtype)
    return (
        jnp.concatenate([value[W:], none]),
        value,
        jnp.concatenate([none, value[: PIX - W]]),
    )


def weight_grad_body(
    mine_turned_ref, other_turned_ref, mine_ref, other_ref, keep_ref, got_ref, out_ref, rhs
):
    total = None
    for n, (ref, turned_ref) in enumerate(
        ((mine_ref, mine_turned_ref), (other_ref, other_turned_ref))
    ):
        for f in range(2):
            where = slice(f * PIX, (f + 1) * PIX)
            for i, tap in enumerate(row_taps(ref[where, :])):
                rhs[n, where, i * HALF : (i + 1) * HALF] = tap
        part = jnp.dot(turned_ref[...], rhs[n], preferred_element_type=F32)
        total = part if total is None else total + part
    out_ref[0 : 3 * C, 0 : 3 * HALF] = total.astype(BF16)
    kept = keep_ref[:, 0:HALF] + got_ref[:, 0:HALF]
    out_ref[0 : 3 * C, 3 * HALF : 4 * HALF] = kept.astype(BF16)
    out_ref[3 * C :, :] = jnp.zeros((1024 - 3 * C, 4 * HALF), BF16)


def weight_gradients(mine_turned, other_turned, mine, other, keep, got):
    return call(
        weight_grad_body,
        shape((1024, 4 * HALF), BF16),
        (pltpu.VMEM((2, ROWS, 3 * HALF), BF16),),
        flops=2_500_000_000,
    )(mine_turned, other_turned, mine, other, keep, got)


def input_grad_body(
    part_ref, h0_ref, h1_ref, clip_ref, total_ref, x_ref, stat_ref, gain_ref, w_ref,
    out_ref, wb, rows, z, dh, grads, lows,
):
    clip_sums = total_ref[0:1, :], total_ref[1:2, :]
    for j in range(3):
        for i in range(3):
            wb[PAD * j : PAD * j + C, C * i : C * (i + 1)] = w_ref[3 * i + j]
        wb[PAD * j + C : PAD * (j + 1), :] = jnp.zeros((PAD - C, 3 * C), BF16)
    gain = gain_ref[...].reshape(1, C)
    edge = column(C)
    half = PIX // STEP
    for f in range(2):
        mean, scale = stat_ref[2 * f : 2 * f + 1, :], stat_ref[2 * f + 1 : 2 * f + 2, :]
        h_ref = (h0_ref, h1_ref)[f]

        def grad_body(step, carry, f=f, h_ref=h_ref):
            base = pl.multiple_of(step * STEP, STEP)
            grad = whole_grad(part_ref, h_ref, clip_ref, clip_sums, base, f)
            grads[pl.ds(base, STEP), :] = grad
            lows[pl.ds(base, STEP), :] = grad.astype(BF16)
            return carry

        lax.fori_loop(0, half, grad_body, 0)
        for i, tap in enumerate(row_taps(lows[...])):
            rows[:, i * C : (i + 1) * C] = tap
        z[...] = times_transposed(rows[...], wb[...])

        def step_body(step, carry, f=f, mean=mean, scale=scale):
            base = pl.multiple_of(step * STEP, STEP)
            here = pl.ds(base, STEP)
            right = jnp.where(edge == W - 1, 0.0, pltpu.roll(z[here, 0:C], STEP - 1, 0))
            left = jnp.where(edge == 0, 0.0, pltpu.roll(z[here, 2 * PAD : 2 * PAD + C], 1, 0))
            acts_grad = right + z[here, PAD : PAD + C] + left
            hat = (x_ref[pl.ds(base + f * PIX, STEP), :].astype(F32) - mean) * scale
            pre = hat * gain
            s = sigmoid(pre)
            dhat = acts_grad * (s * (1.0 + pre * (1.0 - s))) * gain
            dh[here, :] = dhat
            return carry[0] + fold(dhat), carry[1] + fold(dhat * hat)

        zero = jnp.zeros((8, C), F32)
        sums = lax.fori_loop(0, half, step_body, (zero, zero))
        grouped = group_sum(four(*sums)) * (1.0 / (PIX * C // GROUPS))
        first, second = grouped[0:1], grouped[1:2]

        def last_body(step, carry, f=f, mean=mean, scale=scale, first=first, second=second):
            base = pl.multiple_of(step * STEP, STEP)
            there = pl.ds(base + f * PIX, STEP)
            hat = (x_ref[there, :].astype(F32) - mean) * scale
            here = pl.ds(base, STEP)
            value = grads[here, :] + scale * (dh[here, :] - first - hat * second)
            out_ref[there, :] = value.astype(BF16)
            return carry

        lax.fori_loop(0, half, last_body, 0)


def input_gradient(part, h0, h1, clip_stat, total, x, stat, gain, weight):
    return call(
        input_grad_body,
        shape((ROWS, C), BF16),
        (
            pltpu.VMEM((3 * PAD, 3 * C), BF16),
            pltpu.VMEM((PIX, 3 * C), BF16),
            pltpu.VMEM((PIX, 3 * PAD), F32),
            pltpu.VMEM((PIX, C), F32),
            pltpu.VMEM((PIX, C), F32),
            pltpu.VMEM((PIX, C), BF16),
        ),
        flops=2_500_000_000,
        limit=16,
    )(part, h0, h1, clip_stat, total, x, stat, gain, weight)


def unpack_body(mine_ref, other_ref, spatial_ref, temporal_ref):
    core = lax.axis_index("c")
    for j in range(3):
        here = slice(j * C, (j + 1) * C)
        mine, other = mine_ref[here, :], other_ref[here, :]
        left = jnp.where(core == 0, mine, other)
        right = jnp.where(core == 0, other, mine)
        for i in range(4):
            lanes = slice(i * HALF, (i + 1) * HALF)
            if i < 3:
                spatial_ref[3 * i + j, :, 0:HALF] = left[:, lanes]
                spatial_ref[3 * i + j, :, HALF:C] = right[:, lanes]
            else:
                temporal_ref[j, :, 0:HALF] = left[:, lanes]
                temporal_ref[j, :, HALF:C] = right[:, lanes]


def unpack(mine, other):
    return call(unpack_body, (shape((9, C, C), BF16), shape((3, C, C), BF16)))(mine, other)


def neighbours(first, second):
    size = lax.axis_size(FRAME)
    before = lax.ppermute(second, FRAME, [(i, i + 1) for i in range(size - 1)])
    after = lax.ppermute(first, FRAME, [(i + 1, i) for i in range(size - 1)])
    return before, after


def swap_cores(value):
    return lax.ppermute(value, "c", [(0, 1), (1, 0)])


def everyone_total(value):
    plane = lax.axis_size(PLANE)
    value = value.reshape(plane, 1024 // plane, value.shape[1])
    return lax.all_to_all(value, PLANE, 0, 0)


def everyone_share(value):
    plane, line = lax.axis_size(PLANE), lax.axis_size(LINE)
    width = value.shape[2]
    value = jnp.sum(value.astype(F32), axis=0)
    value = value.reshape(line, 1024 // plane // line, width)
    value = jnp.sum(lax.all_to_all(value, LINE, 0, 0), axis=0).astype(BF16)
    value = jnp.broadcast_to(value[None], (line,) + value.shape)
    value = lax.all_to_all(value, LINE, 0, 0).reshape(1024 // plane, width)
    value = jnp.broadcast_to(value[None], (plane,) + value.shape)
    return lax.all_to_all(value, PLANE, 0, 0).reshape(1024, width)


def on_device(clips, cotangent, spatial_weight, temporal_weight, gain_one, gain_two):
    size = lax.axis_size(FRAME)
    count = float(size * ROWS * C // GROUPS)
    x = clips.reshape(ROWS, C)
    cot = cotangent.reshape(ROWS, C)
    spatial_weight = spatial_weight.reshape(9, C, C)
    barrier = lax.optimization_barrier
    cot_before, cot_after = neighbours(cot[:PIX], cot[PIX:])
    h0, h1, mine_turned, stat_one, sums = forward(x, spatial_weight, gain_one, size)
    sums = lax.all_to_all(sums, FRAME, 0, 0)
    edge0, edge1, cot_before, cot_after = barrier((h0, h1, cot_before, cot_after))
    before, after = neighbours(edge0, edge1)
    mixed_grad = mixed_gradient(cot_before, cot, cot_after, temporal_weight)
    sums, mixed_grad, mine_turned = barrier((sums, mixed_grad, mine_turned))
    part, clip_stat, sums = slopes(sums, h0, h1, mixed_grad, cot, gain_two, count)
    sums = lax.all_to_all(sums, FRAME, 0, 0)
    other_turned = swap_cores(mine_turned)
    mixed, temporal_keep, temporal_give = mixed_frames(
        before, h0, h1, after, cot, clip_stat, gain_two
    )
    sums, temporal_give, other_turned = barrier((sums, temporal_give, other_turned))
    temporal_got = swap_cores(temporal_give)
    low_keep, low_give, total = hidden_gradient(sums, clip_stat, part, h0, h1, count)
    low_got = swap_cores(low_give)
    packed = weight_gradients(
        mine_turned, other_turned, low_keep, low_got, temporal_keep, temporal_got
    )
    packed, mixed, part = barrier((packed, mixed, part))
    output = temporal(mixed, h0, h1, temporal_weight)
    input_grad = input_gradient(
        part, h0, h1, clip_stat, total, x, stat_one, gain_one, spatial_weight
    )
    shares = everyone_total(packed)
    shares, output, input_grad = barrier((shares, output, input_grad))
    mine = everyone_share(shares)
    other = swap_cores(mine)
    spatial_grad, temporal_grad = unpack(mine, other)
    return (
        output.reshape(clips.shape),
        input_grad.reshape(clips.shape),
        spatial_grad.reshape(3, 3, C, C),
        temporal_grad,
    )


def solution(mesh):
    fine = Mesh(mesh.devices.reshape(2, 4, 2, 4, 4), ("zl", "x", "c", "y", "zh"))
    return jax.shard_map(
        on_device,
        mesh=fine,
        in_specs=(P(DP, FRAME), P(DP, FRAME), P(), P(), P(), P()),
        out_specs=(P(DP, FRAME), P(DP, FRAME), P(), P()),
        check_vma=False,
    )
```

```python
import functools

import jax
import jax.numpy as jnp
from jax import lax
from jax.experimental import pallas as pl
from jax.experimental.pallas import tpu as pltpu
from jax.sharding import Mesh, PartitionSpec as P

epsilon = 1e-05

GROUPS = 32
DP = ("zl", "x", "c")
FRAME = ("y", "zh")
PLANE = ("x", "y")
LINE = ("zl", "zh")

C = 320
W = 32
PAD = 384
HALF = C // 2
PIX = 512
ROWS = 2 * PIX
STEP = 128
F32 = jnp.float32
BF16 = jnp.bfloat16

MIB = 1024 * 1024


VMEM = pl.BlockSpec(memory_space=pltpu.VMEM)
FAR = pl.BlockSpec(memory_space=pltpu.HBM)


def call(body, out, scratch=(), flops=0, limit=12, ins=None, outs=None):
    specs = {}
    if ins is not None:
        specs = {"in_specs": ins, "out_specs": outs}
    return pl.pallas_call(
        body,
        out_shape=out,
        scratch_shapes=list(scratch),
        compiler_params=pltpu.CompilerParams(vmem_limit_bytes=limit * MIB),
        cost_estimate=pl.CostEstimate(flops=flops, transcendentals=0, bytes_accessed=8_000_000),
        **specs,
    )


def shape(dims, kind):
    return jax.ShapeDtypeStruct(dims, kind)


def far(dims, kind):
    return pltpu.HBM(dims, kind)


def at(step, size=STEP):
    return pl.ds(pl.multiple_of(step * size, size), size)


def group_sum(rows):
    per = C // GROUPS
    one = lax.broadcasted_iota(jnp.int32, (C, C), 0) * 6554 >> 16
    two = lax.broadcasted_iota(jnp.int32, (C, C), 1) * 6554 >> 16
    assert per == 10
    same = jnp.where(one == two, 1.0, 0.0).astype(F32)
    return jnp.dot(rows, same, precision=lax.Precision.HIGHEST, preferred_element_type=F32)


def fold(value):
    return jnp.sum(value.reshape(value.shape[0] // 8, 8, value.shape[1]), axis=0)


def column(width):
    return lax.broadcasted_iota(jnp.int32, (STEP, width), 0) & (W - 1)


def four(*sums):
    return jnp.concatenate([jnp.sum(s, axis=0, keepdims=True) for s in sums] + [jnp.zeros((8 - len(sums), C), F32)])


def sigmoid(value):
    return 1.0 / (1.0 + jnp.exp(-value))


def forward_body(
    x_ref, far_w_ref, gain_ref, h0_ref, h1_ref, far_turned_ref, stat_ref, sums_ref,
    w_ref, wf, x3, y, turned, w_sem, turned_sem,
):
    fetch = pltpu.make_async_copy(far_w_ref, w_ref, w_sem)
    fetch.start()
    zero = jnp.zeros((8, C), F32)

    def moments(step, carry):
        value = x_ref[at(step), :].astype(F32)
        return carry[0] + fold(value), carry[1] + fold(value * value)

    half = PIX // STEP
    s0, q0 = lax.fori_loop(0, half, moments, (zero, zero))
    s1, q1 = lax.fori_loop(half, 2 * half, moments, (zero, zero))
    grouped = group_sum(four(s0, q0, s1, q1)) * (1.0 / (PIX * C // GROUPS))
    stats = []
    for f in range(2):
        mean = grouped[2 * f : 2 * f + 1]
        var = grouped[2 * f + 1 : 2 * f + 2] - mean * mean
        stats += [mean, lax.rsqrt(var + epsilon)]
    stat_ref[...] = jnp.concatenate(stats + [jnp.zeros((4, C), F32)])
    gain = gain_ref[...].reshape(1, C)
    edge = column(C)

    def activate(step, mean, scale):
        value = x_ref[at(step), :].astype(F32)
        pre = (value - mean) * scale * gain
        act = pre / (1.0 + jnp.exp(-pre))
        low = act.astype(BF16)
        act = low.astype(F32)
        x3[at(step), 0:C] = jnp.where(edge == 0, 0.0, pltpu.roll(act, 1, 0)).astype(BF16)
        x3[at(step), C : 2 * C] = low
        x3[at(step), 2 * C : 3 * C] = jnp.where(
            edge == W - 1, 0.0, pltpu.roll(act, STEP - 1, 0)
        ).astype(BF16)

    total = (zero, zero)
    sends = []
    for f in range(2):
        mean, scale = stats[2 * f], stats[2 * f + 1]

        def act_step(step, carry, mean=mean, scale=scale):
            activate(step, mean, scale)
            return carry

        lax.fori_loop(f * half, (f + 1) * half, act_step, 0)
        if f == 0:
            fetch.wait()
            for i in range(3):
                for j in range(3):
                    wf[C * j : C * (j + 1), PAD * i : PAD * i + C] = w_ref[3 * i + j]
        y[f, 0:W, :] = jnp.zeros((W, 3 * PAD), F32)
        y[f, W + PIX : 2 * W + PIX, :] = jnp.zeros((W, 3 * PAD), F32)
        y[f, W : W + PIX, :] = jnp.dot(
            x3[f * PIX : (f + 1) * PIX, :], wf[...], preferred_element_type=F32
        )

        turn(x3[f * PIX : (f + 1) * PIX, C : 2 * C], turned.at[f])
        send = pltpu.make_async_copy(
            turned.at[f], far_turned_ref.at[:, f * PIX : (f + 1) * PIX], turned_sem.at[f]
        )
        send.start()
        sends.append(send)
        h_ref = (h0_ref, h1_ref)[f]

        def finish(step, carry, f=f, h_ref=h_ref):
            base = pl.multiple_of(step * STEP, STEP)
            conv = (
                y[f, pl.ds(base, STEP), 0:C]
                + y[f, pl.ds(base + W, STEP), PAD : PAD + C]
                + y[f, pl.ds(base + 2 * W, STEP), 2 * PAD : 2 * PAD + C]
            )
            value = x_ref[pl.ds(base + f * PIX, STEP), :].astype(F32)
            low = (value + conv).astype(BF16)
            h_ref[pl.ds(base, STEP), :] = low
            value = low.astype(F32)
            return carry[0] + fold(value), carry[1] + fold(value * value)

        total = lax.fori_loop(0, half, finish, total)
    spread(total, sums_ref)
    for send in sends:
        send.wait()


def spread(total, sums_ref):
    first = jnp.sum(total[0], axis=0, keepdims=True)
    second = jnp.sum(total[1], axis=0, keepdims=True)
    both = jnp.concatenate([first, second])
    for k in range(sums_ref.shape[0]):
        sums_ref[k] = both


def turn(acts, out_ref):
    rows = lax.broadcasted_iota(jnp.int32, (C, C), 0)
    same = jnp.where(rows == lax.broadcasted_iota(jnp.int32, (C, C), 1), 1.0, 0.0).astype(BF16)
    lane = lax.broadcasted_iota(jnp.int32, (C, STEP), 1) & (W - 1)
    moved = times_transposed(same, acts)
    for step in range(PIX // STEP):
        part = moved[:, step * STEP : (step + 1) * STEP]
        where = slice(step * STEP, (step + 1) * STEP)
        out_ref[0:C, where] = jnp.where(lane == 0, 0.0, pltpu.roll(part, 1, 1)).astype(BF16)
        out_ref[C : 2 * C, where] = part.astype(BF16)
        out_ref[2 * C : 3 * C, where] = jnp.where(
            lane == W - 1, 0.0, pltpu.roll(part, STEP - 1, 1)
        ).astype(BF16)


def forward(x, weight, gain, peers):
    return call(
        forward_body,
        (
            shape((PIX, C), BF16),
            shape((PIX, C), BF16),
            far((3 * C, ROWS), BF16),
            shape((8, C), F32),
            shape((peers, 2, C), F32),
        ),
        (
            pltpu.VMEM((9, C, C), BF16),
            pltpu.VMEM((3 * C, 3 * PAD), BF16),
            pltpu.VMEM((ROWS, 3 * C), BF16),
            pltpu.VMEM((2, PIX + 2 * W, 3 * PAD), F32),
            pltpu.VMEM((2, 3 * C, PIX), BF16),
            pltpu.SemaphoreType.DMA,
            pltpu.SemaphoreType.DMA((2,)),
        ),
        flops=2_500_000_000,
        limit=24,
        ins=[VMEM, FAR, VMEM],
        outs=(VMEM, VMEM, FAR, VMEM, VMEM),
    )(x, pltpu.with_memory_space_constraint(weight, pltpu.HBM), gain)


def times_transposed(a, b):
    return lax.dot_general(a, b, (((1,), (1,)), ((), ())), preferred_element_type=F32)


def clip_stats(sums_ref, count):
    total = jnp.sum(sums_ref[...], axis=0)
    grouped = group_sum(jnp.concatenate([total, jnp.zeros((6, C), F32)])) * (1.0 / count)
    return grouped[0:1], grouped[1:2]


def mixed_grad_body(before_ref, cot_ref, after_ref, w_ref, out_ref):
    for f in range(2):
        last = cot_ref[0:PIX, :] if f else before_ref[...]
        later = after_ref[...] if f else cot_ref[PIX:ROWS, :]
        total = times_transposed(later, w_ref[0])
        total = total + times_transposed(cot_ref[f * PIX : (f + 1) * PIX, :], w_ref[1])
        total = total + times_transposed(last, w_ref[2])
        out_ref[f * PIX : (f + 1) * PIX, :] = total.astype(BF16)


def mixed_gradient(before, cot, after, weight):
    return call(mixed_grad_body, far((ROWS, C), BF16), flops=1_500_000_000)(
        before, cot, after, weight
    )


def slope_body(
    count, sums_ref, h0_ref, h1_ref, grad_ref, cot_ref, gain_ref, part_ref, stat_ref, out_ref
):
    mean, square = clip_stats(sums_ref, count)
    scale = lax.rsqrt(square - mean * mean + epsilon)
    stat_ref[...] = jnp.concatenate([mean, scale, jnp.zeros((6, C), F32)])
    gain = gain_ref[...].reshape(1, C)
    zero = jnp.zeros((8, C), F32)
    total = (zero, zero)
    for f, h_ref in enumerate((h0_ref, h1_ref)):

        def step_body(step, carry, f=f, h_ref=h_ref):
            base = pl.multiple_of(step * STEP, STEP)
            there = pl.ds(base + f * PIX, STEP)
            hat = (h_ref[pl.ds(base, STEP), :].astype(F32) - mean) * scale
            pre = hat * gain
            s = sigmoid(pre)
            slope = s * (1.0 + pre * (1.0 - s))
            dhat = grad_ref[there, :].astype(F32) * slope * gain
            part_ref[there, :] = cot_ref[there, :].astype(F32) + scale * dhat
            return carry[0] + fold(dhat), carry[1] + fold(dhat * hat)

        total = lax.fori_loop(0, PIX // STEP, step_body, total)
    spread(total, out_ref)


def slopes(sums, h0, h1, grad, cot, gain, count):
    return call(
        functools.partial(slope_body, count),
        (shape((ROWS, C), F32), shape((8, C), F32), shape(sums.shape, F32)),
    )(sums, h0, h1, grad, cot, gain)


def mixed_body(
    hb_ref, h0_ref, h1_ref, ha_ref, cot_ref, stat_ref, gain_ref, sums_ref,
    far_mx_ref, keep_ref, give_ref, mx_ref, turned, sem,
):
    mean, scale = stat_ref[0:1, :], stat_ref[1:2, :]
    gain = gain_ref[...].reshape(1, C)
    place = lax.axis_index(FRAME)
    live = (place > 0, None, None, place < lax.axis_size(FRAME) - 1)
    for n, h_ref in enumerate((hb_ref, h0_ref, h1_ref, ha_ref)):

        def step_body(step, carry, n=n, h_ref=h_ref):
            base = pl.multiple_of(step * STEP, STEP)
            pre = (h_ref[pl.ds(base, STEP), :].astype(F32) - mean) * scale * gain
            act = pre / (1.0 + jnp.exp(-pre))
            if live[n] is not None:
                act = jnp.where(live[n], act, 0.0)
            mx_ref[pl.ds(base + n * PIX, STEP), :] = act.astype(BF16)
            return carry

        lax.fori_loop(0, PIX // STEP, step_body, 0)
    send = pltpu.make_async_copy(mx_ref, far_mx_ref, sem)
    send.start()
    for n in range(4 * PIX // STEP):
        where = slice(n * STEP, (n + 1) * STEP)
        turned[:, where] = mx_ref[where, :].T
    core = lax.axis_index("c")
    for k in range(3):
        part = jnp.dot(
            turned[:, k * PIX : k * PIX + ROWS], cot_ref[...], preferred_element_type=F32
        )
        left, right = part[:, 0:HALF], part[:, HALF:C]
        keep_ref[k * C : (k + 1) * C, 0:HALF] = jnp.where(core == 0, left, right)
        give_ref[k * C : (k + 1) * C, 0:HALF] = jnp.where(core == 0, right, left)
    send.wait()


def mixed_frames(before, h0, h1, after, cot, stat, gain, sums):
    return call(
        mixed_body,
        (far((4 * PIX, C), BF16), shape((3 * C, 256), F32), shape((3 * C, 256), F32)),
        (
            pltpu.VMEM((4 * PIX, C), BF16),
            pltpu.VMEM((C, 4 * PIX), BF16),
            pltpu.SemaphoreType.DMA,
        ),
        flops=1_500_000_000,
        limit=12,
        ins=[VMEM] * 8,
        outs=(FAR, VMEM, VMEM),
    )(before, h0, h1, after, cot, stat, gain, sums)


def temporal_body(mx_ref, h0_ref, h1_ref, w_ref, out_ref):
    for f, h_ref in enumerate((h0_ref, h1_ref)):
        total = None
        for k in range(3):
            part = jnp.dot(
                mx_ref[(f + k) * PIX : (f + k + 1) * PIX, :],
                w_ref[k],
                preferred_element_type=F32,
            )
            total = part if total is None else total + part
        low = total.astype(BF16).astype(F32)
        out_ref[f * PIX : (f + 1) * PIX, :] = (h_ref[...].astype(F32) + low).astype(BF16)


def temporal(mixed, h0, h1, weight):
    return call(temporal_body, shape((ROWS, C), BF16), flops=1_500_000_000)(mixed, h0, h1, weight)


def whole_grad(part_ref, h_ref, stat_ref, sums, base, f):
    mean, scale = stat_ref[0:1, :], stat_ref[1:2, :]
    hat = (h_ref[pl.ds(base, STEP), :].astype(F32) - mean) * scale
    return part_ref[pl.ds(base + f * PIX, STEP), :] - scale * (sums[0] + hat * sums[1])


def hidden_grad_body(
    count, sums_ref, stat_ref, part_ref, h0_ref, h1_ref, keep_ref, give_ref, total_ref
):
    sums = clip_stats(sums_ref, count)
    total_ref[...] = jnp.concatenate([*sums, jnp.zeros((6, C), F32)])
    core = lax.axis_index("c")
    for f, h_ref in enumerate((h0_ref, h1_ref)):

        def step_body(step, carry, f=f, h_ref=h_ref):
            base = pl.multiple_of(step * STEP, STEP)
            here = pl.ds(base + f * PIX, STEP)
            grad = whole_grad(part_ref, h_ref, stat_ref, sums, base, f)
            left, right = grad[:, 0:HALF], grad[:, HALF:C]
            keep_ref[here, :] = jnp.where(core == 0, left, right).astype(BF16)
            give_ref[here, :] = jnp.where(core == 0, right, left).astype(BF16)
            return carry

        lax.fori_loop(0, PIX // STEP, step_body, 0)


def hidden_gradient(sums, stat, part, h0, h1, count):
    return call(
        functools.partial(hidden_grad_body, count),
        (shape((ROWS, HALF), BF16), shape((ROWS, HALF), BF16), shape((8, C), F32)),
    )(sums, stat, part, h0, h1)


def row_taps(value):
    none = jnp.zeros((W, value.shape[1]), value.dtype)
    return (
        jnp.concatenate([value[W:], none]),
        value,
        jnp.concatenate([none, value[: PIX - W]]),
    )


def weight_grad_body(
    mine_turned_ref, other_turned_ref, mine_ref, other_ref, keep_ref, got_ref, out_ref, rhs
):
    total = None
    for n, (ref, turned_ref) in enumerate(
        ((mine_ref, mine_turned_ref), (other_ref, other_turned_ref))
    ):
        for f in range(2):
            where = slice(f * PIX, (f + 1) * PIX)
            for i, tap in enumerate(row_taps(ref[where, :])):
                rhs[n, where, i * HALF : (i + 1) * HALF] = tap
        part = jnp.dot(turned_ref[...], rhs[n], preferred_element_type=F32)
        total = part if total is None else total + part
    out_ref[0 : 3 * C, 0 : 3 * HALF] = total.astype(BF16)
    kept = keep_ref[:, 0:HALF] + got_ref[:, 0:HALF]
    out_ref[0 : 3 * C, 3 * HALF : 4 * HALF] = kept.astype(BF16)
    out_ref[3 * C :, :] = jnp.zeros((1024 - 3 * C, 4 * HALF), BF16)


def weight_gradients(mine_turned, other_turned, mine, other, keep, got):
    return call(
        weight_grad_body,
        shape((1024, 4 * HALF), BF16),
        (pltpu.VMEM((2, ROWS, 3 * HALF), BF16),),
        flops=2_500_000_000,
    )(mine_turned, other_turned, mine, other, keep, got)


def input_grad_body(
    part_ref, h0_ref, h1_ref, clip_ref, total_ref, x_ref, stat_ref, gain_ref, w_ref,
    out_ref, wb, rows, z, dh, grads, lows,
):
    clip_sums = total_ref[0:1, :], total_ref[1:2, :]
    for j in range(3):
        for i in range(3):
            wb[PAD * j : PAD * j + C, C * i : C * (i + 1)] = w_ref[3 * i + j]
        wb[PAD * j + C : PAD * (j + 1), :] = jnp.zeros((PAD - C, 3 * C), BF16)
    gain = gain_ref[...].reshape(1, C)
    edge = column(C)
    half = PIX // STEP
    for f in range(2):
        mean, scale = stat_ref[2 * f : 2 * f + 1, :], stat_ref[2 * f + 1 : 2 * f + 2, :]
        h_ref = (h0_ref, h1_ref)[f]

        def grad_body(step, carry, f=f, h_ref=h_ref):
            base = pl.multiple_of(step * STEP, STEP)
            grad = whole_grad(part_ref, h_ref, clip_ref, clip_sums, base, f)
            grads[pl.ds(base, STEP), :] = grad
            lows[pl.ds(base, STEP), :] = grad.astype(BF16)
            return carry

        lax.fori_loop(0, half, grad_body, 0)
        for i, tap in enumerate(row_taps(lows[...])):
            rows[:, i * C : (i + 1) * C] = tap
        z[...] = times_transposed(rows[...], wb[...])

        def step_body(step, carry, f=f, mean=mean, scale=scale):
            base = pl.multiple_of(step * STEP, STEP)
            here = pl.ds(base, STEP)
            right = jnp.where(edge == W - 1, 0.0, pltpu.roll(z[here, 0:C], STEP - 1, 0))
            left = jnp.where(edge == 0, 0.0, pltpu.roll(z[here, 2 * PAD : 2 * PAD + C], 1, 0))
            acts_grad = right + z[here, PAD : PAD + C] + left
            hat = (x_ref[pl.ds(base + f * PIX, STEP), :].astype(F32) - mean) * scale
            pre = hat * gain
            s = sigmoid(pre)
            dhat = acts_grad * (s * (1.0 + pre * (1.0 - s))) * gain
            dh[here, :] = dhat
            return carry[0] + fold(dhat), carry[1] + fold(dhat * hat)

        zero = jnp.zeros((8, C), F32)
        sums = lax.fori_loop(0, half, step_body, (zero, zero))
        grouped = group_sum(four(*sums)) * (1.0 / (PIX * C // GROUPS))
        first, second = grouped[0:1], grouped[1:2]

        def last_body(step, carry, f=f, mean=mean, scale=scale, first=first, second=second):
            base = pl.multiple_of(step * STEP, STEP)
            there = pl.ds(base + f * PIX, STEP)
            hat = (x_ref[there, :].astype(F32) - mean) * scale
            here = pl.ds(base, STEP)
            value = grads[here, :] + scale * (dh[here, :] - first - hat * second)
            out_ref[there, :] = value.astype(BF16)
            return carry

        lax.fori_loop(0, half, last_body, 0)


def input_gradient(part, h0, h1, clip_stat, total, x, stat, gain, weight):
    return call(
        input_grad_body,
        shape((ROWS, C), BF16),
        (
            pltpu.VMEM((3 * PAD, 3 * C), BF16),
            pltpu.VMEM((PIX, 3 * C), BF16),
            pltpu.VMEM((PIX, 3 * PAD), F32),
            pltpu.VMEM((PIX, C), F32),
            pltpu.VMEM((PIX, C), F32),
            pltpu.VMEM((PIX, C), BF16),
        ),
        flops=2_500_000_000,
        limit=16,
    )(part, h0, h1, clip_stat, total, x, stat, gain, weight)


def unpack_body(mine_ref, other_ref, spatial_ref, temporal_ref):
    core = lax.axis_index("c")
    for j in range(3):
        here = slice(j * C, (j + 1) * C)
        mine, other = mine_ref[here, :], other_ref[here, :]
        left = jnp.where(core == 0, mine, other)
        right = jnp.where(core == 0, other, mine)
        for i in range(4):
            lanes = slice(i * HALF, (i + 1) * HALF)
            if i < 3:
                spatial_ref[3 * i + j, :, 0:HALF] = left[:, lanes]
                spatial_ref[3 * i + j, :, HALF:C] = right[:, lanes]
            else:
                temporal_ref[j, :, 0:HALF] = left[:, lanes]
                temporal_ref[j, :, HALF:C] = right[:, lanes]


def unpack(mine, other):
    return call(unpack_body, (shape((9, C, C), BF16), shape((3, C, C), BF16)))(mine, other)


def neighbours(first, second):
    size = lax.axis_size(FRAME)
    before = lax.ppermute(second, FRAME, [(i, i + 1) for i in range(size - 1)])
    after = lax.ppermute(first, FRAME, [(i + 1, i) for i in range(size - 1)])
    return before, after


def swap_cores(value):
    return lax.ppermute(value, "c", [(0, 1), (1, 0)])


def everyone_total(value):
    plane = lax.axis_size(PLANE)
    value = value.reshape(plane, 1024 // plane, value.shape[1])
    return lax.all_to_all(value, PLANE, 0, 0)


def everyone_share(value):
    plane, line = lax.axis_size(PLANE), lax.axis_size(LINE)
    width = value.shape[2]
    value = jnp.sum(value.astype(F32), axis=0)
    value = value.reshape(line, 1024 // plane // line, width)
    value = jnp.sum(lax.all_to_all(value, LINE, 0, 0), axis=0).astype(BF16)
    value = jnp.broadcast_to(value[None], (line,) + value.shape)
    value = lax.all_to_all(value, LINE, 0, 0).reshape(1024 // plane, width)
    value = jnp.broadcast_to(value[None], (plane,) + value.shape)
    return lax.all_to_all(value, PLANE, 0, 0).reshape(1024, width)


def on_device(clips, cotangent, spatial_weight, temporal_weight, gain_one, gain_two):
    size = lax.axis_size(FRAME)
    count = float(size * ROWS * C // GROUPS)
    x = clips.reshape(ROWS, C)
    cot = cotangent.reshape(ROWS, C)
    spatial_weight = spatial_weight.reshape(9, C, C)
    barrier = lax.optimization_barrier
    cot_before, cot_after = neighbours(cot[:PIX], cot[PIX:])
    h0, h1, mine_turned, stat_one, sums = forward(x, spatial_weight, gain_one, size)
    edge0, edge1, cot_before, cot_after = barrier((h0, h1, cot_before, cot_after))
    before, after = neighbours(edge0, edge1)
    sums = lax.all_to_all(sums, FRAME, 0, 0)
    mixed_grad = mixed_gradient(cot_before, cot, cot_after, temporal_weight)
    sums, mine_turned, mixed_grad = barrier((sums, mine_turned, mixed_grad))
    other_turned = swap_cores(mine_turned)
    part, clip_stat, sums = slopes(
        sums, h0, h1, mixed_grad, cot, gain_two, count
    )
    sums = lax.all_to_all(sums, FRAME, 0, 0)
    mixed, temporal_keep, temporal_give = mixed_frames(
        before, h0, h1, after, cot, clip_stat, gain_two, sums
    )
    temporal_got = swap_cores(temporal_give)
    low_keep, low_give, total = hidden_gradient(sums, clip_stat, part, h0, h1, count)
    low_got = swap_cores(low_give)
    packed = weight_gradients(
        mine_turned, other_turned, low_keep, low_got, temporal_keep, temporal_got
    )
    packed, mixed, total = barrier((packed, mixed, total))
    output = temporal(mixed, h0, h1, temporal_weight)
    input_grad = input_gradient(
        part, h0, h1, clip_stat, total, x, stat_one, gain_one, spatial_weight
    )
    shares = everyone_total(packed)
    shares, output, input_grad = barrier((shares, output, input_grad))
    mine = everyone_share(shares)
    other = swap_cores(mine)
    spatial_grad, temporal_grad = unpack(mine, other)
    return (
        output.reshape(clips.shape),
        input_grad.reshape(clips.shape),
        spatial_grad.reshape(3, 3, C, C),
        temporal_grad,
    )


def solution(mesh):
    fine = Mesh(mesh.devices.reshape(2, 4, 2, 4, 4), ("zl", "x", "c", "y", "zh"))
    return jax.shard_map(
        on_device,
        mesh=fine,
        in_specs=(P(DP, FRAME), P(DP, FRAME), P(), P(), P(), P()),
        out_specs=(P(DP, FRAME), P(DP, FRAME), P(), P()),
        check_vma=False,
    )
```

```python
import functools

import jax
import jax.numpy as jnp
from jax import lax
from jax.experimental import pallas as pl
from jax.experimental.pallas import tpu as pltpu
from jax.sharding import Mesh, PartitionSpec as P

epsilon = 1e-05

GROUPS = 32
DP = ("zl", "x", "c")
FRAME = ("y", "zh")
PLANE = ("x", "y")
LINE = ("zl", "zh")

C = 320
W = 32
PAD = 384
HALF = C // 2
PIX = 512
ROWS = 2 * PIX
STEP = 128
F32 = jnp.float32
BF16 = jnp.bfloat16

MIB = 1024 * 1024


VMEM = pl.BlockSpec(memory_space=pltpu.VMEM)
FAR = pl.BlockSpec(memory_space=pltpu.HBM)


def call(body, out, scratch=(), flops=0, limit=12, ins=None, outs=None):
    specs = {}
    if ins is not None:
        specs = {"in_specs": ins, "out_specs": outs}
    return pl.pallas_call(
        body,
        out_shape=out,
        scratch_shapes=list(scratch),
        compiler_params=pltpu.CompilerParams(vmem_limit_bytes=limit * MIB),
        cost_estimate=pl.CostEstimate(flops=flops, transcendentals=0, bytes_accessed=8_000_000),
        **specs,
    )


def shape(dims, kind):
    return jax.ShapeDtypeStruct(dims, kind)


def far(dims, kind):
    return pltpu.HBM(dims, kind)


def at(step, size=STEP):
    return pl.ds(pl.multiple_of(step * size, size), size)


def group_sum(rows):
    per = C // GROUPS
    one = lax.broadcasted_iota(jnp.int32, (C, C), 0) * 6554 >> 16
    two = lax.broadcasted_iota(jnp.int32, (C, C), 1) * 6554 >> 16
    assert per == 10
    same = jnp.where(one == two, 1.0, 0.0).astype(F32)
    return jnp.dot(rows, same, precision=lax.Precision.HIGHEST, preferred_element_type=F32)


def fold(value):
    return jnp.sum(value.reshape(value.shape[0] // 8, 8, value.shape[1]), axis=0)


def column(width):
    return lax.broadcasted_iota(jnp.int32, (STEP, width), 0) & (W - 1)


def four(*sums):
    return jnp.concatenate([jnp.sum(s, axis=0, keepdims=True) for s in sums] + [jnp.zeros((8 - len(sums), C), F32)])


def sigmoid(value):
    return 1.0 / (1.0 + jnp.exp(-value))


def forward_body(
    x_ref, far_w_ref, gain_ref, h0_ref, h1_ref, far_turned_ref, stat_ref, sums_ref,
    w_ref, wf, x3, y, turned, w_sem, turned_sem,
):
    fetch = pltpu.make_async_copy(far_w_ref, w_ref, w_sem)
    fetch.start()
    zero = jnp.zeros((8, C), F32)

    def moments(step, carry):
        value = x_ref[at(step), :].astype(F32)
        return carry[0] + fold(value), carry[1] + fold(value * value)

    half = PIX // STEP
    s0, q0 = lax.fori_loop(0, half, moments, (zero, zero))
    s1, q1 = lax.fori_loop(half, 2 * half, moments, (zero, zero))
    grouped = group_sum(four(s0, q0, s1, q1)) * (1.0 / (PIX * C // GROUPS))
    stats = []
    for f in range(2):
        mean = grouped[2 * f : 2 * f + 1]
        var = grouped[2 * f + 1 : 2 * f + 2] - mean * mean
        stats += [mean, lax.rsqrt(var + epsilon)]
    stat_ref[...] = jnp.concatenate(stats + [jnp.zeros((4, C), F32)])
    gain = gain_ref[...].reshape(1, C)
    edge = column(C)

    def activate(step, mean, scale):
        value = x_ref[at(step), :].astype(F32)
        pre = (value - mean) * scale * gain
        act = pre / (1.0 + jnp.exp(-pre))
        low = act.astype(BF16)
        act = low.astype(F32)
        x3[at(step), 0:C] = jnp.where(edge == 0, 0.0, pltpu.roll(act, 1, 0)).astype(BF16)
        x3[at(step), C : 2 * C] = low
        x3[at(step), 2 * C : 3 * C] = jnp.where(
            edge == W - 1, 0.0, pltpu.roll(act, STEP - 1, 0)
        ).astype(BF16)

    total = (zero, zero)
    sends = []
    for f in range(2):
        mean, scale = stats[2 * f], stats[2 * f + 1]

        def act_step(step, carry, mean=mean, scale=scale):
            activate(step, mean, scale)
            return carry

        lax.fori_loop(f * half, (f + 1) * half, act_step, 0)
        if f == 0:
            fetch.wait()
            for i in range(3):
                for j in range(3):
                    wf[C * j : C * (j + 1), PAD * i : PAD * i + C] = w_ref[3 * i + j]
        y[f, 0:W, :] = jnp.zeros((W, 3 * PAD), F32)
        y[f, W + PIX : 2 * W + PIX, :] = jnp.zeros((W, 3 * PAD), F32)
        y[f, W : W + PIX, :] = jnp.dot(
            x3[f * PIX : (f + 1) * PIX, :], wf[...], preferred_element_type=F32
        )

        turn(x3[f * PIX : (f + 1) * PIX, C : 2 * C], turned.at[f])
        send = pltpu.make_async_copy(
            turned.at[f], far_turned_ref.at[:, f * PIX : (f + 1) * PIX], turned_sem.at[f]
        )
        send.start()
        sends.append(send)
        h_ref = (h0_ref, h1_ref)[f]

        def finish(step, carry, f=f, h_ref=h_ref):
            base = pl.multiple_of(step * STEP, STEP)
            conv = (
                y[f, pl.ds(base, STEP), 0:C]
                + y[f, pl.ds(base + W, STEP), PAD : PAD + C]
                + y[f, pl.ds(base + 2 * W, STEP), 2 * PAD : 2 * PAD + C]
            )
            value = x_ref[pl.ds(base + f * PIX, STEP), :].astype(F32)
            low = (value + conv).astype(BF16)
            h_ref[pl.ds(base, STEP), :] = low
            value = low.astype(F32)
            return carry[0] + fold(value), carry[1] + fold(value * value)

        total = lax.fori_loop(0, half, finish, total)
    spread(total, sums_ref)
    for send in sends:
        send.wait()


def spread(total, sums_ref):
    first = jnp.sum(total[0], axis=0, keepdims=True)
    second = jnp.sum(total[1], axis=0, keepdims=True)
    both = jnp.concatenate([first, second])
    for k in range(sums_ref.shape[0]):
        sums_ref[k] = both


def turn(acts, out_ref):
    rows = lax.broadcasted_iota(jnp.int32, (C, C), 0)
    same = jnp.where(rows == lax.broadcasted_iota(jnp.int32, (C, C), 1), 1.0, 0.0).astype(BF16)
    lane = lax.broadcasted_iota(jnp.int32, (C, STEP), 1) & (W - 1)
    moved = times_transposed(same, acts)
    for step in range(PIX // STEP):
        part = moved[:, step * STEP : (step + 1) * STEP]
        where = slice(step * STEP, (step + 1) * STEP)
        out_ref[0:C, where] = jnp.where(lane == 0, 0.0, pltpu.roll(part, 1, 1)).astype(BF16)
        out_ref[C : 2 * C, where] = part.astype(BF16)
        out_ref[2 * C : 3 * C, where] = jnp.where(
            lane == W - 1, 0.0, pltpu.roll(part, STEP - 1, 1)
        ).astype(BF16)


def forward(x, weight, gain, peers):
    return call(
        forward_body,
        (
            shape((PIX, C), BF16),
            shape((PIX, C), BF16),
            far((3 * C, ROWS), BF16),
            shape((8, C), F32),
            shape((peers, 2, C), F32),
        ),
        (
            pltpu.VMEM((9, C, C), BF16),
            pltpu.VMEM((3 * C, 3 * PAD), BF16),
            pltpu.VMEM((ROWS, 3 * C), BF16),
            pltpu.VMEM((2, PIX + 2 * W, 3 * PAD), F32),
            pltpu.VMEM((2, 3 * C, PIX), BF16),
            pltpu.SemaphoreType.DMA,
            pltpu.SemaphoreType.DMA((2,)),
        ),
        flops=2_500_000_000,
        limit=24,
        ins=[VMEM, FAR, VMEM],
        outs=(VMEM, VMEM, FAR, VMEM, VMEM),
    )(x, pltpu.with_memory_space_constraint(weight, pltpu.HBM), gain)


def times_transposed(a, b):
    return lax.dot_general(a, b, (((1,), (1,)), ((), ())), preferred_element_type=F32)


def clip_stats(sums_ref, count):
    total = jnp.sum(sums_ref[...], axis=0)
    grouped = group_sum(jnp.concatenate([total, jnp.zeros((6, C), F32)])) * (1.0 / count)
    return grouped[0:1], grouped[1:2]


def mixed_grad_body(before_ref, cot_ref, after_ref, w_ref, out_ref):
    for f in range(2):
        last = cot_ref[0:PIX, :] if f else before_ref[...]
        later = after_ref[...] if f else cot_ref[PIX:ROWS, :]
        total = times_transposed(later, w_ref[0])
        total = total + times_transposed(cot_ref[f * PIX : (f + 1) * PIX, :], w_ref[1])
        total = total + times_transposed(last, w_ref[2])
        out_ref[f * PIX : (f + 1) * PIX, :] = total.astype(BF16)


def mixed_gradient(before, cot, after, weight):
    return call(mixed_grad_body, far((ROWS, C), BF16), flops=1_500_000_000)(
        before, cot, after, weight
    )


def slope_body(
    count, sums_ref, h0_ref, h1_ref, grad_ref, cot_ref, gain_ref, part_ref, stat_ref, out_ref
):
    mean, square = clip_stats(sums_ref, count)
    scale = lax.rsqrt(square - mean * mean + epsilon)
    stat_ref[...] = jnp.concatenate([mean, scale, jnp.zeros((6, C), F32)])
    gain = gain_ref[...].reshape(1, C)
    zero = jnp.zeros((8, C), F32)
    total = (zero, zero)
    for f, h_ref in enumerate((h0_ref, h1_ref)):

        def step_body(step, carry, f=f, h_ref=h_ref):
            base = pl.multiple_of(step * STEP, STEP)
            there = pl.ds(base + f * PIX, STEP)
            hat = (h_ref[pl.ds(base, STEP), :].astype(F32) - mean) * scale
            pre = hat * gain
            s = sigmoid(pre)
            slope = s * (1.0 + pre * (1.0 - s))
            dhat = grad_ref[there, :].astype(F32) * slope * gain
            part_ref[there, :] = cot_ref[there, :].astype(F32) + scale * dhat
            return carry[0] + fold(dhat), carry[1] + fold(dhat * hat)

        total = lax.fori_loop(0, PIX // STEP, step_body, total)
    spread(total, out_ref)


def slopes(sums, h0, h1, grad, cot, gain, count):
    return call(
        functools.partial(slope_body, count),
        (shape((ROWS, C), F32), shape((8, C), F32), shape(sums.shape, F32)),
    )(sums, h0, h1, grad, cot, gain)


def mix(h_ref, base, mean, scale, gain):
    pre = (h_ref[pl.ds(base, STEP), :].astype(F32) - mean) * scale * gain
    return pre / (1.0 + jnp.exp(-pre))


def mixed_body(
    h0_ref, h1_ref, before_ref, cot_ref, after_ref, stat_ref, gain_ref, sums_ref,
    keep_ref, give_ref, turned,
):
    mean, scale = stat_ref[0:1, :], stat_ref[1:2, :]
    gain = gain_ref[...].reshape(1, C)
    for f, h_ref in enumerate((h0_ref, h1_ref)):
        for step in range(PIX // STEP):
            act = mix(h_ref, step * STEP, mean, scale, gain).astype(BF16)
            turned[:, f * PIX + step * STEP : f * PIX + (step + 1) * STEP] = act.T
    core = lax.axis_index("c")
    first, second = turned[:, 0:PIX], turned[:, PIX:ROWS]
    for k in range(3):
        if k == 1:
            part = jnp.dot(turned[...], cot_ref[...], preferred_element_type=F32)
        else:
            one = cot_ref[PIX:ROWS, :] if k == 0 else before_ref[...]
            two = after_ref[...] if k == 0 else cot_ref[0:PIX, :]
            part = jnp.dot(first, one, preferred_element_type=F32)
            part = part + jnp.dot(second, two, preferred_element_type=F32)
        left, right = part[:, 0:HALF], part[:, HALF:C]
        keep_ref[k * C : (k + 1) * C, 0:HALF] = jnp.where(core == 0, left, right)
        give_ref[k * C : (k + 1) * C, 0:HALF] = jnp.where(core == 0, right, left)


def temporal_gradient(h0, h1, before, cot, after, stat, gain, sums):
    return call(
        mixed_body,
        (shape((3 * C, 256), F32), shape((3 * C, 256), F32)),
        (pltpu.VMEM((C, ROWS), BF16),),
        flops=1_500_000_000,
    )(h0, h1, before, cot, after, stat, gain, sums)


def temporal_body(hb_ref, h0_ref, h1_ref, ha_ref, stat_ref, gain_ref, w_ref, out_ref, mx_ref):
    mean, scale = stat_ref[0:1, :], stat_ref[1:2, :]
    gain = gain_ref[...].reshape(1, C)
    place = lax.axis_index(FRAME)
    live = (place > 0, None, None, place < lax.axis_size(FRAME) - 1)
    for n, h_ref in enumerate((hb_ref, h0_ref, h1_ref, ha_ref)):

        def step_body(step, carry, n=n, h_ref=h_ref):
            base = pl.multiple_of(step * STEP, STEP)
            act = mix(h_ref, base, mean, scale, gain)
            if live[n] is not None:
                act = jnp.where(live[n], act, 0.0)
            mx_ref[pl.ds(base + n * PIX, STEP), :] = act.astype(BF16)
            return carry

        lax.fori_loop(0, PIX // STEP, step_body, 0)
    for f, h_ref in enumerate((h0_ref, h1_ref)):
        total = None
        for k in range(3):
            part = jnp.dot(
                mx_ref[(f + k) * PIX : (f + k + 1) * PIX, :],
                w_ref[k],
                preferred_element_type=F32,
            )
            total = part if total is None else total + part
        low = total.astype(BF16).astype(F32)
        out_ref[f * PIX : (f + 1) * PIX, :] = (h_ref[...].astype(F32) + low).astype(BF16)


def temporal(before, h0, h1, after, stat, gain, weight):
    return call(
        temporal_body,
        shape((ROWS, C), BF16),
        (pltpu.VMEM((4 * PIX, C), BF16),),
        flops=1_500_000_000,
    )(before, h0, h1, after, stat, gain, weight)


def whole_grad(part_ref, h_ref, stat_ref, sums, base, f):
    mean, scale = stat_ref[0:1, :], stat_ref[1:2, :]
    hat = (h_ref[pl.ds(base, STEP), :].astype(F32) - mean) * scale
    return part_ref[pl.ds(base + f * PIX, STEP), :] - scale * (sums[0] + hat * sums[1])


def hidden_grad_body(
    count, sums_ref, stat_ref, part_ref, h0_ref, h1_ref, keep_ref, give_ref, total_ref
):
    sums = clip_stats(sums_ref, count)
    total_ref[...] = jnp.concatenate([*sums, jnp.zeros((6, C), F32)])
    core = lax.axis_index("c")
    for f, h_ref in enumerate((h0_ref, h1_ref)):

        def step_body(step, carry, f=f, h_ref=h_ref):
            base = pl.multiple_of(step * STEP, STEP)
            here = pl.ds(base + f * PIX, STEP)
            grad = whole_grad(part_ref, h_ref, stat_ref, sums, base, f)
            left, right = grad[:, 0:HALF], grad[:, HALF:C]
            keep_ref[here, :] = jnp.where(core == 0, left, right).astype(BF16)
            give_ref[here, :] = jnp.where(core == 0, right, left).astype(BF16)
            return carry

        lax.fori_loop(0, PIX // STEP, step_body, 0)


def hidden_gradient(sums, stat, part, h0, h1, count):
    return call(
        functools.partial(hidden_grad_body, count),
        (shape((ROWS, HALF), BF16), shape((ROWS, HALF), BF16), shape((8, C), F32)),
    )(sums, stat, part, h0, h1)


def row_taps(value):
    none = jnp.zeros((W, value.shape[1]), value.dtype)
    return (
        jnp.concatenate([value[W:], none]),
        value,
        jnp.concatenate([none, value[: PIX - W]]),
    )


def weight_grad_body(
    mine_turned_ref, other_turned_ref, mine_ref, other_ref, keep_ref, got_ref, far_ref, rhs, out, sem
):
    for n, ref in enumerate((mine_ref, other_ref)):
        for f in range(2):
            where = slice(f * PIX, (f + 1) * PIX)
            for i, tap in enumerate(row_taps(ref[where, :])):
                rhs[n, where, i * HALF : (i + 1) * HALF] = tap
    sends = []
    for j in range(3):
        here = slice(j * C, (j + 1) * C)
        total = jnp.dot(mine_turned_ref[here, :], rhs[0], preferred_element_type=F32)
        total = total + jnp.dot(other_turned_ref[here, :], rhs[1], preferred_element_type=F32)
        out[here, 0 : 3 * HALF] = total.astype(BF16)
        kept = keep_ref[here, 0:HALF] + got_ref[here, 0:HALF]
        out[here, 3 * HALF : 4 * HALF] = kept.astype(BF16)
        if j == 2:
            out[3 * C :, :] = jnp.zeros((1024 - 3 * C, 4 * HALF), BF16)
            here = slice(j * C, 1024)
        send = pltpu.make_async_copy(out.at[here, :], far_ref.at[here, :], sem.at[j])
        send.start()
        sends.append(send)
    for send in sends:
        send.wait()


def weight_gradients(mine_turned, other_turned, mine, other, keep, got):
    return call(
        weight_grad_body,
        far((1024, 4 * HALF), BF16),
        (
            pltpu.VMEM((2, ROWS, 3 * HALF), BF16),
            pltpu.VMEM((1024, 4 * HALF), BF16),
            pltpu.SemaphoreType.DMA((3,)),
        ),
        flops=2_500_000_000,
        ins=[VMEM] * 6,
        outs=FAR,
    )(mine_turned, other_turned, mine, other, keep, got)


def input_grad_body(
    part_ref, h0_ref, h1_ref, clip_ref, total_ref, x_ref, stat_ref, gain_ref, w_ref,
    out_ref, wb, rows, z, dh, grads, lows,
):
    clip_sums = total_ref[0:1, :], total_ref[1:2, :]
    for j in range(3):
        for i in range(3):
            wb[PAD * j : PAD * j + C, C * i : C * (i + 1)] = w_ref[3 * i + j]
        wb[PAD * j + C : PAD * (j + 1), :] = jnp.zeros((PAD - C, 3 * C), BF16)
    gain = gain_ref[...].reshape(1, C)
    edge = column(C)
    half = PIX // STEP
    for f in range(2):
        mean, scale = stat_ref[2 * f : 2 * f + 1, :], stat_ref[2 * f + 1 : 2 * f + 2, :]
        h_ref = (h0_ref, h1_ref)[f]

        def grad_body(step, carry, f=f, h_ref=h_ref):
            base = pl.multiple_of(step * STEP, STEP)
            grad = whole_grad(part_ref, h_ref, clip_ref, clip_sums, base, f)
            grads[pl.ds(base, STEP), :] = grad
            lows[pl.ds(base, STEP), :] = grad.astype(BF16)
            return carry

        lax.fori_loop(0, half, grad_body, 0)
        for i, tap in enumerate(row_taps(lows[...])):
            rows[:, i * C : (i + 1) * C] = tap
        z[...] = times_transposed(rows[...], wb[...])

        def step_body(step, carry, f=f, mean=mean, scale=scale):
            base = pl.multiple_of(step * STEP, STEP)
            here = pl.ds(base, STEP)
            right = jnp.where(edge == W - 1, 0.0, pltpu.roll(z[here, 0:C], STEP - 1, 0))
            left = jnp.where(edge == 0, 0.0, pltpu.roll(z[here, 2 * PAD : 2 * PAD + C], 1, 0))
            acts_grad = right + z[here, PAD : PAD + C] + left
            hat = (x_ref[pl.ds(base + f * PIX, STEP), :].astype(F32) - mean) * scale
            pre = hat * gain
            s = sigmoid(pre)
            dhat = acts_grad * (s * (1.0 + pre * (1.0 - s))) * gain
            dh[here, :] = dhat
            return carry[0] + fold(dhat), carry[1] + fold(dhat * hat)

        zero = jnp.zeros((8, C), F32)
        sums = lax.fori_loop(0, half, step_body, (zero, zero))
        grouped = group_sum(four(*sums)) * (1.0 / (PIX * C // GROUPS))
        first, second = grouped[0:1], grouped[1:2]

        def last_body(step, carry, f=f, mean=mean, scale=scale, first=first, second=second):
            base = pl.multiple_of(step * STEP, STEP)
            there = pl.ds(base + f * PIX, STEP)
            hat = (x_ref[there, :].astype(F32) - mean) * scale
            here = pl.ds(base, STEP)
            value = grads[here, :] + scale * (dh[here, :] - first - hat * second)
            out_ref[there, :] = value.astype(BF16)
            return carry

        lax.fori_loop(0, half, last_body, 0)


def input_gradient(part, h0, h1, clip_stat, total, x, stat, gain, weight):
    return call(
        input_grad_body,
        shape((ROWS, C), BF16),
        (
            pltpu.VMEM((3 * PAD, 3 * C), BF16),
            pltpu.VMEM((PIX, 3 * C), BF16),
            pltpu.VMEM((PIX, 3 * PAD), F32),
            pltpu.VMEM((PIX, C), F32),
            pltpu.VMEM((PIX, C), F32),
            pltpu.VMEM((PIX, C), BF16),
        ),
        flops=2_500_000_000,
        limit=16,
    )(part, h0, h1, clip_stat, total, x, stat, gain, weight)


def unpack_body(mine_ref, other_ref, spatial_ref, temporal_ref):
    core = lax.axis_index("c")
    for j in range(3):
        here = slice(j * C, (j + 1) * C)
        mine, other = mine_ref[here, :], other_ref[here, :]
        left = jnp.where(core == 0, mine, other)
        right = jnp.where(core == 0, other, mine)
        for i in range(4):
            lanes = slice(i * HALF, (i + 1) * HALF)
            if i < 3:
                spatial_ref[3 * i + j, :, 0:HALF] = left[:, lanes]
                spatial_ref[3 * i + j, :, HALF:C] = right[:, lanes]
            else:
                temporal_ref[j, :, 0:HALF] = left[:, lanes]
                temporal_ref[j, :, HALF:C] = right[:, lanes]


def unpack(mine, other):
    return call(unpack_body, (shape((9, C, C), BF16), shape((3, C, C), BF16)))(mine, other)


def neighbours(first, second):
    size = lax.axis_size(FRAME)
    before = lax.ppermute(second, FRAME, [(i, i + 1) for i in range(size - 1)])
    after = lax.ppermute(first, FRAME, [(i + 1, i) for i in range(size - 1)])
    return before, after


def swap_cores(value):
    return lax.ppermute(value, "c", [(0, 1), (1, 0)])


def everyone_total(value):
    plane = lax.axis_size(PLANE)
    value = value.reshape(plane, 1024 // plane, value.shape[1])
    return lax.all_to_all(value, PLANE, 0, 0)


def everyone_share(value):
    plane, line = lax.axis_size(PLANE), lax.axis_size(LINE)
    width = value.shape[2]
    value = jnp.sum(value.astype(F32), axis=0)
    value = value.reshape(line, 1024 // plane // line, width)
    value = jnp.sum(lax.all_to_all(value, LINE, 0, 0), axis=0).astype(BF16)
    value = jnp.broadcast_to(value[None], (line,) + value.shape)
    return lax.all_to_all(value, LINE, 0, 0).reshape(1024 // plane, width)


def everyone_gets(value):
    plane = lax.axis_size(PLANE)
    value = jnp.broadcast_to(value[None], (plane,) + value.shape)
    return lax.all_to_all(value, PLANE, 0, 0).reshape(1024, value.shape[2])


def on_device(clips, cotangent, spatial_weight, temporal_weight, gain_one, gain_two):
    size = lax.axis_size(FRAME)
    count = float(size * ROWS * C // GROUPS)
    x = clips.reshape(ROWS, C)
    cot = cotangent.reshape(ROWS, C)
    spatial_weight = spatial_weight.reshape(9, C, C)
    barrier = lax.optimization_barrier
    cot_before, cot_after = neighbours(cot[:PIX], cot[PIX:])
    h0, h1, mine_turned, stat_one, sums = forward(x, spatial_weight, gain_one, size)
    sums = lax.all_to_all(sums, FRAME, 0, 0)
    mixed_grad = mixed_gradient(cot_before, cot, cot_after, temporal_weight)
    sums, mine_turned, mixed_grad = barrier((sums, mine_turned, mixed_grad))
    other_turned = swap_cores(mine_turned)
    part, clip_stat, sums = slopes(sums, h0, h1, mixed_grad, cot, gain_two, count)
    sums = lax.all_to_all(sums, FRAME, 0, 0)
    temporal_keep, temporal_give = temporal_gradient(
        h0, h1, cot_before, cot, cot_after, clip_stat, gain_two, sums
    )
    temporal_got = swap_cores(temporal_give)
    low_keep, low_give, total = hidden_gradient(sums, clip_stat, part, h0, h1, count)
    low_got = swap_cores(low_give)
    packed = weight_gradients(
        mine_turned, other_turned, low_keep, low_got, temporal_keep, temporal_got
    )
    packed, total, edge0, edge1 = barrier((packed, total, h0, h1))
    shares = everyone_total(packed)
    before, after = neighbours(edge0, edge1)
    input_grad = input_gradient(
        part, h0, h1, clip_stat, total, x, stat_one, gain_one, spatial_weight
    )
    shares, input_grad, before, after = barrier((shares, input_grad, before, after))
    mine = everyone_share(shares)
    mine, before, after = barrier((mine, before, after))
    output = temporal(before, h0, h1, after, clip_stat, gain_two, temporal_weight)
    mine, output = barrier((everyone_gets(mine), output))
    other = swap_cores(mine)
    spatial_grad, temporal_grad = unpack(mine, other)
    return (
        output.reshape(clips.shape),
        input_grad.reshape(clips.shape),
        spatial_grad.reshape(3, 3, C, C),
        temporal_grad,
    )


def solution(mesh):
    fine = Mesh(mesh.devices.reshape(2, 4, 2, 4, 4), ("zl", "x", "c", "y", "zh"))
    return jax.shard_map(
        on_device,
        mesh=fine,
        in_specs=(P(DP, FRAME), P(DP, FRAME), P(), P(), P(), P()),
        out_specs=(P(DP, FRAME), P(DP, FRAME), P(), P()),
        check_vma=False,
    )
```

```python
import functools

import jax
import jax.numpy as jnp
from jax import lax
from jax.experimental import pallas as pl
from jax.experimental.pallas import tpu as pltpu
from jax.sharding import Mesh, PartitionSpec as P

epsilon = 1e-05

GROUPS = 32
DP = ("zl", "x", "c")
FRAME = ("y", "zh")
PLANE = ("x", "y")
LINE = ("zl", "zh")

C = 320
W = 32
PAD = 384
HALF = C // 2
PIX = 512
ROWS = 2 * PIX
STEP = 128
F32 = jnp.float32
BF16 = jnp.bfloat16

MIB = 1024 * 1024


VMEM = pl.BlockSpec(memory_space=pltpu.VMEM)
FAR = pl.BlockSpec(memory_space=pltpu.HBM)


def call(body, out, scratch=(), flops=0, limit=12, ins=None, outs=None):
    specs = {}
    if ins is not None:
        specs = {"in_specs": ins, "out_specs": outs}
    return pl.pallas_call(
        body,
        out_shape=out,
        scratch_shapes=list(scratch),
        compiler_params=pltpu.CompilerParams(vmem_limit_bytes=limit * MIB),
        cost_estimate=pl.CostEstimate(flops=flops, transcendentals=0, bytes_accessed=8_000_000),
        **specs,
    )


def shape(dims, kind):
    return jax.ShapeDtypeStruct(dims, kind)


def far(dims, kind):
    return pltpu.HBM(dims, kind)


def in_hbm(value):
    return pltpu.with_memory_space_constraint(value, pltpu.HBM)


def at(step, size=STEP):
    return pl.ds(pl.multiple_of(step * size, size), size)


def group_sum(rows):
    per = C // GROUPS
    one = lax.broadcasted_iota(jnp.int32, (C, C), 0) * 6554 >> 16
    two = lax.broadcasted_iota(jnp.int32, (C, C), 1) * 6554 >> 16
    assert per == 10
    same = jnp.where(one == two, 1.0, 0.0).astype(F32)
    return jnp.dot(rows, same, precision=lax.Precision.HIGHEST, preferred_element_type=F32)


def fold(value):
    return jnp.sum(value.reshape(value.shape[0] // 8, 8, value.shape[1]), axis=0)


def column(width):
    return lax.broadcasted_iota(jnp.int32, (STEP, width), 0) & (W - 1)


def four(*sums):
    return jnp.concatenate([jnp.sum(s, axis=0, keepdims=True) for s in sums] + [jnp.zeros((8 - len(sums), C), F32)])


def sigmoid(value):
    return 1.0 / (1.0 + jnp.exp(-value))


def forward_body(
    x_ref, far_w_ref, gain_ref, h0_ref, h1_ref, far_turned_ref, far_stat_ref, sums_ref,
    w_ref, wf, x3, y, turned, stat_ref, w_sem, turned_sem, stat_sem,
):
    fetch = pltpu.make_async_copy(far_w_ref, w_ref, w_sem)
    fetch.start()
    zero = jnp.zeros((8, C), F32)

    def moments(step, carry):
        value = x_ref[at(step), :].astype(F32)
        return carry[0] + fold(value), carry[1] + fold(value * value)

    half = PIX // STEP
    s0, q0 = lax.fori_loop(0, half, moments, (zero, zero))
    s1, q1 = lax.fori_loop(half, 2 * half, moments, (zero, zero))
    grouped = group_sum(four(s0, q0, s1, q1)) * (1.0 / (PIX * C // GROUPS))
    stats = []
    for f in range(2):
        mean = grouped[2 * f : 2 * f + 1]
        var = grouped[2 * f + 1 : 2 * f + 2] - mean * mean
        stats += [mean, lax.rsqrt(var + epsilon)]
    gain = gain_ref[...].reshape(1, C)
    stat_ref[...] = jnp.concatenate([*stats, gain, jnp.zeros((3, C), F32)])
    sends = [pltpu.make_async_copy(stat_ref, far_stat_ref, stat_sem)]
    sends[0].start()
    edge = column(C)

    def activate(step, mean, scale):
        value = x_ref[at(step), :].astype(F32)
        pre = (value - mean) * scale * gain
        act = pre / (1.0 + jnp.exp(-pre))
        low = act.astype(BF16)
        act = low.astype(F32)
        x3[at(step), 0:C] = jnp.where(edge == 0, 0.0, pltpu.roll(act, 1, 0)).astype(BF16)
        x3[at(step), C : 2 * C] = low
        x3[at(step), 2 * C : 3 * C] = jnp.where(
            edge == W - 1, 0.0, pltpu.roll(act, STEP - 1, 0)
        ).astype(BF16)

    total = (zero, zero)
    for f in range(2):
        mean, scale = stats[2 * f], stats[2 * f + 1]

        def act_step(step, carry, mean=mean, scale=scale):
            activate(step, mean, scale)
            return carry

        lax.fori_loop(f * half, (f + 1) * half, act_step, 0)
        if f == 0:
            fetch.wait()
            for i in range(3):
                for j in range(3):
                    wf[C * j : C * (j + 1), PAD * i : PAD * i + C] = w_ref[3 * i + j]
        y[f, 0:W, :] = jnp.zeros((W, 3 * PAD), F32)
        y[f, W + PIX : 2 * W + PIX, :] = jnp.zeros((W, 3 * PAD), F32)
        y[f, W : W + PIX, :] = jnp.dot(
            x3[f * PIX : (f + 1) * PIX, :], wf[...], preferred_element_type=F32
        )

        turn(x3[f * PIX : (f + 1) * PIX, C : 2 * C], turned.at[f])
        send = pltpu.make_async_copy(
            turned.at[f], far_turned_ref.at[:, f * PIX : (f + 1) * PIX], turned_sem.at[f]
        )
        send.start()
        sends.append(send)
        h_ref = (h0_ref, h1_ref)[f]

        def finish(step, carry, f=f, h_ref=h_ref):
            base = pl.multiple_of(step * STEP, STEP)
            conv = (
                y[f, pl.ds(base, STEP), 0:C]
                + y[f, pl.ds(base + W, STEP), PAD : PAD + C]
                + y[f, pl.ds(base + 2 * W, STEP), 2 * PAD : 2 * PAD + C]
            )
            value = x_ref[pl.ds(base + f * PIX, STEP), :].astype(F32)
            low = (value + conv).astype(BF16)
            h_ref[pl.ds(base, STEP), :] = low
            value = low.astype(F32)
            return carry[0] + fold(value), carry[1] + fold(value * value)

        total = lax.fori_loop(0, half, finish, total)
    spread(total, sums_ref)
    for send in sends:
        send.wait()


def spread(total, sums_ref):
    first = jnp.sum(total[0], axis=0, keepdims=True)
    second = jnp.sum(total[1], axis=0, keepdims=True)
    both = jnp.concatenate([first, second])
    for k in range(sums_ref.shape[0]):
        sums_ref[k] = both


def turn(acts, out_ref):
    rows = lax.broadcasted_iota(jnp.int32, (C, C), 0)
    same = jnp.where(rows == lax.broadcasted_iota(jnp.int32, (C, C), 1), 1.0, 0.0).astype(BF16)
    lane = lax.broadcasted_iota(jnp.int32, (C, STEP), 1) & (W - 1)
    moved = times_transposed(same, acts)
    for step in range(PIX // STEP):
        part = moved[:, step * STEP : (step + 1) * STEP]
        where = slice(step * STEP, (step + 1) * STEP)
        out_ref[0:C, where] = jnp.where(lane == 0, 0.0, pltpu.roll(part, 1, 1)).astype(BF16)
        out_ref[C : 2 * C, where] = part.astype(BF16)
        out_ref[2 * C : 3 * C, where] = jnp.where(
            lane == W - 1, 0.0, pltpu.roll(part, STEP - 1, 1)
        ).astype(BF16)


def forward(x, weight, gain, peers):
    return call(
        forward_body,
        (
            shape((PIX, C), BF16),
            shape((PIX, C), BF16),
            far((3 * C, ROWS), BF16),
            far((8, C), F32),
            shape((peers, 2, C), F32),
        ),
        (
            pltpu.VMEM((9, C, C), BF16),
            pltpu.VMEM((3 * C, 3 * PAD), BF16),
            pltpu.VMEM((ROWS, 3 * C), BF16),
            pltpu.VMEM((2, PIX + 2 * W, 3 * PAD), F32),
            pltpu.VMEM((2, 3 * C, PIX), BF16),
            pltpu.VMEM((8, C), F32),
            pltpu.SemaphoreType.DMA,
            pltpu.SemaphoreType.DMA((2,)),
            pltpu.SemaphoreType.DMA,
        ),
        flops=2_500_000_000,
        limit=24,
        ins=[VMEM, FAR, VMEM],
        outs=(VMEM, VMEM, FAR, FAR, VMEM),
    )(x, in_hbm(weight), gain)


def times_transposed(a, b):
    return lax.dot_general(a, b, (((1,), (1,)), ((), ())), preferred_element_type=F32)


def clip_stats(sums_ref, count):
    total = jnp.sum(sums_ref[...], axis=0)
    grouped = group_sum(jnp.concatenate([total, jnp.zeros((6, C), F32)])) * (1.0 / count)
    return grouped[0:1], grouped[1:2]


def mixed_grad_body(before_ref, cot_ref, after_ref, w_ref, out_ref):
    for f in range(2):
        last = cot_ref[0:PIX, :] if f else before_ref[...]
        later = after_ref[...] if f else cot_ref[PIX:ROWS, :]
        total = times_transposed(later, w_ref[0])
        total = total + times_transposed(cot_ref[f * PIX : (f + 1) * PIX, :], w_ref[1])
        total = total + times_transposed(last, w_ref[2])
        out_ref[f * PIX : (f + 1) * PIX, :] = total.astype(BF16)


def mixed_gradient(before, cot, after, weight):
    return call(mixed_grad_body, far((ROWS, C), BF16), flops=1_500_000_000)(
        before, cot, after, weight
    )


def slope_body(
    count, sums_ref, h0_ref, h1_ref, far_grad_ref, cot_ref, gain_ref,
    part_ref, stat_ref, out_ref, far_stat_ref, grad_ref, sem, grad_sem,
):
    fetch = pltpu.make_async_copy(far_grad_ref, grad_ref, grad_sem)
    fetch.start()
    mean, square = clip_stats(sums_ref, count)
    scale = lax.rsqrt(square - mean * mean + epsilon)
    gain = gain_ref[...].reshape(1, C)
    stat_ref[...] = jnp.concatenate([mean, scale, gain, jnp.zeros((5, C), F32)])
    send = pltpu.make_async_copy(stat_ref, far_stat_ref, sem)
    send.start()
    fetch.wait()
    zero = jnp.zeros((8, C), F32)
    total = (zero, zero)
    for f, h_ref in enumerate((h0_ref, h1_ref)):

        def step_body(step, carry, f=f, h_ref=h_ref):
            base = pl.multiple_of(step * STEP, STEP)
            there = pl.ds(base + f * PIX, STEP)
            hat = (h_ref[pl.ds(base, STEP), :].astype(F32) - mean) * scale
            pre = hat * gain
            s = sigmoid(pre)
            slope = s * (1.0 + pre * (1.0 - s))
            dhat = grad_ref[there, :].astype(F32) * slope * gain
            part_ref[there, :] = cot_ref[there, :].astype(F32) + scale * dhat
            return carry[0] + fold(dhat), carry[1] + fold(dhat * hat)

        total = lax.fori_loop(0, PIX // STEP, step_body, total)
    spread(total, out_ref)
    send.wait()


def slopes(sums, h0, h1, grad, cot, gain, count):
    return call(
        functools.partial(slope_body, count),
        (shape((ROWS, C), F32), shape((8, C), F32), shape(sums.shape, F32), far((8, C), F32)),
        (pltpu.VMEM((ROWS, C), BF16), pltpu.SemaphoreType.DMA, pltpu.SemaphoreType.DMA),
        ins=[VMEM] * 3 + [FAR] + [VMEM] * 2,
        outs=(VMEM, VMEM, VMEM, FAR),
    )(sums, h0, h1, in_hbm(grad), cot, gain)


def mix(h_ref, base, mean, scale, gain):
    pre = (h_ref[pl.ds(base, STEP), :].astype(F32) - mean) * scale * gain
    return pre / (1.0 + jnp.exp(-pre))


def mixed_body(
    h0_ref, h1_ref, before_ref, cot_ref, after_ref, stat_ref, sums_ref,
    keep_ref, give_ref, turned,
):
    mean, scale, gain = stat_ref[0:1, :], stat_ref[1:2, :], stat_ref[2:3, :]
    for f, h_ref in enumerate((h0_ref, h1_ref)):
        for step in range(PIX // STEP):
            act = mix(h_ref, step * STEP, mean, scale, gain).astype(BF16)
            turned[:, f * PIX + step * STEP : f * PIX + (step + 1) * STEP] = act.T
    core = lax.axis_index("c")
    first, second = turned[:, 0:PIX], turned[:, PIX:ROWS]
    for k in range(3):
        if k == 1:
            part = jnp.dot(turned[...], cot_ref[...], preferred_element_type=F32)
        else:
            one = cot_ref[PIX:ROWS, :] if k == 0 else before_ref[...]
            two = after_ref[...] if k == 0 else cot_ref[0:PIX, :]
            part = jnp.dot(first, one, preferred_element_type=F32)
            part = part + jnp.dot(second, two, preferred_element_type=F32)
        left, right = part[:, 0:HALF], part[:, HALF:C]
        keep_ref[k * C : (k + 1) * C, 0:HALF] = jnp.where(core == 0, left, right)
        give_ref[k * C : (k + 1) * C, 0:HALF] = jnp.where(core == 0, right, left)


def temporal_gradient(h0, h1, before, cot, after, stat, sums):
    return call(
        mixed_body,
        (shape((3 * C, 256), F32), shape((3 * C, 256), F32)),
        (pltpu.VMEM((C, ROWS), BF16),),
        flops=1_500_000_000,
    )(h0, h1, before, cot, after, stat, sums)


def temporal_body(
    hb_ref, h0_ref, h1_ref, ha_ref, far_stat_ref, w_ref, out_ref, mx_ref, stat_ref, sem
):
    fetch = pltpu.make_async_copy(far_stat_ref, stat_ref, sem)
    fetch.start()
    fetch.wait()
    mean, scale, gain = stat_ref[0:1, :], stat_ref[1:2, :], stat_ref[2:3, :]
    place = lax.axis_index(FRAME)
    live = (place > 0, None, None, place < lax.axis_size(FRAME) - 1)
    for n, h_ref in enumerate((hb_ref, h0_ref, h1_ref, ha_ref)):

        def step_body(step, carry, n=n, h_ref=h_ref):
            base = pl.multiple_of(step * STEP, STEP)
            act = mix(h_ref, base, mean, scale, gain)
            if live[n] is not None:
                act = jnp.where(live[n], act, 0.0)
            mx_ref[pl.ds(base + n * PIX, STEP), :] = act.astype(BF16)
            return carry

        lax.fori_loop(0, PIX // STEP, step_body, 0)
    for f, h_ref in enumerate((h0_ref, h1_ref)):
        total = None
        for k in range(3):
            part = jnp.dot(
                mx_ref[(f + k) * PIX : (f + k + 1) * PIX, :],
                w_ref[k],
                preferred_element_type=F32,
            )
            total = part if total is None else total + part
        low = total.astype(BF16).astype(F32)
        out_ref[f * PIX : (f + 1) * PIX, :] = (h_ref[...].astype(F32) + low).astype(BF16)


def temporal(before, h0, h1, after, stat, weight):
    return call(
        temporal_body,
        shape((ROWS, C), BF16),
        (pltpu.VMEM((4 * PIX, C), BF16), pltpu.VMEM((8, C), F32), pltpu.SemaphoreType.DMA),
        flops=1_500_000_000,
        ins=[VMEM] * 4 + [FAR, VMEM],
        outs=VMEM,
    )(before, h0, h1, after, in_hbm(stat), weight)


def whole_grad(part_ref, h_ref, stat_ref, sums, base, f):
    mean, scale = stat_ref[0:1, :], stat_ref[1:2, :]
    hat = (h_ref[pl.ds(base, STEP), :].astype(F32) - mean) * scale
    return part_ref[pl.ds(base + f * PIX, STEP), :] - scale * (sums[0] + hat * sums[1])


def hidden_grad_body(
    count, sums_ref, stat_ref, part_ref, h0_ref, h1_ref,
    keep_ref, give_ref, far_total_ref, total_ref, sem,
):
    sums = clip_stats(sums_ref, count)
    total_ref[...] = jnp.concatenate([*sums, jnp.zeros((6, C), F32)])
    send = pltpu.make_async_copy(total_ref, far_total_ref, sem)
    send.start()
    core = lax.axis_index("c")
    for f, h_ref in enumerate((h0_ref, h1_ref)):

        def step_body(step, carry, f=f, h_ref=h_ref):
            base = pl.multiple_of(step * STEP, STEP)
            here = pl.ds(base + f * PIX, STEP)
            grad = whole_grad(part_ref, h_ref, stat_ref, sums, base, f)
            left, right = grad[:, 0:HALF], grad[:, HALF:C]
            keep_ref[here, :] = jnp.where(core == 0, left, right).astype(BF16)
            give_ref[here, :] = jnp.where(core == 0, right, left).astype(BF16)
            return carry

        lax.fori_loop(0, PIX // STEP, step_body, 0)
    send.wait()


def hidden_gradient(sums, stat, part, h0, h1, count):
    return call(
        functools.partial(hidden_grad_body, count),
        (shape((ROWS, HALF), BF16), shape((ROWS, HALF), BF16), far((8, C), F32)),
        (pltpu.VMEM((8, C), F32), pltpu.SemaphoreType.DMA),
        ins=[VMEM] * 5,
        outs=(VMEM, VMEM, FAR),
    )(sums, stat, part, h0, h1)


def row_taps(value):
    none = jnp.zeros((W, value.shape[1]), value.dtype)
    return (
        jnp.concatenate([value[W:], none]),
        value,
        jnp.concatenate([none, value[: PIX - W]]),
    )


def weight_grad_body(
    mine_turned_ref, other_turned_ref, mine_ref, other_ref, keep_ref, got_ref, far_ref, rhs, out, sem
):
    for n, ref in enumerate((mine_ref, other_ref)):
        for f in range(2):
            where = slice(f * PIX, (f + 1) * PIX)
            for i, tap in enumerate(row_taps(ref[where, :])):
                rhs[n, where, i * HALF : (i + 1) * HALF] = tap
    sends = []
    for j in range(3):
        here = slice(j * C, (j + 1) * C)
        total = jnp.dot(mine_turned_ref[here, :], rhs[0], preferred_element_type=F32)
        total = total + jnp.dot(other_turned_ref[here, :], rhs[1], preferred_element_type=F32)
        out[here, 0 : 3 * HALF] = total.astype(BF16)
        kept = keep_ref[here, 0:HALF] + got_ref[here, 0:HALF]
        out[here, 3 * HALF : 4 * HALF] = kept.astype(BF16)
        if j == 2:
            out[3 * C :, :] = jnp.zeros((1024 - 3 * C, 4 * HALF), BF16)
            here = slice(j * C, 1024)
        send = pltpu.make_async_copy(out.at[here, :], far_ref.at[here, :], sem.at[j])
        send.start()
        sends.append(send)
    for send in sends:
        send.wait()


def weight_gradients(mine_turned, other_turned, mine, other, keep, got):
    return call(
        weight_grad_body,
        far((1024, 4 * HALF), BF16),
        (
            pltpu.VMEM((2, ROWS, 3 * HALF), BF16),
            pltpu.VMEM((1024, 4 * HALF), BF16),
            pltpu.SemaphoreType.DMA((3,)),
        ),
        flops=2_500_000_000,
        ins=[VMEM] * 6,
        outs=FAR,
    )(mine_turned, other_turned, mine, other, keep, got)


def input_grad_body(
    part_ref, h0_ref, h1_ref, far_clip_ref, far_total_ref, x_ref, far_stat_ref, far_w_ref,
    out_ref, wb, rows, z, dh, grads, lows, clip_ref, total_ref, stat_ref, w_ref, sem,
):
    pairs = (far_clip_ref, clip_ref), (far_total_ref, total_ref), (far_stat_ref, stat_ref)
    fetches = [
        pltpu.make_async_copy(one, two, sem.at[n])
        for n, (one, two) in enumerate((*pairs, (far_w_ref, w_ref)))
    ]
    for fetch in fetches:
        fetch.start()
    for fetch in fetches[:3]:
        fetch.wait()
    clip_sums = total_ref[0:1, :], total_ref[1:2, :]
    gain = stat_ref[4:5, :]
    edge = column(C)
    half = PIX // STEP
    for f in range(2):
        mean, scale = stat_ref[2 * f : 2 * f + 1, :], stat_ref[2 * f + 1 : 2 * f + 2, :]
        h_ref = (h0_ref, h1_ref)[f]

        def grad_body(step, carry, f=f, h_ref=h_ref):
            base = pl.multiple_of(step * STEP, STEP)
            grad = whole_grad(part_ref, h_ref, clip_ref, clip_sums, base, f)
            grads[pl.ds(base, STEP), :] = grad
            lows[pl.ds(base, STEP), :] = grad.astype(BF16)
            return carry

        lax.fori_loop(0, half, grad_body, 0)
        if f == 0:
            fetches[3].wait()
            for j in range(3):
                for i in range(3):
                    wb[PAD * j : PAD * j + C, C * i : C * (i + 1)] = w_ref[3 * i + j]
                wb[PAD * j + C : PAD * (j + 1), :] = jnp.zeros((PAD - C, 3 * C), BF16)
        for i, tap in enumerate(row_taps(lows[...])):
            rows[:, i * C : (i + 1) * C] = tap
        z[...] = times_transposed(rows[...], wb[...])

        def step_body(step, carry, f=f, mean=mean, scale=scale):
            base = pl.multiple_of(step * STEP, STEP)
            here = pl.ds(base, STEP)
            right = jnp.where(edge == W - 1, 0.0, pltpu.roll(z[here, 0:C], STEP - 1, 0))
            left = jnp.where(edge == 0, 0.0, pltpu.roll(z[here, 2 * PAD : 2 * PAD + C], 1, 0))
            acts_grad = right + z[here, PAD : PAD + C] + left
            hat = (x_ref[pl.ds(base + f * PIX, STEP), :].astype(F32) - mean) * scale
            pre = hat * gain
            s = sigmoid(pre)
            dhat = acts_grad * (s * (1.0 + pre * (1.0 - s))) * gain
            dh[here, :] = dhat
            return carry[0] + fold(dhat), carry[1] + fold(dhat * hat)

        zero = jnp.zeros((8, C), F32)
        sums = lax.fori_loop(0, half, step_body, (zero, zero))
        grouped = group_sum(four(*sums)) * (1.0 / (PIX * C // GROUPS))
        first, second = grouped[0:1], grouped[1:2]

        def last_body(step, carry, f=f, mean=mean, scale=scale, first=first, second=second):
            base = pl.multiple_of(step * STEP, STEP)
            there = pl.ds(base + f * PIX, STEP)
            hat = (x_ref[there, :].astype(F32) - mean) * scale
            here = pl.ds(base, STEP)
            value = grads[here, :] + scale * (dh[here, :] - first - hat * second)
            out_ref[there, :] = value.astype(BF16)
            return carry

        lax.fori_loop(0, half, last_body, 0)


def input_gradient(part, h0, h1, clip_stat, total, x, stat, weight):
    return call(
        input_grad_body,
        shape((ROWS, C), BF16),
        (
            pltpu.VMEM((3 * PAD, 3 * C), BF16),
            pltpu.VMEM((PIX, 3 * C), BF16),
            pltpu.VMEM((PIX, 3 * PAD), F32),
            pltpu.VMEM((PIX, C), F32),
            pltpu.VMEM((PIX, C), F32),
            pltpu.VMEM((PIX, C), BF16),
            pltpu.VMEM((8, C), F32),
            pltpu.VMEM((8, C), F32),
            pltpu.VMEM((8, C), F32),
            pltpu.VMEM((9, C, C), BF16),
            pltpu.SemaphoreType.DMA((4,)),
        ),
        flops=2_500_000_000,
        limit=18,
        ins=[VMEM] * 3 + [FAR] * 2 + [VMEM] + [FAR] * 2,
        outs=VMEM,
    )(part, h0, h1, in_hbm(clip_stat), in_hbm(total), x, in_hbm(stat), in_hbm(weight))


def unpack_body(mine_ref, other_ref, spatial_ref, temporal_ref):
    core = lax.axis_index("c")
    for j in range(3):
        here = slice(j * C, (j + 1) * C)
        mine, other = mine_ref[here, :], other_ref[here, :]
        left = jnp.where(core == 0, mine, other)
        right = jnp.where(core == 0, other, mine)
        for i in range(4):
            lanes = slice(i * HALF, (i + 1) * HALF)
            if i < 3:
                spatial_ref[3 * i + j, :, 0:HALF] = left[:, lanes]
                spatial_ref[3 * i + j, :, HALF:C] = right[:, lanes]
            else:
                temporal_ref[j, :, 0:HALF] = left[:, lanes]
                temporal_ref[j, :, HALF:C] = right[:, lanes]


def unpack(mine, other):
    return call(unpack_body, (shape((9, C, C), BF16), shape((3, C, C), BF16)))(mine, other)


def neighbours(first, second):
    size = lax.axis_size(FRAME)
    before = lax.ppermute(second, FRAME, [(i, i + 1) for i in range(size - 1)])
    after = lax.ppermute(first, FRAME, [(i + 1, i) for i in range(size - 1)])
    return before, after


def swap_cores(value):
    return lax.ppermute(value, "c", [(0, 1), (1, 0)])


def everyone_total(value):
    plane = lax.axis_size(PLANE)
    value = value.reshape(plane, 1024 // plane, value.shape[1])
    return lax.all_to_all(value, PLANE, 0, 0)


def everyone_share(value, beside):
    plane, line = lax.axis_size(PLANE), lax.axis_size(LINE)
    width = value.shape[2]
    value = jnp.sum(value.astype(F32), axis=0)
    value = value.reshape(line, 1024 // plane // line, width)
    value = jnp.sum(lax.all_to_all(value, LINE, 0, 0), axis=0).astype(BF16)
    value, *beside = lax.optimization_barrier((value, *beside))
    value = jnp.broadcast_to(value[None], (line,) + value.shape)
    return beside, lax.all_to_all(value, LINE, 0, 0).reshape(1024 // plane, width)


def everyone_gets(value):
    plane = lax.axis_size(PLANE)
    value = jnp.broadcast_to(value[None], (plane,) + value.shape)
    return lax.all_to_all(value, PLANE, 0, 0).reshape(1024, value.shape[2])


def on_device(clips, cotangent, spatial_weight, temporal_weight, gain_one, gain_two):
    size = lax.axis_size(FRAME)
    count = float(size * ROWS * C // GROUPS)
    x = clips.reshape(ROWS, C)
    cot = cotangent.reshape(ROWS, C)
    spatial_weight = spatial_weight.reshape(9, C, C)
    barrier = lax.optimization_barrier
    cot_before, cot_after = neighbours(cot[:PIX], cot[PIX:])
    h0, h1, mine_turned, stat_one, sums = forward(x, spatial_weight, gain_one, size)
    sums = lax.all_to_all(sums, FRAME, 0, 0)
    mixed_grad = mixed_gradient(cot_before, cot, cot_after, temporal_weight)
    sums, mine_turned, mixed_grad = barrier((sums, mine_turned, mixed_grad))
    other_turned = swap_cores(mine_turned)
    part, clip_stat, sums, far_stat = slopes(sums, h0, h1, mixed_grad, cot, gain_two, count)
    sums = lax.all_to_all(sums, FRAME, 0, 0)
    temporal_keep, temporal_give = temporal_gradient(
        h0, h1, cot_before, cot, cot_after, clip_stat, sums
    )
    temporal_got = swap_cores(temporal_give)
    low_keep, low_give, total = hidden_gradient(sums, clip_stat, part, h0, h1, count)
    low_got = swap_cores(low_give)
    packed = weight_gradients(
        mine_turned, other_turned, low_keep, low_got, temporal_keep, temporal_got
    )
    packed, total, edge0, edge1 = barrier((packed, total, h0, h1))
    shares = everyone_total(packed)
    before, after = neighbours(edge0, edge1)
    input_grad = input_gradient(
        part, h0, h1, far_stat, total, x, stat_one, spatial_weight
    )
    shares, input_grad = barrier((shares, input_grad))
    (before, after), mine = everyone_share(shares, (before, after))
    mine, before, after = barrier((mine, before, after))
    output = temporal(before, h0, h1, after, far_stat, temporal_weight)
    mine, output = barrier((everyone_gets(mine), output))
    other = swap_cores(mine)
    spatial_grad, temporal_grad = unpack(mine, other)
    return (
        output.reshape(clips.shape),
        input_grad.reshape(clips.shape),
        spatial_grad.reshape(3, 3, C, C),
        temporal_grad,
    )


def solution(mesh):
    fine = Mesh(mesh.devices.reshape(2, 4, 2, 4, 4), ("zl", "x", "c", "y", "zh"))
    return jax.shard_map(
        on_device,
        mesh=fine,
        in_specs=(P(DP, FRAME), P(DP, FRAME), P(), P(), P(), P()),
        out_specs=(P(DP, FRAME), P(DP, FRAME), P(), P()),
        check_vma=False,
    )
```

```python
import functools

import jax
import jax.numpy as jnp
from jax import lax
from jax.experimental import pallas as pl
from jax.experimental.pallas import tpu as pltpu
from jax.sharding import Mesh, PartitionSpec as P

epsilon = 1e-05

GROUPS = 32
DP = ("zl", "x", "c")
FRAME = ("y", "zh")
PLANE = ("x", "y")
LINE = ("zl", "zh")

C = 320
W = 32
PAD = 384
HALF = C // 2
PIX = 512
ROWS = 2 * PIX
STEP = 128
F32 = jnp.float32
BF16 = jnp.bfloat16

MIB = 1024 * 1024


VMEM = pl.BlockSpec(memory_space=pltpu.VMEM)
FAR = pl.BlockSpec(memory_space=pltpu.HBM)


def call(body, out, scratch=(), flops=0, limit=12, ins=None, outs=None):
    specs = {}
    if ins is not None:
        specs = {"in_specs": ins, "out_specs": outs}
    return pl.pallas_call(
        body,
        out_shape=out,
        scratch_shapes=list(scratch),
        compiler_params=pltpu.CompilerParams(vmem_limit_bytes=limit * MIB),
        cost_estimate=pl.CostEstimate(flops=flops, transcendentals=0, bytes_accessed=8_000_000),
        **specs,
    )


def shape(dims, kind):
    return jax.ShapeDtypeStruct(dims, kind)


def far(dims, kind):
    return pltpu.HBM(dims, kind)


def in_hbm(value):
    return pltpu.with_memory_space_constraint(value, pltpu.HBM)


def at(step, size=STEP):
    return pl.ds(pl.multiple_of(step * size, size), size)


def group_sum(rows):
    per = C // GROUPS
    one = lax.broadcasted_iota(jnp.int32, (C, C), 0) * 6554 >> 16
    two = lax.broadcasted_iota(jnp.int32, (C, C), 1) * 6554 >> 16
    assert per == 10
    same = jnp.where(one == two, 1.0, 0.0).astype(F32)
    return jnp.dot(rows, same, precision=lax.Precision.HIGHEST, preferred_element_type=F32)


def fold(value):
    return jnp.sum(value.reshape(value.shape[0] // 8, 8, value.shape[1]), axis=0)


def column(width):
    return lax.broadcasted_iota(jnp.int32, (STEP, width), 0) & (W - 1)


def four(*sums):
    return jnp.concatenate([jnp.sum(s, axis=0, keepdims=True) for s in sums] + [jnp.zeros((8 - len(sums), C), F32)])


def sigmoid(value):
    return 1.0 / (1.0 + jnp.exp(-value))


def forward_body(
    x_ref, far_w_ref, gain_ref, h0_ref, h1_ref, far_turned_ref, far_stat_ref, sums_ref,
    w_ref, wf, x3, y, turned, stat_ref, w_sem, turned_sem, stat_sem,
):
    fetch = pltpu.make_async_copy(far_w_ref, w_ref, w_sem)
    fetch.start()
    zero = jnp.zeros((8, C), F32)

    def moments(step, carry):
        value = x_ref[at(step), :].astype(F32)
        return carry[0] + fold(value), carry[1] + fold(value * value)

    half = PIX // STEP
    s0, q0 = lax.fori_loop(0, half, moments, (zero, zero))
    s1, q1 = lax.fori_loop(half, 2 * half, moments, (zero, zero))
    grouped = group_sum(four(s0, q0, s1, q1)) * (1.0 / (PIX * C // GROUPS))
    stats = []
    for f in range(2):
        mean = grouped[2 * f : 2 * f + 1]
        var = grouped[2 * f + 1 : 2 * f + 2] - mean * mean
        stats += [mean, lax.rsqrt(var + epsilon)]
    gain = gain_ref[...].reshape(1, C)
    stat_ref[...] = jnp.concatenate([*stats, gain, jnp.zeros((3, C), F32)])
    sends = [pltpu.make_async_copy(stat_ref, far_stat_ref, stat_sem)]
    sends[0].start()
    edge = column(C)

    def activate(step, mean, scale):
        value = x_ref[at(step), :].astype(F32)
        pre = (value - mean) * scale * gain
        act = pre / (1.0 + jnp.exp(-pre))
        low = act.astype(BF16)
        act = low.astype(F32)
        x3[at(step), 0:C] = jnp.where(edge == 0, 0.0, pltpu.roll(act, 1, 0)).astype(BF16)
        x3[at(step), C : 2 * C] = low
        x3[at(step), 2 * C : 3 * C] = jnp.where(
            edge == W - 1, 0.0, pltpu.roll(act, STEP - 1, 0)
        ).astype(BF16)

    total = (zero, zero)
    for f in range(2):
        mean, scale = stats[2 * f], stats[2 * f + 1]

        def act_step(step, carry, mean=mean, scale=scale):
            activate(step, mean, scale)
            return carry

        if f == 0:
            lax.fori_loop(f * half, (f + 1) * half, act_step, 0)
            fetch.wait()
            for i in range(3):
                for j in range(3):
                    wf[C * j : C * (j + 1), PAD * i : PAD * i + C] = w_ref[3 * i + j]
        y[f, 0:W, :] = jnp.zeros((W, 3 * PAD), F32)
        y[f, W + PIX : 2 * W + PIX, :] = jnp.zeros((W, 3 * PAD), F32)
        y[f, W : W + PIX, :] = jnp.dot(
            x3[f * PIX : (f + 1) * PIX, :], wf[...], preferred_element_type=F32
        )
        if f == 0:
            for step in range(half, 2 * half):
                activate(step, stats[2], stats[3])

        turn(x3[f * PIX : (f + 1) * PIX, C : 2 * C], turned.at[f])
        send = pltpu.make_async_copy(
            turned.at[f], far_turned_ref.at[:, f * PIX : (f + 1) * PIX], turned_sem.at[f]
        )
        send.start()
        sends.append(send)
        h_ref = (h0_ref, h1_ref)[f]

        def finish(step, carry, f=f, h_ref=h_ref):
            base = pl.multiple_of(step * STEP, STEP)
            conv = (
                y[f, pl.ds(base, STEP), 0:C]
                + y[f, pl.ds(base + W, STEP), PAD : PAD + C]
                + y[f, pl.ds(base + 2 * W, STEP), 2 * PAD : 2 * PAD + C]
            )
            value = x_ref[pl.ds(base + f * PIX, STEP), :].astype(F32)
            low = (value + conv).astype(BF16)
            h_ref[pl.ds(base, STEP), :] = low
            value = low.astype(F32)
            return carry[0] + fold(value), carry[1] + fold(value * value)

        total = lax.fori_loop(0, half, finish, total)
    spread(total, sums_ref)
    for send in sends:
        send.wait()


def spread(total, sums_ref):
    first = jnp.sum(total[0], axis=0, keepdims=True)
    second = jnp.sum(total[1], axis=0, keepdims=True)
    both = jnp.concatenate([first, second])
    for k in range(sums_ref.shape[0]):
        sums_ref[k] = both


def turn(acts, out_ref):
    rows = lax.broadcasted_iota(jnp.int32, (C, C), 0)
    same = jnp.where(rows == lax.broadcasted_iota(jnp.int32, (C, C), 1), 1.0, 0.0).astype(BF16)
    lane = lax.broadcasted_iota(jnp.int32, (C, STEP), 1) & (W - 1)
    moved = times_transposed(same, acts)
    for step in range(PIX // STEP):
        part = moved[:, step * STEP : (step + 1) * STEP]
        where = slice(step * STEP, (step + 1) * STEP)
        out_ref[0:C, where] = jnp.where(lane == 0, 0.0, pltpu.roll(part, 1, 1)).astype(BF16)
        out_ref[C : 2 * C, where] = part.astype(BF16)
        out_ref[2 * C : 3 * C, where] = jnp.where(
            lane == W - 1, 0.0, pltpu.roll(part, STEP - 1, 1)
        ).astype(BF16)


def forward(x, weight, gain, peers):
    return call(
        forward_body,
        (
            shape((PIX, C), BF16),
            shape((PIX, C), BF16),
            far((3 * C, ROWS), BF16),
            far((8, C), F32),
            shape((peers, 2, C), F32),
        ),
        (
            pltpu.VMEM((9, C, C), BF16),
            pltpu.VMEM((3 * C, 3 * PAD), BF16),
            pltpu.VMEM((ROWS, 3 * C), BF16),
            pltpu.VMEM((2, PIX + 2 * W, 3 * PAD), F32),
            pltpu.VMEM((2, 3 * C, PIX), BF16),
            pltpu.VMEM((8, C), F32),
            pltpu.SemaphoreType.DMA,
            pltpu.SemaphoreType.DMA((2,)),
            pltpu.SemaphoreType.DMA,
        ),
        flops=2_500_000_000,
        limit=24,
        ins=[VMEM, FAR, VMEM],
        outs=(VMEM, VMEM, FAR, FAR, VMEM),
    )(x, in_hbm(weight), gain)


def times_transposed(a, b):
    return lax.dot_general(a, b, (((1,), (1,)), ((), ())), preferred_element_type=F32)


def clip_stats(sums_ref, count):
    total = jnp.sum(sums_ref[...], axis=0)
    grouped = group_sum(jnp.concatenate([total, jnp.zeros((6, C), F32)])) * (1.0 / count)
    return grouped[0:1], grouped[1:2]


def mixed_grad_body(before_ref, cot_ref, after_ref, w_ref, out_ref):
    for f in range(2):
        last = cot_ref[0:PIX, :] if f else before_ref[...]
        later = after_ref[...] if f else cot_ref[PIX:ROWS, :]
        total = times_transposed(later, w_ref[0])
        total = total + times_transposed(cot_ref[f * PIX : (f + 1) * PIX, :], w_ref[1])
        total = total + times_transposed(last, w_ref[2])
        out_ref[f * PIX : (f + 1) * PIX, :] = total.astype(BF16)


def mixed_gradient(before, cot, after, weight):
    return call(mixed_grad_body, far((ROWS, C), BF16), flops=1_500_000_000)(
        before, cot, after, weight
    )


def slope_body(
    count, sums_ref, h0_ref, h1_ref, far_grad_ref, cot_ref, gain_ref,
    part_ref, stat_ref, out_ref, far_stat_ref, grad_ref, sem, grad_sem,
):
    fetch = pltpu.make_async_copy(far_grad_ref, grad_ref, grad_sem)
    fetch.start()
    mean, square = clip_stats(sums_ref, count)
    scale = lax.rsqrt(square - mean * mean + epsilon)
    gain = gain_ref[...].reshape(1, C)
    stat_ref[...] = jnp.concatenate([mean, scale, gain, jnp.zeros((5, C), F32)])
    send = pltpu.make_async_copy(stat_ref, far_stat_ref, sem)
    send.start()
    fetch.wait()
    zero = jnp.zeros((8, C), F32)
    total = (zero, zero)
    for f, h_ref in enumerate((h0_ref, h1_ref)):

        def step_body(step, carry, f=f, h_ref=h_ref):
            base = pl.multiple_of(step * STEP, STEP)
            there = pl.ds(base + f * PIX, STEP)
            hat = (h_ref[pl.ds(base, STEP), :].astype(F32) - mean) * scale
            pre = hat * gain
            s = sigmoid(pre)
            slope = s * (1.0 + pre * (1.0 - s))
            dhat = grad_ref[there, :].astype(F32) * slope * gain
            part_ref[there, :] = cot_ref[there, :].astype(F32) + scale * dhat
            return carry[0] + fold(dhat), carry[1] + fold(dhat * hat)

        total = lax.fori_loop(0, PIX // STEP, step_body, total)
    spread(total, out_ref)
    send.wait()


def slopes(sums, h0, h1, grad, cot, gain, count):
    return call(
        functools.partial(slope_body, count),
        (shape((ROWS, C), F32), shape((8, C), F32), shape(sums.shape, F32), far((8, C), F32)),
        (pltpu.VMEM((ROWS, C), BF16), pltpu.SemaphoreType.DMA, pltpu.SemaphoreType.DMA),
        ins=[VMEM] * 3 + [FAR] + [VMEM] * 2,
        outs=(VMEM, VMEM, VMEM, FAR),
    )(sums, h0, h1, in_hbm(grad), cot, gain)


def mix(h_ref, base, mean, scale, gain):
    pre = (h_ref[pl.ds(base, STEP), :].astype(F32) - mean) * scale * gain
    return pre / (1.0 + jnp.exp(-pre))


def mixed_body(
    h0_ref, h1_ref, before_ref, cot_ref, after_ref, stat_ref, sums_ref,
    keep_ref, give_ref, turned,
):
    mean, scale, gain = stat_ref[0:1, :], stat_ref[1:2, :], stat_ref[2:3, :]
    for f, h_ref in enumerate((h0_ref, h1_ref)):
        for step in range(PIX // STEP):
            act = mix(h_ref, step * STEP, mean, scale, gain).astype(BF16)
            turned[:, f * PIX + step * STEP : f * PIX + (step + 1) * STEP] = act.T
    core = lax.axis_index("c")
    first, second = turned[:, 0:PIX], turned[:, PIX:ROWS]
    for k in range(3):
        if k == 1:
            part = jnp.dot(turned[...], cot_ref[...], preferred_element_type=F32)
        else:
            one = cot_ref[PIX:ROWS, :] if k == 0 else before_ref[...]
            two = after_ref[...] if k == 0 else cot_ref[0:PIX, :]
            part = jnp.dot(first, one, preferred_element_type=F32)
            part = part + jnp.dot(second, two, preferred_element_type=F32)
        left, right = part[:, 0:HALF], part[:, HALF:C]
        keep_ref[k * C : (k + 1) * C, 0:HALF] = jnp.where(core == 0, left, right)
        give_ref[k * C : (k + 1) * C, 0:HALF] = jnp.where(core == 0, right, left)


def temporal_gradient(h0, h1, before, cot, after, stat, sums):
    return call(
        mixed_body,
        (shape((3 * C, 256), F32), shape((3 * C, 256), F32)),
        (pltpu.VMEM((C, ROWS), BF16),),
        flops=1_500_000_000,
    )(h0, h1, before, cot, after, stat, sums)


def temporal_body(
    hb_ref, h0_ref, h1_ref, ha_ref, far_stat_ref, w_ref, out_ref, mx_ref, stat_ref, sem
):
    fetch = pltpu.make_async_copy(far_stat_ref, stat_ref, sem)
    fetch.start()
    fetch.wait()
    mean, scale, gain = stat_ref[0:1, :], stat_ref[1:2, :], stat_ref[2:3, :]
    place = lax.axis_index(FRAME)
    live = (place > 0, None, None, place < lax.axis_size(FRAME) - 1)
    for n, h_ref in enumerate((hb_ref, h0_ref, h1_ref, ha_ref)):

        def step_body(step, carry, n=n, h_ref=h_ref):
            base = pl.multiple_of(step * STEP, STEP)
            act = mix(h_ref, base, mean, scale, gain)
            if live[n] is not None:
                act = jnp.where(live[n], act, 0.0)
            mx_ref[pl.ds(base + n * PIX, STEP), :] = act.astype(BF16)
            return carry

        lax.fori_loop(0, PIX // STEP, step_body, 0)
    for f, h_ref in enumerate((h0_ref, h1_ref)):
        total = None
        for k in range(3):
            part = jnp.dot(
                mx_ref[(f + k) * PIX : (f + k + 1) * PIX, :],
                w_ref[k],
                preferred_element_type=F32,
            )
            total = part if total is None else total + part
        low = total.astype(BF16).astype(F32)
        out_ref[f * PIX : (f + 1) * PIX, :] = (h_ref[...].astype(F32) + low).astype(BF16)


def temporal(before, h0, h1, after, stat, weight):
    return call(
        temporal_body,
        shape((ROWS, C), BF16),
        (pltpu.VMEM((4 * PIX, C), BF16), pltpu.VMEM((8, C), F32), pltpu.SemaphoreType.DMA),
        flops=1_500_000_000,
        ins=[VMEM] * 4 + [FAR, VMEM],
        outs=VMEM,
    )(before, h0, h1, after, in_hbm(stat), weight)


def whole_grad(part_ref, h_ref, stat_ref, sums, base, f):
    mean, scale = stat_ref[0:1, :], stat_ref[1:2, :]
    hat = (h_ref[pl.ds(base, STEP), :].astype(F32) - mean) * scale
    return part_ref[pl.ds(base + f * PIX, STEP), :] - scale * (sums[0] + hat * sums[1])


def hidden_grad_body(
    count, sums_ref, stat_ref, part_ref, h0_ref, h1_ref,
    keep_ref, give_ref, far_total_ref, total_ref, sem,
):
    sums = clip_stats(sums_ref, count)
    total_ref[...] = jnp.concatenate([*sums, jnp.zeros((6, C), F32)])
    send = pltpu.make_async_copy(total_ref, far_total_ref, sem)
    send.start()
    core = lax.axis_index("c")
    for f, h_ref in enumerate((h0_ref, h1_ref)):

        def step_body(step, carry, f=f, h_ref=h_ref):
            base = pl.multiple_of(step * STEP, STEP)
            here = pl.ds(base + f * PIX, STEP)
            grad = whole_grad(part_ref, h_ref, stat_ref, sums, base, f)
            left, right = grad[:, 0:HALF], grad[:, HALF:C]
            keep_ref[here, :] = jnp.where(core == 0, left, right).astype(BF16)
            give_ref[here, :] = jnp.where(core == 0, right, left).astype(BF16)
            return carry

        lax.fori_loop(0, PIX // STEP, step_body, 0)
    send.wait()


def hidden_gradient(sums, stat, part, h0, h1, count):
    return call(
        functools.partial(hidden_grad_body, count),
        (shape((ROWS, HALF), BF16), shape((ROWS, HALF), BF16), far((8, C), F32)),
        (pltpu.VMEM((8, C), F32), pltpu.SemaphoreType.DMA),
        ins=[VMEM] * 5,
        outs=(VMEM, VMEM, FAR),
    )(sums, stat, part, h0, h1)


def row_taps(value):
    none = jnp.zeros((W, value.shape[1]), value.dtype)
    return (
        jnp.concatenate([value[W:], none]),
        value,
        jnp.concatenate([none, value[: PIX - W]]),
    )


def weight_grad_body(
    mine_turned_ref, other_turned_ref, mine_ref, other_ref, keep_ref, got_ref, far_ref, rhs, out, sem
):
    for n, ref in enumerate((mine_ref, other_ref)):
        for f in range(2):
            where = slice(f * PIX, (f + 1) * PIX)
            for i, tap in enumerate(row_taps(ref[where, :])):
                rhs[n, where, i * HALF : (i + 1) * HALF] = tap
    sends = []
    for j in range(3):
        here = slice(j * C, (j + 1) * C)
        total = jnp.dot(mine_turned_ref[here, :], rhs[0], preferred_element_type=F32)
        total = total + jnp.dot(other_turned_ref[here, :], rhs[1], preferred_element_type=F32)
        out[here, 0 : 3 * HALF] = total.astype(BF16)
        kept = keep_ref[here, 0:HALF] + got_ref[here, 0:HALF]
        out[here, 3 * HALF : 4 * HALF] = kept.astype(BF16)
        if j == 2:
            out[3 * C :, :] = jnp.zeros((1024 - 3 * C, 4 * HALF), BF16)
            here = slice(j * C, 1024)
        send = pltpu.make_async_copy(out.at[here, :], far_ref.at[here, :], sem.at[j])
        send.start()
        sends.append(send)
    for send in sends:
        send.wait()


def weight_gradients(mine_turned, other_turned, mine, other, keep, got):
    return call(
        weight_grad_body,
        far((1024, 4 * HALF), BF16),
        (
            pltpu.VMEM((2, ROWS, 3 * HALF), BF16),
            pltpu.VMEM((1024, 4 * HALF), BF16),
            pltpu.SemaphoreType.DMA((3,)),
        ),
        flops=2_500_000_000,
        ins=[VMEM] * 6,
        outs=FAR,
    )(mine_turned, other_turned, mine, other, keep, got)


def input_grad_body(
    f, part_ref, h_ref, far_clip_ref, far_total_ref, x_ref, far_stat_ref, far_w_ref, *rest
):
    far_out_ref, wb, rows, z, dh, grads, lows, clip_ref, total_ref, stat_ref, w_ref, sem = rest[f:]
    pairs = (far_clip_ref, clip_ref), (far_total_ref, total_ref), (far_stat_ref, stat_ref)
    fetches = [
        pltpu.make_async_copy(one, two, sem.at[n])
        for n, (one, two) in enumerate((*pairs, (far_w_ref, w_ref)))
    ]
    for fetch in fetches:
        fetch.start()
    for fetch in fetches[:3]:
        fetch.wait()
    clip_sums = total_ref[0:1, :], total_ref[1:2, :]
    gain = stat_ref[4:5, :]
    edge = column(C)
    half = PIX // STEP
    mean, scale = stat_ref[2 * f : 2 * f + 1, :], stat_ref[2 * f + 1 : 2 * f + 2, :]

    def grad_body(step, carry):
        base = pl.multiple_of(step * STEP, STEP)
        grad = whole_grad(part_ref, h_ref, clip_ref, clip_sums, base, f)
        grads[pl.ds(base, STEP), :] = grad
        lows[pl.ds(base, STEP), :] = grad.astype(BF16)
        return carry

    lax.fori_loop(0, half, grad_body, 0)
    fetches[3].wait()
    for j in range(3):
        for i in range(3):
            wb[PAD * j : PAD * j + C, C * i : C * (i + 1)] = w_ref[3 * i + j]
        wb[PAD * j + C : PAD * (j + 1), :] = jnp.zeros((PAD - C, 3 * C), BF16)
    for i, tap in enumerate(row_taps(lows[...])):
        rows[:, i * C : (i + 1) * C] = tap
    z[...] = times_transposed(rows[...], wb[...])

    def step_body(step, carry):
        base = pl.multiple_of(step * STEP, STEP)
        here = pl.ds(base, STEP)
        right = jnp.where(edge == W - 1, 0.0, pltpu.roll(z[here, 0:C], STEP - 1, 0))
        left = jnp.where(edge == 0, 0.0, pltpu.roll(z[here, 2 * PAD : 2 * PAD + C], 1, 0))
        acts_grad = right + z[here, PAD : PAD + C] + left
        hat = (x_ref[pl.ds(base + f * PIX, STEP), :].astype(F32) - mean) * scale
        pre = hat * gain
        s = sigmoid(pre)
        dhat = acts_grad * (s * (1.0 + pre * (1.0 - s))) * gain
        dh[here, :] = dhat
        return carry[0] + fold(dhat), carry[1] + fold(dhat * hat)

    zero = jnp.zeros((8, C), F32)
    sums = lax.fori_loop(0, half, step_body, (zero, zero))
    grouped = group_sum(four(*sums)) * (1.0 / (PIX * C // GROUPS))
    first, second = grouped[0:1], grouped[1:2]

    def last_body(step, carry):
        base = pl.multiple_of(step * STEP, STEP)
        here = pl.ds(base, STEP)
        hat = (x_ref[pl.ds(base + f * PIX, STEP), :].astype(F32) - mean) * scale
        value = grads[here, :] + scale * (dh[here, :] - first - hat * second)
        lows[here, :] = value.astype(BF16)
        return carry

    lax.fori_loop(0, half, last_body, 0)
    send = pltpu.make_async_copy(lows, far_out_ref.at[f * PIX : (f + 1) * PIX, :], sem.at[4])
    send.start()
    send.wait()


def input_gradient(f, part, h, clip_stat, total, x, stat, weight, *held):
    return pl.pallas_call(
        functools.partial(input_grad_body, f),
        out_shape=far((ROWS, C), BF16),
        in_specs=[VMEM] * 2 + [FAR] * 2 + [VMEM] + [FAR] * (2 + f),
        out_specs=FAR,
        scratch_shapes=[
            pltpu.VMEM((3 * PAD, 3 * C), BF16),
            pltpu.VMEM((PIX, 3 * C), BF16),
            pltpu.VMEM((PIX, 3 * PAD), F32),
            pltpu.VMEM((PIX, C), F32),
            pltpu.VMEM((PIX, C), F32),
            pltpu.VMEM((PIX, C), BF16),
            pltpu.VMEM((8, C), F32),
            pltpu.VMEM((8, C), F32),
            pltpu.VMEM((8, C), F32),
            pltpu.VMEM((9, C, C), BF16),
            pltpu.SemaphoreType.DMA((5,)),
        ],
        input_output_aliases={7: 0} if held else {},
        compiler_params=pltpu.CompilerParams(vmem_limit_bytes=16 * MIB),
        cost_estimate=pl.CostEstimate(
            flops=1_500_000_000, transcendentals=0, bytes_accessed=8_000_000
        ),
    )(part, h, in_hbm(clip_stat), in_hbm(total), x, in_hbm(stat), in_hbm(weight), *held)


def unpack_body(mine_ref, other_ref, far_spatial_ref, far_temporal_ref, taps, sem):
    core = lax.axis_index("c")
    sends = []
    for j in range(3):
        here = slice(j * C, (j + 1) * C)
        mine, other = mine_ref[here, :], other_ref[here, :]
        left = jnp.where(core == 0, mine, other)
        right = jnp.where(core == 0, other, mine)
        for i in range(4):
            n = 3 * i + j
            lanes = slice(i * HALF, (i + 1) * HALF)
            taps[n, :, 0:HALF] = left[:, lanes]
            taps[n, :, HALF:C] = right[:, lanes]
            target = far_spatial_ref.at[n] if i < 3 else far_temporal_ref.at[j]
            send = pltpu.make_async_copy(taps.at[n], target, sem.at[n])
            send.start()
            sends.append(send)
    for send in sends:
        send.wait()


def unpack(mine, other):
    return call(
        unpack_body,
        (far((9, C, C), BF16), far((3, C, C), BF16)),
        (pltpu.VMEM((12, C, C), BF16), pltpu.SemaphoreType.DMA((12,))),
        ins=[VMEM] * 2,
        outs=(FAR, FAR),
    )(mine, other)


def frames_body(value_ref, first_ref, second_ref, sem):
    copies = [
        pltpu.make_async_copy(value_ref.at[0:PIX, :], first_ref, sem.at[0]),
        pltpu.make_async_copy(value_ref.at[PIX:ROWS, :], second_ref, sem.at[1]),
    ]
    for copy in copies:
        copy.start()
    for copy in copies:
        copy.wait()


def frames(value):
    return call(
        frames_body,
        (far((PIX, C), BF16), far((PIX, C), BF16)),
        (pltpu.SemaphoreType.DMA((2,)),),
        limit=1,
        ins=[FAR],
        outs=(FAR, FAR),
    )(in_hbm(value))


def neighbours(first, second):
    size = lax.axis_size(FRAME)
    before = lax.ppermute(second, FRAME, [(i, i + 1) for i in range(size - 1)])
    after = lax.ppermute(first, FRAME, [(i + 1, i) for i in range(size - 1)])
    return before, after


def swap_cores(value):
    return lax.ppermute(value, "c", [(0, 1), (1, 0)])


def everyone_total(value):
    plane = lax.axis_size(PLANE)
    value = value.reshape(plane, 1024 // plane, value.shape[1])
    return lax.all_to_all(value, PLANE, 0, 0)


def everyone_share(value, beside):
    plane, line = lax.axis_size(PLANE), lax.axis_size(LINE)
    width = value.shape[2]
    value = jnp.sum(value.astype(F32), axis=0)
    value = value.reshape(line, 1024 // plane // line, width)
    value = jnp.sum(lax.all_to_all(value, LINE, 0, 0), axis=0).astype(BF16)
    value, *beside = lax.optimization_barrier((value, *beside))
    value = jnp.broadcast_to(value[None], (line,) + value.shape)
    return beside, lax.all_to_all(value, LINE, 0, 0).reshape(1024 // plane, width)


def everyone_gets(value):
    plane = lax.axis_size(PLANE)
    value = jnp.broadcast_to(value[None], (plane,) + value.shape)
    return lax.all_to_all(value, PLANE, 0, 0).reshape(1024, value.shape[2])


def on_device(clips, cotangent, spatial_weight, temporal_weight, gain_one, gain_two):
    size = lax.axis_size(FRAME)
    count = float(size * ROWS * C // GROUPS)
    x = clips.reshape(ROWS, C)
    cot = cotangent.reshape(ROWS, C)
    spatial_weight = spatial_weight.reshape(9, C, C)
    barrier = lax.optimization_barrier
    cot_before, cot_after = neighbours(*frames(cot))
    h0, h1, mine_turned, stat_one, sums = forward(x, spatial_weight, gain_one, size)
    sums = lax.all_to_all(sums, FRAME, 0, 0)
    mixed_grad = mixed_gradient(cot_before, cot, cot_after, temporal_weight)
    sums, mine_turned, mixed_grad = barrier((sums, mine_turned, mixed_grad))
    other_turned = swap_cores(mine_turned)
    part, clip_stat, sums, far_stat = slopes(sums, h0, h1, mixed_grad, cot, gain_two, count)
    sums = lax.all_to_all(sums, FRAME, 0, 0)
    temporal_keep, temporal_give = temporal_gradient(
        h0, h1, cot_before, cot, cot_after, clip_stat, sums
    )
    temporal_got = swap_cores(temporal_give)
    low_keep, low_give, total = hidden_gradient(sums, clip_stat, part, h0, h1, count)
    low_got = swap_cores(low_give)
    packed = weight_gradients(
        mine_turned, other_turned, low_keep, low_got, temporal_keep, temporal_got
    )
    packed, total, edge0, edge1 = barrier((packed, total, h0, h1))
    shares = everyone_total(packed)
    before, after = neighbours(edge0, edge1)
    input_grad = input_gradient(0, part, h0, far_stat, total, x, stat_one, spatial_weight)
    shares, input_grad = barrier((shares, input_grad))
    (before, after), mine = everyone_share(shares, (before, after))
    mine, before, after, input_grad = barrier((mine, before, after, input_grad))
    input_grad = input_gradient(
        1, part, h1, far_stat, total, x, stat_one, spatial_weight, input_grad
    )
    output = temporal(before, h0, h1, after, far_stat, temporal_weight)
    mine, output, input_grad = barrier((everyone_gets(mine), output, input_grad))
    other = swap_cores(mine)
    spatial_grad, temporal_grad = unpack(mine, other)
    return (
        output.reshape(clips.shape),
        input_grad.reshape(clips.shape),
        spatial_grad.reshape(3, 3, C, C),
        temporal_grad,
    )


def solution(mesh):
    fine = Mesh(mesh.devices.reshape(2, 4, 2, 4, 4), ("zl", "x", "c", "y", "zh"))
    return jax.shard_map(
        on_device,
        mesh=fine,
        in_specs=(P(DP, FRAME), P(DP, FRAME), P(), P(), P(), P()),
        out_specs=(P(DP, FRAME), P(DP, FRAME), P(), P()),
        check_vma=False,
    )
```

```python
import functools

import jax
import jax.numpy as jnp
from jax import lax
from jax.experimental import pallas as pl
from jax.experimental.pallas import tpu as pltpu
from jax.sharding import Mesh, PartitionSpec as P

epsilon = 1e-05

GROUPS = 32
DP = ("zl", "x", "c")
FRAME = ("y", "zh")
PLANE = ("x", "y")
LINE = ("zl", "zh")

C = 320
W = 32
PAD = 384
HALF = C // 2
PIX = 512
ROWS = 2 * PIX
STEP = 128
F32 = jnp.float32
BF16 = jnp.bfloat16

MIB = 1024 * 1024


VMEM = pl.BlockSpec(memory_space=pltpu.VMEM)
FAR = pl.BlockSpec(memory_space=pltpu.HBM)


def call(body, out, scratch=(), flops=0, limit=12, ins=None, outs=None):
    specs = {}
    if ins is not None:
        specs = {"in_specs": ins, "out_specs": outs}
    return pl.pallas_call(
        body,
        out_shape=out,
        scratch_shapes=list(scratch),
        compiler_params=pltpu.CompilerParams(vmem_limit_bytes=limit * MIB),
        cost_estimate=pl.CostEstimate(flops=flops, transcendentals=0, bytes_accessed=8_000_000),
        **specs,
    )


def shape(dims, kind):
    return jax.ShapeDtypeStruct(dims, kind)


def far(dims, kind):
    return pltpu.HBM(dims, kind)


def in_hbm(value):
    return pltpu.with_memory_space_constraint(value, pltpu.HBM)


def at(step, size=STEP):
    return pl.ds(pl.multiple_of(step * size, size), size)


def group_sum(rows):
    per = C // GROUPS
    one = lax.broadcasted_iota(jnp.int32, (C, C), 0) * 6554 >> 16
    two = lax.broadcasted_iota(jnp.int32, (C, C), 1) * 6554 >> 16
    assert per == 10
    same = jnp.where(one == two, 1.0, 0.0).astype(F32)
    return jnp.dot(rows, same, precision=lax.Precision.HIGHEST, preferred_element_type=F32)


def fold(value):
    return jnp.sum(value.reshape(value.shape[0] // 8, 8, value.shape[1]), axis=0)


def column(width):
    return lax.broadcasted_iota(jnp.int32, (STEP, width), 0) & (W - 1)


def four(*sums):
    return jnp.concatenate([jnp.sum(s, axis=0, keepdims=True) for s in sums] + [jnp.zeros((8 - len(sums), C), F32)])


def sigmoid(value):
    return 1.0 / (1.0 + jnp.exp(-value))


def forward_body(
    x_ref, far_w_ref, gain_ref, h0_ref, h1_ref, far_turned_ref, far_stat_ref, sums_ref,
    w_ref, wf, x3, y, turned, stat_ref, w_sem, turned_sem, stat_sem,
):
    fetch = pltpu.make_async_copy(far_w_ref, w_ref, w_sem)
    fetch.start()
    zero = jnp.zeros((8, C), F32)

    def moments(step, carry):
        value = x_ref[at(step), :].astype(F32)
        return carry[0] + fold(value), carry[1] + fold(value * value)

    half = PIX // STEP
    s0, q0 = lax.fori_loop(0, half, moments, (zero, zero))
    s1, q1 = lax.fori_loop(half, 2 * half, moments, (zero, zero))
    grouped = group_sum(four(s0, q0, s1, q1)) * (1.0 / (PIX * C // GROUPS))
    stats = []
    for f in range(2):
        mean = grouped[2 * f : 2 * f + 1]
        var = grouped[2 * f + 1 : 2 * f + 2] - mean * mean
        stats += [mean, lax.rsqrt(var + epsilon)]
    gain = gain_ref[...].reshape(1, C)
    stat_ref[...] = jnp.concatenate([*stats, gain, jnp.zeros((3, C), F32)])
    sends = [pltpu.make_async_copy(stat_ref, far_stat_ref, stat_sem)]
    sends[0].start()
    edge = column(C)

    def activate(step, mean, scale):
        value = x_ref[at(step), :].astype(F32)
        pre = (value - mean) * scale * gain
        act = pre / (1.0 + jnp.exp(-pre))
        low = act.astype(BF16)
        act = low.astype(F32)
        x3[at(step), 0:C] = jnp.where(edge == 0, 0.0, pltpu.roll(act, 1, 0)).astype(BF16)
        x3[at(step), C : 2 * C] = low
        x3[at(step), 2 * C : 3 * C] = jnp.where(
            edge == W - 1, 0.0, pltpu.roll(act, STEP - 1, 0)
        ).astype(BF16)

    total = (zero, zero)
    for f in range(2):
        mean, scale = stats[2 * f], stats[2 * f + 1]

        def act_step(step, carry, mean=mean, scale=scale):
            activate(step, mean, scale)
            return carry

        if f == 0:
            lax.fori_loop(f * half, (f + 1) * half, act_step, 0)
            fetch.wait()
            for i in range(3):
                for j in range(3):
                    wf[C * j : C * (j + 1), PAD * i : PAD * i + C] = w_ref[3 * i + j]
        y[f, 0:W, :] = jnp.zeros((W, 3 * PAD), F32)
        y[f, W + PIX : 2 * W + PIX, :] = jnp.zeros((W, 3 * PAD), F32)
        y[f, W : W + PIX, :] = jnp.dot(
            x3[f * PIX : (f + 1) * PIX, :], wf[...], preferred_element_type=F32
        )
        if f == 0:
            for step in range(half, 2 * half):
                activate(step, stats[2], stats[3])

        turn(x3[f * PIX : (f + 1) * PIX, C : 2 * C], turned.at[f])
        send = pltpu.make_async_copy(
            turned.at[f], far_turned_ref.at[:, f * PIX : (f + 1) * PIX], turned_sem.at[f]
        )
        send.start()
        sends.append(send)
        h_ref = (h0_ref, h1_ref)[f]

        def finish(step, carry, f=f, h_ref=h_ref):
            base = pl.multiple_of(step * STEP, STEP)
            conv = (
                y[f, pl.ds(base, STEP), 0:C]
                + y[f, pl.ds(base + W, STEP), PAD : PAD + C]
                + y[f, pl.ds(base + 2 * W, STEP), 2 * PAD : 2 * PAD + C]
            )
            value = x_ref[pl.ds(base + f * PIX, STEP), :].astype(F32)
            low = (value + conv).astype(BF16)
            h_ref[pl.ds(base, STEP), :] = low
            value = low.astype(F32)
            return carry[0] + fold(value), carry[1] + fold(value * value)

        total = lax.fori_loop(0, half, finish, total)
    spread(total, sums_ref)
    for send in sends:
        send.wait()


def spread(total, sums_ref):
    first = jnp.sum(total[0], axis=0, keepdims=True)
    second = jnp.sum(total[1], axis=0, keepdims=True)
    both = jnp.concatenate([first, second])
    for k in range(sums_ref.shape[0]):
        sums_ref[k] = both


def turn(acts, out_ref):
    rows = lax.broadcasted_iota(jnp.int32, (C, C), 0)
    same = jnp.where(rows == lax.broadcasted_iota(jnp.int32, (C, C), 1), 1.0, 0.0).astype(BF16)
    lane = lax.broadcasted_iota(jnp.int32, (C, STEP), 1) & (W - 1)
    moved = times_transposed(same, acts)
    for step in range(PIX // STEP):
        part = moved[:, step * STEP : (step + 1) * STEP]
        where = slice(step * STEP, (step + 1) * STEP)
        out_ref[0:C, where] = jnp.where(lane == 0, 0.0, pltpu.roll(part, 1, 1)).astype(BF16)
        out_ref[C : 2 * C, where] = part.astype(BF16)
        out_ref[2 * C : 3 * C, where] = jnp.where(
            lane == W - 1, 0.0, pltpu.roll(part, STEP - 1, 1)
        ).astype(BF16)


def forward(x, weight, gain, peers):
    return call(
        forward_body,
        (
            shape((PIX, C), BF16),
            shape((PIX, C), BF16),
            far((3 * C, ROWS), BF16),
            far((8, C), F32),
            shape((peers, 2, C), F32),
        ),
        (
            pltpu.VMEM((9, C, C), BF16),
            pltpu.VMEM((3 * C, 3 * PAD), BF16),
            pltpu.VMEM((ROWS, 3 * C), BF16),
            pltpu.VMEM((2, PIX + 2 * W, 3 * PAD), F32),
            pltpu.VMEM((2, 3 * C, PIX), BF16),
            pltpu.VMEM((8, C), F32),
            pltpu.SemaphoreType.DMA,
            pltpu.SemaphoreType.DMA((2,)),
            pltpu.SemaphoreType.DMA,
        ),
        flops=2_500_000_000,
        limit=24,
        ins=[VMEM, FAR, VMEM],
        outs=(VMEM, VMEM, FAR, FAR, VMEM),
    )(x, in_hbm(weight), gain)


def times_transposed(a, b):
    return lax.dot_general(a, b, (((1,), (1,)), ((), ())), preferred_element_type=F32)


def clip_stats(sums_ref, count):
    total = jnp.sum(sums_ref[...], axis=0)
    grouped = group_sum(jnp.concatenate([total, jnp.zeros((6, C), F32)])) * (1.0 / count)
    return grouped[0:1], grouped[1:2]


def mixed_grad_body(before_ref, cot_ref, after_ref, w_ref, far_ref, out_ref, sem):
    sends = []
    for f in range(2):
        here = slice(f * PIX, (f + 1) * PIX)
        last = cot_ref[0:PIX, :] if f else before_ref[...]
        later = after_ref[...] if f else cot_ref[PIX:ROWS, :]
        total = times_transposed(later, w_ref[0])
        total = total + times_transposed(cot_ref[here, :], w_ref[1])
        total = total + times_transposed(last, w_ref[2])
        out_ref[here, :] = total.astype(BF16)
        send = pltpu.make_async_copy(out_ref.at[here, :], far_ref.at[here, :], sem.at[f])
        send.start()
        sends.append(send)
    for send in sends:
        send.wait()


def mixed_gradient(before, cot, after, weight):
    return call(
        mixed_grad_body,
        far((ROWS, C), BF16),
        (pltpu.VMEM((ROWS, C), BF16), pltpu.SemaphoreType.DMA((2,))),
        flops=1_500_000_000,
        ins=[VMEM] * 4,
        outs=FAR,
    )(before, cot, after, weight)


def slope_body(
    count, sums_ref, h0_ref, h1_ref, far_grad_ref, cot_ref, gain_ref,
    part_ref, stat_ref, out_ref, far_stat_ref, grad_ref, sem, grad_sem,
):
    fetch = pltpu.make_async_copy(far_grad_ref, grad_ref, grad_sem)
    fetch.start()
    mean, square = clip_stats(sums_ref, count)
    scale = lax.rsqrt(square - mean * mean + epsilon)
    gain = gain_ref[...].reshape(1, C)
    stat_ref[...] = jnp.concatenate([mean, scale, gain, jnp.zeros((5, C), F32)])
    send = pltpu.make_async_copy(stat_ref, far_stat_ref, sem)
    send.start()
    fetch.wait()
    zero = jnp.zeros((8, C), F32)
    total = (zero, zero)
    for f, h_ref in enumerate((h0_ref, h1_ref)):

        def step_body(step, carry, f=f, h_ref=h_ref):
            base = pl.multiple_of(step * STEP, STEP)
            there = pl.ds(base + f * PIX, STEP)
            hat = (h_ref[pl.ds(base, STEP), :].astype(F32) - mean) * scale
            pre = hat * gain
            s = sigmoid(pre)
            slope = s * (1.0 + pre * (1.0 - s))
            dhat = grad_ref[there, :].astype(F32) * slope * gain
            part_ref[there, :] = cot_ref[there, :].astype(F32) + scale * dhat
            return carry[0] + fold(dhat), carry[1] + fold(dhat * hat)

        total = lax.fori_loop(0, PIX // STEP, step_body, total)
    spread(total, out_ref)
    send.wait()


def slopes(sums, h0, h1, grad, cot, gain, count):
    return call(
        functools.partial(slope_body, count),
        (shape((ROWS, C), F32), shape((8, C), F32), shape(sums.shape, F32), far((8, C), F32)),
        (pltpu.VMEM((ROWS, C), BF16), pltpu.SemaphoreType.DMA, pltpu.SemaphoreType.DMA),
        ins=[VMEM] * 3 + [FAR] + [VMEM] * 2,
        outs=(VMEM, VMEM, VMEM, FAR),
    )(sums, h0, h1, in_hbm(grad), cot, gain)


def mix(h_ref, base, mean, scale, gain):
    pre = (h_ref[pl.ds(base, STEP), :].astype(F32) - mean) * scale * gain
    return pre / (1.0 + jnp.exp(-pre))


def mixed_body(
    h0_ref, h1_ref, before_ref, cot_ref, after_ref, stat_ref, sums_ref,
    keep_ref, give_ref, turned,
):
    mean, scale, gain = stat_ref[0:1, :], stat_ref[1:2, :], stat_ref[2:3, :]
    for f, h_ref in enumerate((h0_ref, h1_ref)):
        for step in range(PIX // STEP):
            act = mix(h_ref, step * STEP, mean, scale, gain).astype(BF16)
            turned[:, f * PIX + step * STEP : f * PIX + (step + 1) * STEP] = act.T
    core = lax.axis_index("c")
    first, second = turned[:, 0:PIX], turned[:, PIX:ROWS]
    for k in range(3):
        if k == 1:
            part = jnp.dot(turned[...], cot_ref[...], preferred_element_type=F32)
        else:
            one = cot_ref[PIX:ROWS, :] if k == 0 else before_ref[...]
            two = after_ref[...] if k == 0 else cot_ref[0:PIX, :]
            part = jnp.dot(first, one, preferred_element_type=F32)
            part = part + jnp.dot(second, two, preferred_element_type=F32)
        left, right = part[:, 0:HALF], part[:, HALF:C]
        keep_ref[k * C : (k + 1) * C, 0:HALF] = jnp.where(core == 0, left, right)
        give_ref[k * C : (k + 1) * C, 0:HALF] = jnp.where(core == 0, right, left)


def temporal_gradient(h0, h1, before, cot, after, stat, sums):
    return call(
        mixed_body,
        (shape((3 * C, 256), F32), shape((3 * C, 256), F32)),
        (pltpu.VMEM((C, ROWS), BF16),),
        flops=1_500_000_000,
    )(h0, h1, before, cot, after, stat, sums)


def temporal_body(
    hb_ref, h0_ref, h1_ref, ha_ref, far_stat_ref, w_ref, out_ref, mx_ref, stat_ref, sem
):
    fetch = pltpu.make_async_copy(far_stat_ref, stat_ref, sem)
    fetch.start()
    fetch.wait()
    mean, scale, gain = stat_ref[0:1, :], stat_ref[1:2, :], stat_ref[2:3, :]
    place = lax.axis_index(FRAME)
    live = (place > 0, None, None, place < lax.axis_size(FRAME) - 1)
    for n, h_ref in enumerate((hb_ref, h0_ref, h1_ref, ha_ref)):

        def step_body(step, carry, n=n, h_ref=h_ref):
            base = pl.multiple_of(step * STEP, STEP)
            act = mix(h_ref, base, mean, scale, gain)
            if live[n] is not None:
                act = jnp.where(live[n], act, 0.0)
            mx_ref[pl.ds(base + n * PIX, STEP), :] = act.astype(BF16)
            return carry

        lax.fori_loop(0, PIX // STEP, step_body, 0)
    for f, h_ref in enumerate((h0_ref, h1_ref)):
        total = None
        for k in range(3):
            part = jnp.dot(
                mx_ref[(f + k) * PIX : (f + k + 1) * PIX, :],
                w_ref[k],
                preferred_element_type=F32,
            )
            total = part if total is None else total + part
        low = total.astype(BF16).astype(F32)
        out_ref[f * PIX : (f + 1) * PIX, :] = (h_ref[...].astype(F32) + low).astype(BF16)


def temporal(before, h0, h1, after, stat, weight):
    return call(
        temporal_body,
        shape((ROWS, C), BF16),
        (pltpu.VMEM((4 * PIX, C), BF16), pltpu.VMEM((8, C), F32), pltpu.SemaphoreType.DMA),
        flops=1_500_000_000,
        ins=[VMEM] * 4 + [FAR, VMEM],
        outs=VMEM,
    )(before, h0, h1, after, in_hbm(stat), weight)


def whole_grad(part_ref, h_ref, stat_ref, sums, base, f):
    mean, scale = stat_ref[0:1, :], stat_ref[1:2, :]
    hat = (h_ref[pl.ds(base, STEP), :].astype(F32) - mean) * scale
    return part_ref[pl.ds(base + f * PIX, STEP), :] - scale * (sums[0] + hat * sums[1])


def hidden_grad_body(
    count, sums_ref, stat_ref, part_ref, h0_ref, h1_ref,
    keep_ref, give_ref, far_total_ref, total_ref, sem,
):
    sums = clip_stats(sums_ref, count)
    total_ref[...] = jnp.concatenate([*sums, jnp.zeros((6, C), F32)])
    send = pltpu.make_async_copy(total_ref, far_total_ref, sem)
    send.start()
    core = lax.axis_index("c")
    for f, h_ref in enumerate((h0_ref, h1_ref)):

        def step_body(step, carry, f=f, h_ref=h_ref):
            base = pl.multiple_of(step * STEP, STEP)
            here = pl.ds(base + f * PIX, STEP)
            grad = whole_grad(part_ref, h_ref, stat_ref, sums, base, f)
            left, right = grad[:, 0:HALF], grad[:, HALF:C]
            keep_ref[here, :] = jnp.where(core == 0, left, right).astype(BF16)
            give_ref[here, :] = jnp.where(core == 0, right, left).astype(BF16)
            return carry

        lax.fori_loop(0, PIX // STEP, step_body, 0)
    send.wait()


def hidden_gradient(sums, stat, part, h0, h1, count):
    return call(
        functools.partial(hidden_grad_body, count),
        (shape((ROWS, HALF), BF16), shape((ROWS, HALF), BF16), far((8, C), F32)),
        (pltpu.VMEM((8, C), F32), pltpu.SemaphoreType.DMA),
        ins=[VMEM] * 5,
        outs=(VMEM, VMEM, FAR),
    )(sums, stat, part, h0, h1)


def row_taps(value):
    none = jnp.zeros((W, value.shape[1]), value.dtype)
    return (
        jnp.concatenate([value[W:], none]),
        value,
        jnp.concatenate([none, value[: PIX - W]]),
    )


def weight_grad_body(
    mine_turned_ref, other_turned_ref, mine_ref, other_ref, keep_ref, got_ref, far_ref, rhs, out, sem
):
    for n, ref in enumerate((mine_ref, other_ref)):
        for f in range(2):
            where = slice(f * PIX, (f + 1) * PIX)
            for i, tap in enumerate(row_taps(ref[where, :])):
                rhs[n, where, i * HALF : (i + 1) * HALF] = tap
    sends = []
    for j in range(3):
        here = slice(j * C, (j + 1) * C)
        total = jnp.dot(mine_turned_ref[here, :], rhs[0], preferred_element_type=F32)
        total = total + jnp.dot(other_turned_ref[here, :], rhs[1], preferred_element_type=F32)
        out[here, 0 : 3 * HALF] = total.astype(BF16)
        kept = keep_ref[here, 0:HALF] + got_ref[here, 0:HALF]
        out[here, 3 * HALF : 4 * HALF] = kept.astype(BF16)
        if j == 2:
            out[3 * C :, :] = jnp.zeros((1024 - 3 * C, 4 * HALF), BF16)
            here = slice(j * C, 1024)
        send = pltpu.make_async_copy(out.at[here, :], far_ref.at[here, :], sem.at[j])
        send.start()
        sends.append(send)
    for send in sends:
        send.wait()


def weight_gradients(mine_turned, other_turned, mine, other, keep, got):
    return call(
        weight_grad_body,
        far((1024, 4 * HALF), BF16),
        (
            pltpu.VMEM((2, ROWS, 3 * HALF), BF16),
            pltpu.VMEM((1024, 4 * HALF), BF16),
            pltpu.SemaphoreType.DMA((3,)),
        ),
        flops=2_500_000_000,
        ins=[VMEM] * 6,
        outs=FAR,
    )(mine_turned, other_turned, mine, other, keep, got)


def input_grad_body(
    part_ref, h0_ref, h1_ref, far_clip_ref, far_total_ref, x_ref, far_stat_ref, far_w_ref,
    out_ref, wb, rows, z, dh, grads, lows, clip_ref, total_ref, stat_ref, w_ref, sem,
):
    pairs = (far_clip_ref, clip_ref), (far_total_ref, total_ref), (far_stat_ref, stat_ref)
    fetches = [
        pltpu.make_async_copy(one, two, sem.at[n])
        for n, (one, two) in enumerate((*pairs, (far_w_ref, w_ref)))
    ]
    for fetch in fetches:
        fetch.start()
    for fetch in fetches[:3]:
        fetch.wait()
    clip_sums = total_ref[0:1, :], total_ref[1:2, :]
    gain = stat_ref[4:5, :]
    edge = column(C)
    half = PIX // STEP
    for f in range(2):
        mean, scale = stat_ref[2 * f : 2 * f + 1, :], stat_ref[2 * f + 1 : 2 * f + 2, :]
        h_ref = (h0_ref, h1_ref)[f]

        def grad_body(step, carry, f=f, h_ref=h_ref):
            base = pl.multiple_of(step * STEP, STEP)
            grad = whole_grad(part_ref, h_ref, clip_ref, clip_sums, base, f)
            grads[pl.ds(base, STEP), :] = grad
            lows[pl.ds(base, STEP), :] = grad.astype(BF16)
            return carry

        lax.fori_loop(0, half, grad_body, 0)
        if f == 0:
            fetches[3].wait()
            for j in range(3):
                for i in range(3):
                    wb[PAD * j : PAD * j + C, C * i : C * (i + 1)] = w_ref[3 * i + j]
                wb[PAD * j + C : PAD * (j + 1), :] = jnp.zeros((PAD - C, 3 * C), BF16)
        for i, tap in enumerate(row_taps(lows[...])):
            rows[:, i * C : (i + 1) * C] = tap
        z[...] = times_transposed(rows[...], wb[...])

        def step_body(step, carry, f=f, mean=mean, scale=scale):
            base = pl.multiple_of(step * STEP, STEP)
            here = pl.ds(base, STEP)
            right = jnp.where(edge == W - 1, 0.0, pltpu.roll(z[here, 0:C], STEP - 1, 0))
            left = jnp.where(edge == 0, 0.0, pltpu.roll(z[here, 2 * PAD : 2 * PAD + C], 1, 0))
            acts_grad = right + z[here, PAD : PAD + C] + left
            hat = (x_ref[pl.ds(base + f * PIX, STEP), :].astype(F32) - mean) * scale
            pre = hat * gain
            s = sigmoid(pre)
            dhat = acts_grad * (s * (1.0 + pre * (1.0 - s))) * gain
            dh[here, :] = dhat
            return carry[0] + fold(dhat), carry[1] + fold(dhat * hat)

        zero = jnp.zeros((8, C), F32)
        sums = lax.fori_loop(0, half, step_body, (zero, zero))
        grouped = group_sum(four(*sums)) * (1.0 / (PIX * C // GROUPS))
        first, second = grouped[0:1], grouped[1:2]

        def last_body(step, carry, f=f, mean=mean, scale=scale, first=first, second=second):
            base = pl.multiple_of(step * STEP, STEP)
            there = pl.ds(base + f * PIX, STEP)
            hat = (x_ref[there, :].astype(F32) - mean) * scale
            here = pl.ds(base, STEP)
            value = grads[here, :] + scale * (dh[here, :] - first - hat * second)
            out_ref[there, :] = value.astype(BF16)
            return carry

        lax.fori_loop(0, half, last_body, 0)


def input_gradient(part, h0, h1, clip_stat, total, x, stat, weight):
    return call(
        input_grad_body,
        shape((ROWS, C), BF16),
        (
            pltpu.VMEM((3 * PAD, 3 * C), BF16),
            pltpu.VMEM((PIX, 3 * C), BF16),
            pltpu.VMEM((PIX, 3 * PAD), F32),
            pltpu.VMEM((PIX, C), F32),
            pltpu.VMEM((PIX, C), F32),
            pltpu.VMEM((PIX, C), BF16),
            pltpu.VMEM((8, C), F32),
            pltpu.VMEM((8, C), F32),
            pltpu.VMEM((8, C), F32),
            pltpu.VMEM((9, C, C), BF16),
            pltpu.SemaphoreType.DMA((4,)),
        ),
        flops=2_500_000_000,
        limit=18,
        ins=[VMEM] * 3 + [FAR] * 2 + [VMEM] + [FAR] * 2,
        outs=VMEM,
    )(part, h0, h1, in_hbm(clip_stat), in_hbm(total), x, in_hbm(stat), in_hbm(weight))


def unpack_body(mine_ref, other_ref, far_spatial_ref, far_temporal_ref, taps, sem):
    core = lax.axis_index("c")
    sends = []
    for j in range(3):
        here = slice(j * C, (j + 1) * C)
        mine, other = mine_ref[here, :], other_ref[here, :]
        left = jnp.where(core == 0, mine, other)
        right = jnp.where(core == 0, other, mine)
        for i in range(4):
            n = 3 * i + j
            lanes = slice(i * HALF, (i + 1) * HALF)
            taps[n, :, 0:HALF] = left[:, lanes]
            taps[n, :, HALF:C] = right[:, lanes]
            target = far_spatial_ref.at[n] if i < 3 else far_temporal_ref.at[j]
            send = pltpu.make_async_copy(taps.at[n], target, sem.at[n])
            send.start()
            sends.append(send)
    for send in sends:
        send.wait()


def unpack(mine, other):
    return call(
        unpack_body,
        (far((9, C, C), BF16), far((3, C, C), BF16)),
        (pltpu.VMEM((12, C, C), BF16), pltpu.SemaphoreType.DMA((12,))),
        ins=[VMEM] * 2,
        outs=(FAR, FAR),
    )(mine, other)


def frames_body(value_ref, first_ref, second_ref, sem):
    copies = [
        pltpu.make_async_copy(value_ref.at[0:PIX, :], first_ref, sem.at[0]),
        pltpu.make_async_copy(value_ref.at[PIX:ROWS, :], second_ref, sem.at[1]),
    ]
    for copy in copies:
        copy.start()
    for copy in copies:
        copy.wait()


def frames(value):
    return call(
        frames_body,
        (shape((PIX, C), BF16), shape((PIX, C), BF16)),
        (pltpu.SemaphoreType.DMA((2,)),),
        limit=2,
        ins=[FAR],
        outs=(VMEM, VMEM),
    )(in_hbm(value))


def neighbours(first, second):
    size = lax.axis_size(FRAME)
    before = lax.ppermute(second, FRAME, [(i, i + 1) for i in range(size - 1)])
    after = lax.ppermute(first, FRAME, [(i + 1, i) for i in range(size - 1)])
    return before, after


def swap_cores(value):
    return lax.ppermute(value, "c", [(0, 1), (1, 0)])


def everyone_total(value):
    plane = lax.axis_size(PLANE)
    value = value.reshape(plane, 1024 // plane, value.shape[1])
    return lax.all_to_all(value, PLANE, 0, 0)


def everyone_share(value):
    value = jnp.sum(value.astype(F32), axis=0)
    return lax.psum(value, LINE).astype(BF16)


def everyone_gets(value):
    plane = lax.axis_size(PLANE)
    value = jnp.broadcast_to(value[None], (plane,) + value.shape)
    return lax.all_to_all(value, PLANE, 0, 0).reshape(1024, value.shape[2])


def on_device(clips, cotangent, spatial_weight, temporal_weight, gain_one, gain_two):
    size = lax.axis_size(FRAME)
    count = float(size * ROWS * C // GROUPS)
    x = clips.reshape(ROWS, C)
    cot = cotangent.reshape(ROWS, C)
    spatial_weight = spatial_weight.reshape(9, C, C)
    barrier = lax.optimization_barrier
    cot_before, cot_after = neighbours(*frames(cot))
    h0, h1, mine_turned, stat_one, sums = forward(x, spatial_weight, gain_one, size)
    sums = lax.all_to_all(sums, FRAME, 0, 0)
    mixed_grad = mixed_gradient(cot_before, cot, cot_after, temporal_weight)
    sums, mine_turned, mixed_grad = barrier((sums, mine_turned, mixed_grad))
    other_turned = swap_cores(mine_turned)
    part, clip_stat, sums, far_stat = slopes(sums, h0, h1, mixed_grad, cot, gain_two, count)
    sums = lax.all_to_all(sums, FRAME, 0, 0)
    temporal_keep, temporal_give = temporal_gradient(
        h0, h1, cot_before, cot, cot_after, clip_stat, sums
    )
    temporal_got = swap_cores(temporal_give)
    low_keep, low_give, total = hidden_gradient(sums, clip_stat, part, h0, h1, count)
    low_got = swap_cores(low_give)
    packed = weight_gradients(
        mine_turned, other_turned, low_keep, low_got, temporal_keep, temporal_got
    )
    packed, total, edge0, edge1 = barrier((packed, total, h0, h1))
    shares = everyone_total(packed)
    before, after = neighbours(edge0, edge1)
    input_grad = input_gradient(
        part, h0, h1, far_stat, total, x, stat_one, spatial_weight
    )
    shares, input_grad = barrier((shares, input_grad))
    mine = everyone_share(shares)
    mine, before, after = barrier((mine, before, after))
    output = temporal(before, h0, h1, after, far_stat, temporal_weight)
    mine, output = barrier((everyone_gets(mine), output))
    other = swap_cores(mine)
    spatial_grad, temporal_grad = unpack(mine, other)
    return (
        output.reshape(clips.shape),
        input_grad.reshape(clips.shape),
        spatial_grad.reshape(3, 3, C, C),
        temporal_grad,
    )


def solution(mesh):
    fine = Mesh(mesh.devices.reshape(2, 4, 2, 4, 4), ("zl", "x", "c", "y", "zh"))
    return jax.shard_map(
        on_device,
        mesh=fine,
        in_specs=(P(DP, FRAME), P(DP, FRAME), P(), P(), P(), P()),
        out_specs=(P(DP, FRAME), P(DP, FRAME), P(), P()),
        check_vma=False,
    )
```

```python
import functools

import jax
import jax.numpy as jnp
from jax import lax
from jax.experimental import pallas as pl
from jax.experimental.pallas import tpu as pltpu
from jax.sharding import Mesh, PartitionSpec as P

epsilon = 1e-05

GROUPS = 32
DP = ("zl", "x", "c")
FRAME = ("y", "zh")
PLANE = ("x", "y")
LINE = ("zl", "zh")

C = 320
W = 32
PAD = 384
HALF = C // 2
PIX = 512
ROWS = 2 * PIX
STEP = 128
F32 = jnp.float32
BF16 = jnp.bfloat16

MIB = 1024 * 1024


VMEM = pl.BlockSpec(memory_space=pltpu.VMEM)
FAR = pl.BlockSpec(memory_space=pltpu.HBM)


def call(body, out, scratch=(), flops=0, limit=12, ins=None, outs=None):
    specs = {}
    if ins is not None:
        specs = {"in_specs": ins, "out_specs": outs}
    return pl.pallas_call(
        body,
        out_shape=out,
        scratch_shapes=list(scratch),
        compiler_params=pltpu.CompilerParams(vmem_limit_bytes=limit * MIB),
        cost_estimate=pl.CostEstimate(flops=flops, transcendentals=0, bytes_accessed=8_000_000),
        **specs,
    )


def shape(dims, kind):
    return jax.ShapeDtypeStruct(dims, kind)


def far(dims, kind):
    return pltpu.HBM(dims, kind)


def in_hbm(value):
    return pltpu.with_memory_space_constraint(value, pltpu.HBM)


def at(step, size=STEP):
    return pl.ds(pl.multiple_of(step * size, size), size)


def group_sum(rows):
    per = C // GROUPS
    one = lax.broadcasted_iota(jnp.int32, (C, C), 0) * 6554 >> 16
    two = lax.broadcasted_iota(jnp.int32, (C, C), 1) * 6554 >> 16
    assert per == 10
    same = jnp.where(one == two, 1.0, 0.0).astype(F32)
    return jnp.dot(rows, same, precision=lax.Precision.HIGHEST, preferred_element_type=F32)


def fold(value):
    return jnp.sum(value.reshape(value.shape[0] // 8, 8, value.shape[1]), axis=0)


def column(width):
    return lax.broadcasted_iota(jnp.int32, (STEP, width), 0) & (W - 1)


def four(*sums):
    return jnp.concatenate([jnp.sum(s, axis=0, keepdims=True) for s in sums] + [jnp.zeros((8 - len(sums), C), F32)])


def sigmoid(value):
    return 1.0 / (1.0 + jnp.exp(-value))


def forward_body(
    x_ref, far_w_ref, gain_ref, h0_ref, h1_ref, far_turned_ref, far_stat_ref, sums_ref,
    w_ref, wf, x3, y, turned, stat_ref, w_sem, turned_sem, stat_sem,
):
    fetch = pltpu.make_async_copy(far_w_ref, w_ref, w_sem)
    fetch.start()
    zero = jnp.zeros((8, C), F32)

    def moments(step, carry):
        value = x_ref[at(step), :].astype(F32)
        return carry[0] + fold(value), carry[1] + fold(value * value)

    half = PIX // STEP
    s0, q0 = lax.fori_loop(0, half, moments, (zero, zero))
    s1, q1 = lax.fori_loop(half, 2 * half, moments, (zero, zero))
    grouped = group_sum(four(s0, q0, s1, q1)) * (1.0 / (PIX * C // GROUPS))
    stats = []
    for f in range(2):
        mean = grouped[2 * f : 2 * f + 1]
        var = grouped[2 * f + 1 : 2 * f + 2] - mean * mean
        stats += [mean, lax.rsqrt(var + epsilon)]
    gain = gain_ref[...].reshape(1, C)
    stat_ref[...] = jnp.concatenate([*stats, gain, jnp.zeros((3, C), F32)])
    sends = [pltpu.make_async_copy(stat_ref, far_stat_ref, stat_sem)]
    sends[0].start()
    edge = column(C)

    def activate(step, mean, scale):
        value = x_ref[at(step), :].astype(F32)
        pre = (value - mean) * scale * gain
        act = pre / (1.0 + jnp.exp(-pre))
        low = act.astype(BF16)
        act = low.astype(F32)
        x3[at(step), 0:C] = jnp.where(edge == 0, 0.0, pltpu.roll(act, 1, 0)).astype(BF16)
        x3[at(step), C : 2 * C] = low
        x3[at(step), 2 * C : 3 * C] = jnp.where(
            edge == W - 1, 0.0, pltpu.roll(act, STEP - 1, 0)
        ).astype(BF16)

    def act_step(step, carry):
        activate(step, stats[0], stats[1])
        return carry

    lax.fori_loop(0, half, act_step, 0)
    fetch.wait()
    for i in range(3):
        for j in range(3):
            wf[C * j : C * (j + 1), PAD * i : PAD * i + C] = w_ref[3 * i + j]

    def product(f):
        y[f, 0:W, :] = jnp.zeros((W, 3 * PAD), F32)
        y[f, W + PIX : 2 * W + PIX, :] = jnp.zeros((W, 3 * PAD), F32)
        y[f, W : W + PIX, :] = jnp.dot(
            x3[f * PIX : (f + 1) * PIX, :], wf[...], preferred_element_type=F32
        )

    def turn_frame(f):
        turn(x3[f * PIX : (f + 1) * PIX, C : 2 * C], turned.at[f])
        send = pltpu.make_async_copy(
            turned.at[f], far_turned_ref.at[:, f * PIX : (f + 1) * PIX], turned_sem.at[f]
        )
        send.start()
        sends.append(send)

    def finish(f, h_ref, base, carry):
        conv = (
            y[f, pl.ds(base, STEP), 0:C]
            + y[f, pl.ds(base + W, STEP), PAD : PAD + C]
            + y[f, pl.ds(base + 2 * W, STEP), 2 * PAD : 2 * PAD + C]
        )
        value = x_ref[pl.ds(base + f * PIX, STEP), :].astype(F32)
        low = (value + conv).astype(BF16)
        h_ref[pl.ds(base, STEP), :] = low
        value = low.astype(F32)
        return carry[0] + fold(value), carry[1] + fold(value * value)

    product(0)
    for step in range(half, 2 * half):
        activate(step, stats[2], stats[3])
    turn_frame(0)
    product(1)
    total = (zero, zero)
    for step in range(half):
        total = finish(0, h0_ref, step * STEP, total)
    turn_frame(1)

    def last_step(step, carry):
        return finish(1, h1_ref, pl.multiple_of(step * STEP, STEP), carry)

    total = lax.fori_loop(0, half, last_step, total)
    spread(total, sums_ref)
    for send in sends:
        send.wait()


def spread(total, sums_ref):
    first = jnp.sum(total[0], axis=0, keepdims=True)
    second = jnp.sum(total[1], axis=0, keepdims=True)
    both = jnp.concatenate([first, second])
    for k in range(sums_ref.shape[0]):
        sums_ref[k] = both


def turn(acts, out_ref):
    rows = lax.broadcasted_iota(jnp.int32, (C, C), 0)
    same = jnp.where(rows == lax.broadcasted_iota(jnp.int32, (C, C), 1), 1.0, 0.0).astype(BF16)
    lane = lax.broadcasted_iota(jnp.int32, (C, STEP), 1) & (W - 1)
    moved = times_transposed(same, acts)
    for step in range(PIX // STEP):
        part = moved[:, step * STEP : (step + 1) * STEP]
        where = slice(step * STEP, (step + 1) * STEP)
        out_ref[0:C, where] = jnp.where(lane == 0, 0.0, pltpu.roll(part, 1, 1)).astype(BF16)
        out_ref[C : 2 * C, where] = part.astype(BF16)
        out_ref[2 * C : 3 * C, where] = jnp.where(
            lane == W - 1, 0.0, pltpu.roll(part, STEP - 1, 1)
        ).astype(BF16)


def forward(x, weight, gain, peers):
    return call(
        forward_body,
        (
            shape((PIX, C), BF16),
            shape((PIX, C), BF16),
            far((3 * C, ROWS), BF16),
            far((8, C), F32),
            shape((peers, 2, C), F32),
        ),
        (
            pltpu.VMEM((9, C, C), BF16),
            pltpu.VMEM((3 * C, 3 * PAD), BF16),
            pltpu.VMEM((ROWS, 3 * C), BF16),
            pltpu.VMEM((2, PIX + 2 * W, 3 * PAD), F32),
            pltpu.VMEM((2, 3 * C, PIX), BF16),
            pltpu.VMEM((8, C), F32),
            pltpu.SemaphoreType.DMA,
            pltpu.SemaphoreType.DMA((2,)),
            pltpu.SemaphoreType.DMA,
        ),
        flops=2_500_000_000,
        limit=24,
        ins=[VMEM, FAR, VMEM],
        outs=(VMEM, VMEM, FAR, FAR, VMEM),
    )(x, in_hbm(weight), gain)


def times_transposed(a, b):
    return lax.dot_general(a, b, (((1,), (1,)), ((), ())), preferred_element_type=F32)


def clip_stats(sums_ref, count):
    total = jnp.sum(sums_ref[...], axis=0)
    grouped = group_sum(jnp.concatenate([total, jnp.zeros((6, C), F32)])) * (1.0 / count)
    return grouped[0:1], grouped[1:2]


def mixed_grad_body(before_ref, cot_ref, after_ref, w_ref, far_ref, out_ref, sem):
    sends = []
    for f in range(2):
        here = slice(f * PIX, (f + 1) * PIX)
        last = cot_ref[0:PIX, :] if f else before_ref[...]
        later = after_ref[...] if f else cot_ref[PIX:ROWS, :]
        total = times_transposed(later, w_ref[0])
        total = total + times_transposed(cot_ref[here, :], w_ref[1])
        total = total + times_transposed(last, w_ref[2])
        out_ref[here, :] = total.astype(BF16)
        send = pltpu.make_async_copy(out_ref.at[here, :], far_ref.at[here, :], sem.at[f])
        send.start()
        sends.append(send)
    for send in sends:
        send.wait()


def mixed_gradient(before, cot, after, weight):
    return call(
        mixed_grad_body,
        far((ROWS, C), BF16),
        (pltpu.VMEM((ROWS, C), BF16), pltpu.SemaphoreType.DMA((2,))),
        flops=1_500_000_000,
        ins=[VMEM] * 4,
        outs=FAR,
    )(before, cot, after, weight)


def slope_body(
    count, sums_ref, h0_ref, h1_ref, far_grad_ref, cot_ref, gain_ref,
    part_ref, stat_ref, out_ref, far_stat_ref, grad_ref, sem, grad_sem,
):
    fetch = pltpu.make_async_copy(far_grad_ref, grad_ref, grad_sem)
    fetch.start()
    mean, square = clip_stats(sums_ref, count)
    scale = lax.rsqrt(square - mean * mean + epsilon)
    gain = gain_ref[...].reshape(1, C)
    stat_ref[...] = jnp.concatenate([mean, scale, gain, jnp.zeros((5, C), F32)])
    send = pltpu.make_async_copy(stat_ref, far_stat_ref, sem)
    send.start()
    fetch.wait()
    zero = jnp.zeros((8, C), F32)
    total = (zero, zero)
    for f, h_ref in enumerate((h0_ref, h1_ref)):

        def step_body(step, carry, f=f, h_ref=h_ref):
            base = pl.multiple_of(step * STEP, STEP)
            there = pl.ds(base + f * PIX, STEP)
            hat = (h_ref[pl.ds(base, STEP), :].astype(F32) - mean) * scale
            pre = hat * gain
            s = sigmoid(pre)
            slope = s * (1.0 + pre * (1.0 - s))
            dhat = grad_ref[there, :].astype(F32) * slope * gain
            part_ref[there, :] = cot_ref[there, :].astype(F32) + scale * dhat
            return carry[0] + fold(dhat), carry[1] + fold(dhat * hat)

        total = lax.fori_loop(0, PIX // STEP, step_body, total)
    spread(total, out_ref)
    send.wait()


def slopes(sums, h0, h1, grad, cot, gain, count):
    return call(
        functools.partial(slope_body, count),
        (shape((ROWS, C), F32), shape((8, C), F32), shape(sums.shape, F32), far((8, C), F32)),
        (pltpu.VMEM((ROWS, C), BF16), pltpu.SemaphoreType.DMA, pltpu.SemaphoreType.DMA),
        ins=[VMEM] * 3 + [FAR] + [VMEM] * 2,
        outs=(VMEM, VMEM, VMEM, FAR),
    )(sums, h0, h1, in_hbm(grad), cot, gain)


def mix(h_ref, base, mean, scale, gain):
    pre = (h_ref[pl.ds(base, STEP), :].astype(F32) - mean) * scale * gain
    return pre / (1.0 + jnp.exp(-pre))


def mixed_body(
    h0_ref, h1_ref, before_ref, cot_ref, after_ref, stat_ref, sums_ref,
    keep_ref, give_ref, turned,
):
    mean, scale, gain = stat_ref[0:1, :], stat_ref[1:2, :], stat_ref[2:3, :]
    for f, h_ref in enumerate((h0_ref, h1_ref)):
        for step in range(PIX // STEP):
            act = mix(h_ref, step * STEP, mean, scale, gain).astype(BF16)
            turned[:, f * PIX + step * STEP : f * PIX + (step + 1) * STEP] = act.T
    core = lax.axis_index("c")
    first, second = turned[:, 0:PIX], turned[:, PIX:ROWS]
    for k in range(3):
        if k == 1:
            part = jnp.dot(turned[...], cot_ref[...], preferred_element_type=F32)
        else:
            one = cot_ref[PIX:ROWS, :] if k == 0 else before_ref[...]
            two = after_ref[...] if k == 0 else cot_ref[0:PIX, :]
            part = jnp.dot(first, one, preferred_element_type=F32)
            part = part + jnp.dot(second, two, preferred_element_type=F32)
        left, right = part[:, 0:HALF], part[:, HALF:C]
        keep_ref[k * C : (k + 1) * C, 0:HALF] = jnp.where(core == 0, left, right)
        give_ref[k * C : (k + 1) * C, 0:HALF] = jnp.where(core == 0, right, left)


def temporal_gradient(h0, h1, before, cot, after, stat, sums):
    return call(
        mixed_body,
        (shape((3 * C, 256), F32), shape((3 * C, 256), F32)),
        (pltpu.VMEM((C, ROWS), BF16),),
        flops=1_500_000_000,
    )(h0, h1, before, cot, after, stat, sums)


def temporal_body(
    hb_ref, h0_ref, h1_ref, ha_ref, far_stat_ref, w_ref, out_ref, mx_ref, stat_ref, sem
):
    fetch = pltpu.make_async_copy(far_stat_ref, stat_ref, sem)
    fetch.start()
    fetch.wait()
    mean, scale, gain = stat_ref[0:1, :], stat_ref[1:2, :], stat_ref[2:3, :]
    place = lax.axis_index(FRAME)
    live = (place > 0, None, None, place < lax.axis_size(FRAME) - 1)
    for n, h_ref in enumerate((hb_ref, h0_ref, h1_ref, ha_ref)):

        def step_body(step, carry, n=n, h_ref=h_ref):
            base = pl.multiple_of(step * STEP, STEP)
            act = mix(h_ref, base, mean, scale, gain)
            if live[n] is not None:
                act = jnp.where(live[n], act, 0.0)
            mx_ref[pl.ds(base + n * PIX, STEP), :] = act.astype(BF16)
            return carry

        lax.fori_loop(0, PIX // STEP, step_body, 0)
    for f, h_ref in enumerate((h0_ref, h1_ref)):
        total = None
        for k in range(3):
            part = jnp.dot(
                mx_ref[(f + k) * PIX : (f + k + 1) * PIX, :],
                w_ref[k],
                preferred_element_type=F32,
            )
            total = part if total is None else total + part
        low = total.astype(BF16).astype(F32)
        out_ref[f * PIX : (f + 1) * PIX, :] = (h_ref[...].astype(F32) + low).astype(BF16)


def temporal(before, h0, h1, after, stat, weight):
    return call(
        temporal_body,
        shape((ROWS, C), BF16),
        (pltpu.VMEM((4 * PIX, C), BF16), pltpu.VMEM((8, C), F32), pltpu.SemaphoreType.DMA),
        flops=1_500_000_000,
        ins=[VMEM] * 4 + [FAR, VMEM],
        outs=VMEM,
    )(before, h0, h1, after, in_hbm(stat), weight)


def whole_grad(part_ref, h_ref, stat_ref, sums, base, f):
    mean, scale = stat_ref[0:1, :], stat_ref[1:2, :]
    hat = (h_ref[pl.ds(base, STEP), :].astype(F32) - mean) * scale
    return part_ref[pl.ds(base + f * PIX, STEP), :] - scale * (sums[0] + hat * sums[1])


def hidden_grad_body(
    count, sums_ref, stat_ref, part_ref, h0_ref, h1_ref,
    keep_ref, give_ref, far_total_ref, total_ref, sem,
):
    sums = clip_stats(sums_ref, count)
    total_ref[...] = jnp.concatenate([*sums, jnp.zeros((6, C), F32)])
    send = pltpu.make_async_copy(total_ref, far_total_ref, sem)
    send.start()
    core = lax.axis_index("c")
    for f, h_ref in enumerate((h0_ref, h1_ref)):

        def step_body(step, carry, f=f, h_ref=h_ref):
            base = pl.multiple_of(step * STEP, STEP)
            here = pl.ds(base + f * PIX, STEP)
            grad = whole_grad(part_ref, h_ref, stat_ref, sums, base, f)
            left, right = grad[:, 0:HALF], grad[:, HALF:C]
            keep_ref[here, :] = jnp.where(core == 0, left, right).astype(BF16)
            give_ref[here, :] = jnp.where(core == 0, right, left).astype(BF16)
            return carry

        lax.fori_loop(0, PIX // STEP, step_body, 0)
    send.wait()


def hidden_gradient(sums, stat, part, h0, h1, count):
    return call(
        functools.partial(hidden_grad_body, count),
        (shape((ROWS, HALF), BF16), shape((ROWS, HALF), BF16), far((8, C), F32)),
        (pltpu.VMEM((8, C), F32), pltpu.SemaphoreType.DMA),
        ins=[VMEM] * 5,
        outs=(VMEM, VMEM, FAR),
    )(sums, stat, part, h0, h1)


def row_taps(value):
    none = jnp.zeros((W, value.shape[1]), value.dtype)
    return (
        jnp.concatenate([value[W:], none]),
        value,
        jnp.concatenate([none, value[: PIX - W]]),
    )


def weight_grad_body(
    mine_turned_ref, other_turned_ref, mine_ref, other_ref, keep_ref, got_ref, far_ref, rhs, out, sem
):
    for n, ref in enumerate((mine_ref, other_ref)):
        for f in range(2):
            where = slice(f * PIX, (f + 1) * PIX)
            for i, tap in enumerate(row_taps(ref[where, :])):
                rhs[n, where, i * HALF : (i + 1) * HALF] = tap
    sends = []
    for j in range(3):
        here = slice(j * C, (j + 1) * C)
        total = jnp.dot(mine_turned_ref[here, :], rhs[0], preferred_element_type=F32)
        total = total + jnp.dot(other_turned_ref[here, :], rhs[1], preferred_element_type=F32)
        out[here, 0 : 3 * HALF] = total.astype(BF16)
        kept = keep_ref[here, 0:HALF] + got_ref[here, 0:HALF]
        out[here, 3 * HALF : 4 * HALF] = kept.astype(BF16)
        if j == 2:
            out[3 * C :, :] = jnp.zeros((1024 - 3 * C, 4 * HALF), BF16)
            here = slice(j * C, 1024)
        send = pltpu.make_async_copy(out.at[here, :], far_ref.at[here, :], sem.at[j])
        send.start()
        sends.append(send)
    for send in sends:
        send.wait()


def weight_gradients(mine_turned, other_turned, mine, other, keep, got):
    return call(
        weight_grad_body,
        far((1024, 4 * HALF), BF16),
        (
            pltpu.VMEM((2, ROWS, 3 * HALF), BF16),
            pltpu.VMEM((1024, 4 * HALF), BF16),
            pltpu.SemaphoreType.DMA((3,)),
        ),
        flops=2_500_000_000,
        ins=[VMEM] * 6,
        outs=FAR,
    )(mine_turned, other_turned, mine, other, keep, got)


def input_grad_body(
    part_ref, h0_ref, h1_ref, far_clip_ref, far_total_ref, x_ref, far_stat_ref, far_w_ref,
    out_ref, wb, rows, z, dh, grads, lows, clip_ref, total_ref, stat_ref, w_ref, sem,
):
    pairs = (far_clip_ref, clip_ref), (far_total_ref, total_ref), (far_stat_ref, stat_ref)
    fetches = [
        pltpu.make_async_copy(one, two, sem.at[n])
        for n, (one, two) in enumerate((*pairs, (far_w_ref, w_ref)))
    ]
    for fetch in fetches:
        fetch.start()
    for fetch in fetches[:3]:
        fetch.wait()
    clip_sums = total_ref[0:1, :], total_ref[1:2, :]
    gain = stat_ref[4:5, :]
    edge = column(C)
    half = PIX // STEP
    for f in range(2):
        mean, scale = stat_ref[2 * f : 2 * f + 1, :], stat_ref[2 * f + 1 : 2 * f + 2, :]
        h_ref = (h0_ref, h1_ref)[f]

        def grad_body(step, carry, f=f, h_ref=h_ref):
            base = pl.multiple_of(step * STEP, STEP)
            grad = whole_grad(part_ref, h_ref, clip_ref, clip_sums, base, f)
            grads[pl.ds(base, STEP), :] = grad
            lows[pl.ds(base, STEP), :] = grad.astype(BF16)
            return carry

        lax.fori_loop(0, half, grad_body, 0)
        if f == 0:
            fetches[3].wait()
            for j in range(3):
                for i in range(3):
                    wb[PAD * j : PAD * j + C, C * i : C * (i + 1)] = w_ref[3 * i + j]
                wb[PAD * j + C : PAD * (j + 1), :] = jnp.zeros((PAD - C, 3 * C), BF16)
        for i, tap in enumerate(row_taps(lows[...])):
            rows[:, i * C : (i + 1) * C] = tap
        z[...] = times_transposed(rows[...], wb[...])

        def step_body(step, carry, f=f, mean=mean, scale=scale):
            base = pl.multiple_of(step * STEP, STEP)
            here = pl.ds(base, STEP)
            right = jnp.where(edge == W - 1, 0.0, pltpu.roll(z[here, 0:C], STEP - 1, 0))
            left = jnp.where(edge == 0, 0.0, pltpu.roll(z[here, 2 * PAD : 2 * PAD + C], 1, 0))
            acts_grad = right + z[here, PAD : PAD + C] + left
            hat = (x_ref[pl.ds(base + f * PIX, STEP), :].astype(F32) - mean) * scale
            pre = hat * gain
            s = sigmoid(pre)
            dhat = acts_grad * (s * (1.0 + pre * (1.0 - s))) * gain
            dh[here, :] = dhat
            return carry[0] + fold(dhat), carry[1] + fold(dhat * hat)

        zero = jnp.zeros((8, C), F32)
        sums = lax.fori_loop(0, half, step_body, (zero, zero))
        grouped = group_sum(four(*sums)) * (1.0 / (PIX * C // GROUPS))
        first, second = grouped[0:1], grouped[1:2]

        def last_body(step, carry, f=f, mean=mean, scale=scale, first=first, second=second):
            base = pl.multiple_of(step * STEP, STEP)
            there = pl.ds(base + f * PIX, STEP)
            hat = (x_ref[there, :].astype(F32) - mean) * scale
            here = pl.ds(base, STEP)
            value = grads[here, :] + scale * (dh[here, :] - first - hat * second)
            out_ref[there, :] = value.astype(BF16)
            return carry

        lax.fori_loop(0, half, last_body, 0)


def input_gradient(part, h0, h1, clip_stat, total, x, stat, weight):
    return call(
        input_grad_body,
        shape((ROWS, C), BF16),
        (
            pltpu.VMEM((3 * PAD, 3 * C), BF16),
            pltpu.VMEM((PIX, 3 * C), BF16),
            pltpu.VMEM((PIX, 3 * PAD), F32),
            pltpu.VMEM((PIX, C), F32),
            pltpu.VMEM((PIX, C), F32),
            pltpu.VMEM((PIX, C), BF16),
            pltpu.VMEM((8, C), F32),
            pltpu.VMEM((8, C), F32),
            pltpu.VMEM((8, C), F32),
            pltpu.VMEM((9, C, C), BF16),
            pltpu.SemaphoreType.DMA((4,)),
        ),
        flops=2_500_000_000,
        limit=18,
        ins=[VMEM] * 3 + [FAR] * 2 + [VMEM] + [FAR] * 2,
        outs=VMEM,
    )(part, h0, h1, in_hbm(clip_stat), in_hbm(total), x, in_hbm(stat), in_hbm(weight))


def unpack_body(mine_ref, other_ref, far_spatial_ref, far_temporal_ref, taps, sem):
    core = lax.axis_index("c")
    sends = []
    for j in range(3):
        here = slice(j * C, (j + 1) * C)
        mine, other = mine_ref[here, :], other_ref[here, :]
        left = jnp.where(core == 0, mine, other)
        right = jnp.where(core == 0, other, mine)
        for i in range(4):
            n = 3 * i + j
            lanes = slice(i * HALF, (i + 1) * HALF)
            taps[n, :, 0:HALF] = left[:, lanes]
            taps[n, :, HALF:C] = right[:, lanes]
            target = far_spatial_ref.at[n] if i < 3 else far_temporal_ref.at[j]
            send = pltpu.make_async_copy(taps.at[n], target, sem.at[n])
            send.start()
            sends.append(send)
    for send in sends:
        send.wait()


def unpack(mine, other):
    return call(
        unpack_body,
        (far((9, C, C), BF16), far((3, C, C), BF16)),
        (pltpu.VMEM((12, C, C), BF16), pltpu.SemaphoreType.DMA((12,))),
        ins=[VMEM] * 2,
        outs=(FAR, FAR),
    )(mine, other)


def neighbours(first, second):
    size = lax.axis_size(FRAME)
    before = lax.ppermute(second, FRAME, [(i, i + 1) for i in range(size - 1)])
    after = lax.ppermute(first, FRAME, [(i + 1, i) for i in range(size - 1)])
    return before, after


def swap_cores(value):
    return lax.ppermute(value, "c", [(0, 1), (1, 0)])


def everyone_total(value):
    plane = lax.axis_size(PLANE)
    value = value.reshape(plane, 1024 // plane, value.shape[1])
    return lax.all_to_all(value, PLANE, 0, 0)


def everyone_share(value, beside):
    plane, line = lax.axis_size(PLANE), lax.axis_size(LINE)
    width = value.shape[2]
    value = jnp.sum(value.astype(F32), axis=0)
    value = value.reshape(line, 1024 // plane // line, width)
    value = jnp.sum(lax.all_to_all(value, LINE, 0, 0), axis=0).astype(BF16)
    value, *beside = lax.optimization_barrier((value, *beside))
    value = jnp.broadcast_to(value[None], (line,) + value.shape)
    return beside, lax.all_to_all(value, LINE, 0, 0).reshape(1024 // plane, width)


def everyone_gets(value):
    plane = lax.axis_size(PLANE)
    value = jnp.broadcast_to(value[None], (plane,) + value.shape)
    return lax.all_to_all(value, PLANE, 0, 0).reshape(1024, value.shape[2])


def on_device(clips, cotangent, spatial_weight, temporal_weight, gain_one, gain_two):
    size = lax.axis_size(FRAME)
    count = float(size * ROWS * C // GROUPS)
    x = clips.reshape(ROWS, C)
    cot = cotangent.reshape(ROWS, C)
    spatial_weight = spatial_weight.reshape(9, C, C)
    barrier = lax.optimization_barrier
    cot_before, cot_after = neighbours(cot[:PIX], cot[PIX:])
    h0, h1, mine_turned, stat_one, sums = forward(x, spatial_weight, gain_one, size)
    sums = lax.all_to_all(sums, FRAME, 0, 0)
    mixed_grad = mixed_gradient(cot_before, cot, cot_after, temporal_weight)
    sums, mine_turned, mixed_grad = barrier((sums, mine_turned, mixed_grad))
    other_turned = swap_cores(mine_turned)
    part, clip_stat, sums, far_stat = slopes(sums, h0, h1, mixed_grad, cot, gain_two, count)
    sums = lax.all_to_all(sums, FRAME, 0, 0)
    temporal_keep, temporal_give = temporal_gradient(
        h0, h1, cot_before, cot, cot_after, clip_stat, sums
    )
    temporal_got = swap_cores(temporal_give)
    low_keep, low_give, total = hidden_gradient(sums, clip_stat, part, h0, h1, count)
    low_got = swap_cores(low_give)
    packed = weight_gradients(
        mine_turned, other_turned, low_keep, low_got, temporal_keep, temporal_got
    )
    packed, total, edge0, edge1 = barrier((packed, total, h0, h1))
    shares = everyone_total(packed)
    before, after = neighbours(edge0, edge1)
    input_grad = input_gradient(
        part, h0, h1, far_stat, total, x, stat_one, spatial_weight
    )
    shares, input_grad = barrier((shares, input_grad))
    (before, after), mine = everyone_share(shares, (before, after))
    mine, before, after = barrier((mine, before, after))
    output = temporal(before, h0, h1, after, far_stat, temporal_weight)
    mine, output = barrier((everyone_gets(mine), output))
    other = swap_cores(mine)
    spatial_grad, temporal_grad = unpack(mine, other)
    return (
        output.reshape(clips.shape),
        input_grad.reshape(clips.shape),
        spatial_grad.reshape(3, 3, C, C),
        temporal_grad,
    )


def solution(mesh):
    fine = Mesh(mesh.devices.reshape(2, 4, 2, 4, 4), ("zl", "x", "c", "y", "zh"))
    return jax.shard_map(
        on_device,
        mesh=fine,
        in_specs=(P(DP, FRAME), P(DP, FRAME), P(), P(), P(), P()),
        out_specs=(P(DP, FRAME), P(DP, FRAME), P(), P()),
        check_vma=False,
    )
```

```python
import functools

import jax
import jax.numpy as jnp
from jax import lax
from jax.experimental import pallas as pl
from jax.experimental.pallas import tpu as pltpu
from jax.sharding import Mesh, PartitionSpec as P

epsilon = 1e-05

GROUPS = 32
DP = ("zl", "x", "c")
FRAME = ("y", "zh")
PLANE = ("x", "y")
LINE = ("zl", "zh")

C = 320
W = 32
PAD = 384
HALF = C // 2
PIX = 512
ROWS = 2 * PIX
STEP = 128
F32 = jnp.float32
BF16 = jnp.bfloat16

MIB = 1024 * 1024


VMEM = pl.BlockSpec(memory_space=pltpu.VMEM)
FAR = pl.BlockSpec(memory_space=pltpu.HBM)


def call(body, out, scratch=(), flops=0, limit=12, ins=None, outs=None):
    specs = {}
    if ins is not None:
        specs = {"in_specs": ins, "out_specs": outs}
    return pl.pallas_call(
        body,
        out_shape=out,
        scratch_shapes=list(scratch),
        compiler_params=pltpu.CompilerParams(vmem_limit_bytes=limit * MIB),
        cost_estimate=pl.CostEstimate(flops=flops, transcendentals=0, bytes_accessed=8_000_000),
        **specs,
    )


def shape(dims, kind):
    return jax.ShapeDtypeStruct(dims, kind)


def far(dims, kind):
    return pltpu.HBM(dims, kind)


def in_hbm(value):
    return pltpu.with_memory_space_constraint(value, pltpu.HBM)


def at(step, size=STEP):
    return pl.ds(pl.multiple_of(step * size, size), size)


def group_sum(rows):
    per = C // GROUPS
    one = lax.broadcasted_iota(jnp.int32, (C, C), 0) * 6554 >> 16
    two = lax.broadcasted_iota(jnp.int32, (C, C), 1) * 6554 >> 16
    assert per == 10
    same = jnp.where(one == two, 1.0, 0.0).astype(F32)
    return jnp.dot(rows, same, precision=lax.Precision.HIGHEST, preferred_element_type=F32)


def fold(value):
    return jnp.sum(value.reshape(value.shape[0] // 8, 8, value.shape[1]), axis=0)


def column(width):
    return lax.broadcasted_iota(jnp.int32, (STEP, width), 0) & (W - 1)


def four(*sums):
    return jnp.concatenate([jnp.sum(s, axis=0, keepdims=True) for s in sums] + [jnp.zeros((8 - len(sums), C), F32)])


def sigmoid(value):
    return 1.0 / (1.0 + jnp.exp(-value))


def forward_body(
    x_ref, far_w_ref, gain_ref, h0_ref, h1_ref, far_turned_ref, far_stat_ref, sums_ref,
    w_ref, wf, x3, y, turned, stat_ref, w_sem, turned_sem, stat_sem,
):
    fetch = pltpu.make_async_copy(far_w_ref, w_ref, w_sem)
    fetch.start()
    zero = jnp.zeros((8, C), F32)

    def moments(step, carry):
        value = x_ref[at(step), :].astype(F32)
        return carry[0] + fold(value), carry[1] + fold(value * value)

    half = PIX // STEP
    s0, q0 = lax.fori_loop(0, half, moments, (zero, zero))
    s1, q1 = lax.fori_loop(half, 2 * half, moments, (zero, zero))
    grouped = group_sum(four(s0, q0, s1, q1)) * (1.0 / (PIX * C // GROUPS))
    stats = []
    for f in range(2):
        mean = grouped[2 * f : 2 * f + 1]
        var = grouped[2 * f + 1 : 2 * f + 2] - mean * mean
        stats += [mean, lax.rsqrt(var + epsilon)]
    gain = gain_ref[...].reshape(1, C)
    stat_ref[...] = jnp.concatenate([*stats, gain, jnp.zeros((3, C), F32)])
    sends = [pltpu.make_async_copy(stat_ref, far_stat_ref, stat_sem)]
    sends[0].start()
    edge = column(C)

    def activate(step, mean, scale):
        value = x_ref[at(step), :].astype(F32)
        pre = (value - mean) * scale * gain
        act = pre / (1.0 + jnp.exp(-pre))
        low = act.astype(BF16)
        act = low.astype(F32)
        x3[at(step), 0:C] = jnp.where(edge == 0, 0.0, pltpu.roll(act, 1, 0)).astype(BF16)
        x3[at(step), C : 2 * C] = low
        x3[at(step), 2 * C : 3 * C] = jnp.where(
            edge == W - 1, 0.0, pltpu.roll(act, STEP - 1, 0)
        ).astype(BF16)

    def act_step(step, carry):
        activate(step, stats[0], stats[1])
        return carry

    lax.fori_loop(0, half, act_step, 0)
    fetch.wait()
    for i in range(3):
        for j in range(3):
            wf[C * j : C * (j + 1), PAD * i : PAD * i + C] = w_ref[3 * i + j]

    def product(f):
        y[f, 0:W, :] = jnp.zeros((W, 3 * PAD), F32)
        y[f, W + PIX : 2 * W + PIX, :] = jnp.zeros((W, 3 * PAD), F32)
        y[f, W : W + PIX, :] = jnp.dot(
            x3[f * PIX : (f + 1) * PIX, :], wf[...], preferred_element_type=F32
        )

    def turn_frame(f):
        turn(x3[f * PIX : (f + 1) * PIX, C : 2 * C], turned.at[f])
        send = pltpu.make_async_copy(
            turned.at[f], far_turned_ref.at[:, f * PIX : (f + 1) * PIX], turned_sem.at[f]
        )
        send.start()
        sends.append(send)

    def finish(f, h_ref, base, carry):
        conv = (
            y[f, pl.ds(base, STEP), 0:C]
            + y[f, pl.ds(base + W, STEP), PAD : PAD + C]
            + y[f, pl.ds(base + 2 * W, STEP), 2 * PAD : 2 * PAD + C]
        )
        value = x_ref[pl.ds(base + f * PIX, STEP), :].astype(F32)
        low = (value + conv).astype(BF16)
        h_ref[pl.ds(base, STEP), :] = low
        value = low.astype(F32)
        return carry[0] + fold(value), carry[1] + fold(value * value)

    product(0)
    for step in range(half, 2 * half):
        activate(step, stats[2], stats[3])
    turn_frame(0)
    product(1)
    total = (zero, zero)
    for step in range(half):
        total = finish(0, h0_ref, step * STEP, total)
    turn_frame(1)

    def last_step(step, carry):
        return finish(1, h1_ref, pl.multiple_of(step * STEP, STEP), carry)

    total = lax.fori_loop(0, half, last_step, total)
    spread(total, sums_ref)
    for send in sends:
        send.wait()


def spread(total, sums_ref):
    first = jnp.sum(total[0], axis=0, keepdims=True)
    second = jnp.sum(total[1], axis=0, keepdims=True)
    both = jnp.concatenate([first, second])
    for k in range(sums_ref.shape[0]):
        sums_ref[k] = both


def turn(acts, out_ref):
    rows = lax.broadcasted_iota(jnp.int32, (C, C), 0)
    same = jnp.where(rows == lax.broadcasted_iota(jnp.int32, (C, C), 1), 1.0, 0.0).astype(BF16)
    lane = lax.broadcasted_iota(jnp.int32, (C, STEP), 1) & (W - 1)
    moved = times_transposed(same, acts)
    for step in range(PIX // STEP):
        part = moved[:, step * STEP : (step + 1) * STEP]
        where = slice(step * STEP, (step + 1) * STEP)
        out_ref[0:C, where] = jnp.where(lane == 0, 0.0, pltpu.roll(part, 1, 1)).astype(BF16)
        out_ref[C : 2 * C, where] = part.astype(BF16)
        out_ref[2 * C : 3 * C, where] = jnp.where(
            lane == W - 1, 0.0, pltpu.roll(part, STEP - 1, 1)
        ).astype(BF16)


def forward(x, weight, gain, peers):
    return call(
        forward_body,
        (
            shape((PIX, C), BF16),
            shape((PIX, C), BF16),
            far((3 * C, ROWS), BF16),
            far((8, C), F32),
            shape((peers, 2, C), F32),
        ),
        (
            pltpu.VMEM((9, C, C), BF16),
            pltpu.VMEM((3 * C, 3 * PAD), BF16),
            pltpu.VMEM((ROWS, 3 * C), BF16),
            pltpu.VMEM((2, PIX + 2 * W, 3 * PAD), F32),
            pltpu.VMEM((2, 3 * C, PIX), BF16),
            pltpu.VMEM((8, C), F32),
            pltpu.SemaphoreType.DMA,
            pltpu.SemaphoreType.DMA((2,)),
            pltpu.SemaphoreType.DMA,
        ),
        flops=2_500_000_000,
        limit=24,
        ins=[VMEM, FAR, VMEM],
        outs=(VMEM, VMEM, FAR, FAR, VMEM),
    )(x, in_hbm(weight), gain)


def times_transposed(a, b):
    return lax.dot_general(a, b, (((1,), (1,)), ((), ())), preferred_element_type=F32)


def clip_stats(sums_ref, count):
    total = jnp.sum(sums_ref[...], axis=0)
    grouped = group_sum(jnp.concatenate([total, jnp.zeros((6, C), F32)])) * (1.0 / count)
    return grouped[0:1], grouped[1:2]


def mixed_grad_body(before_ref, cot_ref, after_ref, w_ref, far_ref, out_ref, sem):
    sends = []
    for f in range(2):
        here = slice(f * PIX, (f + 1) * PIX)
        last = cot_ref[0:PIX, :] if f else before_ref[...]
        later = after_ref[...] if f else cot_ref[PIX:ROWS, :]
        total = times_transposed(later, w_ref[0])
        total = total + times_transposed(cot_ref[here, :], w_ref[1])
        total = total + times_transposed(last, w_ref[2])
        out_ref[here, :] = total.astype(BF16)
        send = pltpu.make_async_copy(out_ref.at[here, :], far_ref.at[here, :], sem.at[f])
        send.start()
        sends.append(send)
    for send in sends:
        send.wait()


def mixed_gradient(before, cot, after, weight):
    return call(
        mixed_grad_body,
        far((ROWS, C), BF16),
        (pltpu.VMEM((ROWS, C), BF16), pltpu.SemaphoreType.DMA((2,))),
        flops=1_500_000_000,
        ins=[VMEM] * 4,
        outs=FAR,
    )(before, cot, after, weight)


def slope_body(
    count, sums_ref, h0_ref, h1_ref, far_grad_ref, cot_ref, gain_ref,
    part_ref, stat_ref, out_ref, far_stat_ref, grad_ref, sem, grad_sem,
):
    fetch = pltpu.make_async_copy(far_grad_ref, grad_ref, grad_sem)
    fetch.start()
    mean, square = clip_stats(sums_ref, count)
    scale = lax.rsqrt(square - mean * mean + epsilon)
    gain = gain_ref[...].reshape(1, C)
    stat_ref[...] = jnp.concatenate([mean, scale, gain, jnp.zeros((5, C), F32)])
    send = pltpu.make_async_copy(stat_ref, far_stat_ref, sem)
    send.start()
    fetch.wait()
    zero = jnp.zeros((8, C), F32)
    total = (zero, zero)
    for f, h_ref in enumerate((h0_ref, h1_ref)):

        def step_body(step, carry, f=f, h_ref=h_ref):
            base = pl.multiple_of(step * STEP, STEP)
            there = pl.ds(base + f * PIX, STEP)
            hat = (h_ref[pl.ds(base, STEP), :].astype(F32) - mean) * scale
            pre = hat * gain
            s = sigmoid(pre)
            slope = s * (1.0 + pre * (1.0 - s))
            dhat = grad_ref[there, :].astype(F32) * slope * gain
            part_ref[there, :] = cot_ref[there, :].astype(F32) + scale * dhat
            return carry[0] + fold(dhat), carry[1] + fold(dhat * hat)

        total = lax.fori_loop(0, PIX // STEP, step_body, total)
    spread(total, out_ref)
    send.wait()


def slopes(sums, h0, h1, grad, cot, gain, count):
    return call(
        functools.partial(slope_body, count),
        (shape((ROWS, C), F32), shape((8, C), F32), shape(sums.shape, F32), far((8, C), F32)),
        (pltpu.VMEM((ROWS, C), BF16), pltpu.SemaphoreType.DMA, pltpu.SemaphoreType.DMA),
        ins=[VMEM] * 3 + [FAR] + [VMEM] * 2,
        outs=(VMEM, VMEM, VMEM, FAR),
    )(sums, h0, h1, in_hbm(grad), cot, gain)


def mix(h_ref, base, mean, scale, gain):
    pre = (h_ref[pl.ds(base, STEP), :].astype(F32) - mean) * scale * gain
    return pre / (1.0 + jnp.exp(-pre))


def mixed_body(
    h0_ref, h1_ref, before_ref, cot_ref, after_ref, stat_ref,
    far_keep_ref, far_give_ref, turned, keep_ref, give_ref, sem,
):
    mean, scale, gain = stat_ref[0:1, :], stat_ref[1:2, :], stat_ref[2:3, :]
    for f, h_ref in enumerate((h0_ref, h1_ref)):
        for step in range(PIX // STEP):
            act = mix(h_ref, step * STEP, mean, scale, gain).astype(BF16)
            turned[:, f * PIX + step * STEP : f * PIX + (step + 1) * STEP] = act.T
    core = lax.axis_index("c")
    first, second = turned[:, 0:PIX], turned[:, PIX:ROWS]
    sends = []
    for k in range(3):
        if k == 1:
            part = jnp.dot(turned[...], cot_ref[...], preferred_element_type=F32)
        else:
            one = cot_ref[PIX:ROWS, :] if k == 0 else before_ref[...]
            two = after_ref[...] if k == 0 else cot_ref[0:PIX, :]
            part = jnp.dot(first, one, preferred_element_type=F32)
            part = part + jnp.dot(second, two, preferred_element_type=F32)
        left, right = part[:, 0:HALF], part[:, HALF:C]
        keep_ref[k * C : (k + 1) * C, 0:HALF] = jnp.where(core == 0, left, right)
        give_ref[k * C : (k + 1) * C, 0:HALF] = jnp.where(core == 0, right, left)
        here = slice(k * C, (k + 1) * C)
        sends += [
            pltpu.make_async_copy(give_ref.at[here, :], far_give_ref.at[here, :], sem.at[2 * k]),
            pltpu.make_async_copy(keep_ref.at[here, :], far_keep_ref.at[here, :], sem.at[2 * k + 1]),
        ]
        for send in sends[-2:]:
            send.start()
    for send in sends:
        send.wait()


def temporal_gradient(h0, h1, before, cot, after, stat):
    return call(
        mixed_body,
        (far((3 * C, 256), F32), far((3 * C, 256), F32)),
        (
            pltpu.VMEM((C, ROWS), BF16),
            pltpu.VMEM((3 * C, 256), F32),
            pltpu.VMEM((3 * C, 256), F32),
            pltpu.SemaphoreType.DMA((6,)),
        ),
        flops=1_500_000_000,
        ins=[VMEM] * 6,
        outs=(FAR, FAR),
    )(h0, h1, before, cot, after, stat)


def temporal_body(
    hb_ref, h0_ref, h1_ref, ha_ref, far_stat_ref, w_ref, out_ref, mx_ref, stat_ref, sem
):
    fetch = pltpu.make_async_copy(far_stat_ref, stat_ref, sem)
    fetch.start()
    fetch.wait()
    mean, scale, gain = stat_ref[0:1, :], stat_ref[1:2, :], stat_ref[2:3, :]
    place = lax.axis_index(FRAME)
    live = (place > 0, None, None, place < lax.axis_size(FRAME) - 1)
    for n, h_ref in enumerate((hb_ref, h0_ref, h1_ref, ha_ref)):

        def step_body(step, carry, n=n, h_ref=h_ref):
            base = pl.multiple_of(step * STEP, STEP)
            act = mix(h_ref, base, mean, scale, gain)
            if live[n] is not None:
                act = jnp.where(live[n], act, 0.0)
            mx_ref[pl.ds(base + n * PIX, STEP), :] = act.astype(BF16)
            return carry

        lax.fori_loop(0, PIX // STEP, step_body, 0)
    for f, h_ref in enumerate((h0_ref, h1_ref)):
        total = None
        for k in range(3):
            part = jnp.dot(
                mx_ref[(f + k) * PIX : (f + k + 1) * PIX, :],
                w_ref[k],
                preferred_element_type=F32,
            )
            total = part if total is None else total + part
        low = total.astype(BF16).astype(F32)
        out_ref[f * PIX : (f + 1) * PIX, :] = (h_ref[...].astype(F32) + low).astype(BF16)


def temporal(before, h0, h1, after, stat, weight):
    return call(
        temporal_body,
        shape((ROWS, C), BF16),
        (pltpu.VMEM((4 * PIX, C), BF16), pltpu.VMEM((8, C), F32), pltpu.SemaphoreType.DMA),
        flops=1_500_000_000,
        ins=[VMEM] * 4 + [FAR, VMEM],
        outs=VMEM,
    )(before, h0, h1, after, in_hbm(stat), weight)


def whole_grad(part_ref, h_ref, stat_ref, sums, base, f):
    mean, scale = stat_ref[0:1, :], stat_ref[1:2, :]
    hat = (h_ref[pl.ds(base, STEP), :].astype(F32) - mean) * scale
    return part_ref[pl.ds(base + f * PIX, STEP), :] - scale * (sums[0] + hat * sums[1])


def hidden_grad_body(
    count, sums_ref, stat_ref, part_ref, h0_ref, h1_ref,
    keep_ref, give_ref, far_total_ref, total_ref, sem,
):
    sums = clip_stats(sums_ref, count)
    total_ref[...] = jnp.concatenate([*sums, jnp.zeros((6, C), F32)])
    send = pltpu.make_async_copy(total_ref, far_total_ref, sem)
    send.start()
    core = lax.axis_index("c")
    for f, h_ref in enumerate((h0_ref, h1_ref)):

        def step_body(step, carry, f=f, h_ref=h_ref):
            base = pl.multiple_of(step * STEP, STEP)
            here = pl.ds(base + f * PIX, STEP)
            grad = whole_grad(part_ref, h_ref, stat_ref, sums, base, f)
            left, right = grad[:, 0:HALF], grad[:, HALF:C]
            keep_ref[here, :] = jnp.where(core == 0, left, right).astype(BF16)
            give_ref[here, :] = jnp.where(core == 0, right, left).astype(BF16)
            return carry

        lax.fori_loop(0, PIX // STEP, step_body, 0)
    send.wait()


def hidden_gradient(sums, stat, part, h0, h1, count):
    return call(
        functools.partial(hidden_grad_body, count),
        (shape((ROWS, HALF), BF16), shape((ROWS, HALF), BF16), far((8, C), F32)),
        (pltpu.VMEM((8, C), F32), pltpu.SemaphoreType.DMA),
        ins=[VMEM] * 5,
        outs=(VMEM, VMEM, FAR),
    )(sums, stat, part, h0, h1)


def row_taps(value):
    none = jnp.zeros((W, value.shape[1]), value.dtype)
    return (
        jnp.concatenate([value[W:], none]),
        value,
        jnp.concatenate([none, value[: PIX - W]]),
    )


def weight_grad_body(
    mine_turned_ref, other_turned_ref, mine_ref, other_ref, keep_ref, got_ref, far_ref, rhs, out, sem
):
    for n, ref in enumerate((mine_ref, other_ref)):
        for f in range(2):
            where = slice(f * PIX, (f + 1) * PIX)
            for i, tap in enumerate(row_taps(ref[where, :])):
                rhs[n, where, i * HALF : (i + 1) * HALF] = tap
    sends = []
    for j in range(3):
        here = slice(j * C, (j + 1) * C)
        total = jnp.dot(mine_turned_ref[here, :], rhs[0], preferred_element_type=F32)
        total = total + jnp.dot(other_turned_ref[here, :], rhs[1], preferred_element_type=F32)
        out[here, 0 : 3 * HALF] = total.astype(BF16)
        kept = keep_ref[here, 0:HALF] + got_ref[here, 0:HALF]
        out[here, 3 * HALF : 4 * HALF] = kept.astype(BF16)
        if j == 2:
            out[3 * C :, :] = jnp.zeros((1024 - 3 * C, 4 * HALF), BF16)
            here = slice(j * C, 1024)
        send = pltpu.make_async_copy(out.at[here, :], far_ref.at[here, :], sem.at[j])
        send.start()
        sends.append(send)
    for send in sends:
        send.wait()


def weight_gradients(mine_turned, other_turned, mine, other, keep, got):
    return call(
        weight_grad_body,
        far((1024, 4 * HALF), BF16),
        (
            pltpu.VMEM((2, ROWS, 3 * HALF), BF16),
            pltpu.VMEM((1024, 4 * HALF), BF16),
            pltpu.SemaphoreType.DMA((3,)),
        ),
        flops=2_500_000_000,
        ins=[VMEM] * 6,
        outs=FAR,
    )(mine_turned, other_turned, mine, other, keep, got)


def input_grad_body(
    part_ref, h0_ref, h1_ref, far_clip_ref, far_total_ref, x_ref, far_stat_ref, far_w_ref,
    out_ref, wb, rows, z, dh, grads, lows, clip_ref, total_ref, stat_ref, w_ref, sem,
):
    pairs = (far_clip_ref, clip_ref), (far_total_ref, total_ref), (far_stat_ref, stat_ref)
    fetches = [
        pltpu.make_async_copy(one, two, sem.at[n])
        for n, (one, two) in enumerate((*pairs, (far_w_ref, w_ref)))
    ]
    for fetch in fetches:
        fetch.start()
    for fetch in fetches[:3]:
        fetch.wait()
    clip_sums = total_ref[0:1, :], total_ref[1:2, :]
    gain = stat_ref[4:5, :]
    edge = column(C)
    half = PIX // STEP
    for f in range(2):
        mean, scale = stat_ref[2 * f : 2 * f + 1, :], stat_ref[2 * f + 1 : 2 * f + 2, :]
        h_ref = (h0_ref, h1_ref)[f]

        def grad_body(step, carry, f=f, h_ref=h_ref):
            base = pl.multiple_of(step * STEP, STEP)
            grad = whole_grad(part_ref, h_ref, clip_ref, clip_sums, base, f)
            grads[pl.ds(base, STEP), :] = grad
            lows[pl.ds(base, STEP), :] = grad.astype(BF16)
            return carry

        lax.fori_loop(0, half, grad_body, 0)
        if f == 0:
            fetches[3].wait()
            for j in range(3):
                for i in range(3):
                    wb[PAD * j : PAD * j + C, C * i : C * (i + 1)] = w_ref[3 * i + j]
                wb[PAD * j + C : PAD * (j + 1), :] = jnp.zeros((PAD - C, 3 * C), BF16)
        for i, tap in enumerate(row_taps(lows[...])):
            rows[:, i * C : (i + 1) * C] = tap
        z[...] = times_transposed(rows[...], wb[...])

        def step_body(step, carry, f=f, mean=mean, scale=scale):
            base = pl.multiple_of(step * STEP, STEP)
            here = pl.ds(base, STEP)
            right = jnp.where(edge == W - 1, 0.0, pltpu.roll(z[here, 0:C], STEP - 1, 0))
            left = jnp.where(edge == 0, 0.0, pltpu.roll(z[here, 2 * PAD : 2 * PAD + C], 1, 0))
            acts_grad = right + z[here, PAD : PAD + C] + left
            hat = (x_ref[pl.ds(base + f * PIX, STEP), :].astype(F32) - mean) * scale
            pre = hat * gain
            s = sigmoid(pre)
            dhat = acts_grad * (s * (1.0 + pre * (1.0 - s))) * gain
            dh[here, :] = dhat
            return carry[0] + fold(dhat), carry[1] + fold(dhat * hat)

        zero = jnp.zeros((8, C), F32)
        sums = lax.fori_loop(0, half, step_body, (zero, zero))
        grouped = group_sum(four(*sums)) * (1.0 / (PIX * C // GROUPS))
        first, second = grouped[0:1], grouped[1:2]

        def last_body(step, carry, f=f, mean=mean, scale=scale, first=first, second=second):
            base = pl.multiple_of(step * STEP, STEP)
            there = pl.ds(base + f * PIX, STEP)
            hat = (x_ref[there, :].astype(F32) - mean) * scale
            here = pl.ds(base, STEP)
            value = grads[here, :] + scale * (dh[here, :] - first - hat * second)
            out_ref[there, :] = value.astype(BF16)
            return carry

        lax.fori_loop(0, half, last_body, 0)


def input_gradient(part, h0, h1, clip_stat, total, x, stat, weight):
    return call(
        input_grad_body,
        shape((ROWS, C), BF16),
        (
            pltpu.VMEM((3 * PAD, 3 * C), BF16),
            pltpu.VMEM((PIX, 3 * C), BF16),
            pltpu.VMEM((PIX, 3 * PAD), F32),
            pltpu.VMEM((PIX, C), F32),
            pltpu.VMEM((PIX, C), F32),
            pltpu.VMEM((PIX, C), BF16),
            pltpu.VMEM((8, C), F32),
            pltpu.VMEM((8, C), F32),
            pltpu.VMEM((8, C), F32),
            pltpu.VMEM((9, C, C), BF16),
            pltpu.SemaphoreType.DMA((4,)),
        ),
        flops=2_500_000_000,
        limit=18,
        ins=[VMEM] * 3 + [FAR] * 2 + [VMEM] + [FAR] * 2,
        outs=VMEM,
    )(part, h0, h1, in_hbm(clip_stat), in_hbm(total), x, in_hbm(stat), in_hbm(weight))


def unpack_body(mine_ref, other_ref, far_spatial_ref, far_temporal_ref, taps, sem):
    core = lax.axis_index("c")
    sends = []
    for j in range(3):
        here = slice(j * C, (j + 1) * C)
        mine, other = mine_ref[here, :], other_ref[here, :]
        left = jnp.where(core == 0, mine, other)
        right = jnp.where(core == 0, other, mine)
        for i in range(4):
            n = 3 * i + j
            lanes = slice(i * HALF, (i + 1) * HALF)
            taps[n, :, 0:HALF] = left[:, lanes]
            taps[n, :, HALF:C] = right[:, lanes]
            target = far_spatial_ref.at[n] if i < 3 else far_temporal_ref.at[j]
            send = pltpu.make_async_copy(taps.at[n], target, sem.at[n])
            send.start()
            sends.append(send)
    for send in sends:
        send.wait()


def unpack(mine, other):
    return call(
        unpack_body,
        (far((9, C, C), BF16), far((3, C, C), BF16)),
        (pltpu.VMEM((12, C, C), BF16), pltpu.SemaphoreType.DMA((12,))),
        ins=[VMEM] * 2,
        outs=(FAR, FAR),
    )(mine, other)


def neighbours(first, second):
    size = lax.axis_size(FRAME)
    before = lax.ppermute(second, FRAME, [(i, i + 1) for i in range(size - 1)])
    after = lax.ppermute(first, FRAME, [(i + 1, i) for i in range(size - 1)])
    return before, after


def swap_cores(value):
    return lax.ppermute(value, "c", [(0, 1), (1, 0)])


def everyone_total(value):
    plane = lax.axis_size(PLANE)
    value = value.reshape(plane, 1024 // plane, value.shape[1])
    return lax.all_to_all(value, PLANE, 0, 0)


def everyone_share(value, beside):
    plane, line = lax.axis_size(PLANE), lax.axis_size(LINE)
    width = value.shape[2]
    value = jnp.sum(value.astype(F32), axis=0)
    value = value.reshape(line, 1024 // plane // line, width)
    value = jnp.sum(lax.all_to_all(value, LINE, 0, 0), axis=0).astype(BF16)
    value, *beside = lax.optimization_barrier((value, *beside))
    value = jnp.broadcast_to(value[None], (line,) + value.shape)
    return beside, lax.all_to_all(value, LINE, 0, 0).reshape(1024 // plane, width)


def everyone_gets(value):
    plane = lax.axis_size(PLANE)
    value = jnp.broadcast_to(value[None], (plane,) + value.shape)
    return lax.all_to_all(value, PLANE, 0, 0).reshape(1024, value.shape[2])


def on_device(clips, cotangent, spatial_weight, temporal_weight, gain_one, gain_two):
    size = lax.axis_size(FRAME)
    count = float(size * ROWS * C // GROUPS)
    x = clips.reshape(ROWS, C)
    cot = cotangent.reshape(ROWS, C)
    spatial_weight = spatial_weight.reshape(9, C, C)
    barrier = lax.optimization_barrier
    cot_before, cot_after = neighbours(cot[:PIX], cot[PIX:])
    h0, h1, mine_turned, stat_one, sums = forward(x, spatial_weight, gain_one, size)
    sums = lax.all_to_all(sums, FRAME, 0, 0)
    mixed_grad = mixed_gradient(cot_before, cot, cot_after, temporal_weight)
    sums, mine_turned, mixed_grad = barrier((sums, mine_turned, mixed_grad))
    other_turned = swap_cores(mine_turned)
    part, clip_stat, sums, far_stat = slopes(sums, h0, h1, mixed_grad, cot, gain_two, count)
    sums = lax.all_to_all(sums, FRAME, 0, 0)
    temporal_keep, temporal_give = temporal_gradient(
        h0, h1, cot_before, cot, cot_after, clip_stat
    )
    sums, temporal_give = barrier((sums, temporal_give))
    temporal_got = swap_cores(temporal_give)
    low_keep, low_give, total = hidden_gradient(sums, clip_stat, part, h0, h1, count)
    low_got = swap_cores(low_give)
    packed = weight_gradients(
        mine_turned, other_turned, low_keep, low_got, temporal_keep, temporal_got
    )
    packed, total, edge0, edge1 = barrier((packed, total, h0, h1))
    shares = everyone_total(packed)
    before, after = neighbours(edge0, edge1)
    input_grad = input_gradient(
        part, h0, h1, far_stat, total, x, stat_one, spatial_weight
    )
    shares, input_grad = barrier((shares, input_grad))
    (before, after), mine = everyone_share(shares, (before, after))
    mine, before, after = barrier((mine, before, after))
    output = temporal(before, h0, h1, after, far_stat, temporal_weight)
    mine, output = barrier((everyone_gets(mine), output))
    other = swap_cores(mine)
    spatial_grad, temporal_grad = unpack(mine, other)
    return (
        output.reshape(clips.shape),
        input_grad.reshape(clips.shape),
        spatial_grad.reshape(3, 3, C, C),
        temporal_grad,
    )


def solution(mesh):
    fine = Mesh(mesh.devices.reshape(2, 4, 2, 4, 4), ("zl", "x", "c", "y", "zh"))
    return jax.shard_map(
        on_device,
        mesh=fine,
        in_specs=(P(DP, FRAME), P(DP, FRAME), P(), P(), P(), P()),
        out_specs=(P(DP, FRAME), P(DP, FRAME), P(), P()),
        check_vma=False,
    )
```

```python
import functools

import jax
import jax.numpy as jnp
from jax import lax
from jax.experimental import pallas as pl
from jax.experimental.pallas import tpu as pltpu
from jax.sharding import Mesh, PartitionSpec as P

epsilon = 1e-05

GROUPS = 32
DP = ("zl", "x", "c")
FRAME = ("y", "zh")
PLANE = ("x", "y")
LINE = ("zl", "zh")

C = 320
W = 32
PAD = 384
HALF = C // 2
PIX = 512
ROWS = 2 * PIX
STEP = 128
F32 = jnp.float32
BF16 = jnp.bfloat16

MIB = 1024 * 1024


VMEM = pl.BlockSpec(memory_space=pltpu.VMEM)
FAR = pl.BlockSpec(memory_space=pltpu.HBM)


def call(body, out, scratch=(), flops=0, limit=12, ins=None, outs=None):
    specs = {}
    if ins is not None:
        specs = {"in_specs": ins, "out_specs": outs}
    return pl.pallas_call(
        body,
        out_shape=out,
        scratch_shapes=list(scratch),
        compiler_params=pltpu.CompilerParams(vmem_limit_bytes=limit * MIB),
        cost_estimate=pl.CostEstimate(flops=flops, transcendentals=0, bytes_accessed=8_000_000),
        **specs,
    )


def shape(dims, kind):
    return jax.ShapeDtypeStruct(dims, kind)


def far(dims, kind):
    return pltpu.HBM(dims, kind)


def in_hbm(value):
    return pltpu.with_memory_space_constraint(value, pltpu.HBM)


def at(step, size=STEP):
    return pl.ds(pl.multiple_of(step * size, size), size)


def group_sum(rows):
    per = C // GROUPS
    one = lax.broadcasted_iota(jnp.int32, (C, C), 0) * 6554 >> 16
    two = lax.broadcasted_iota(jnp.int32, (C, C), 1) * 6554 >> 16
    assert per == 10
    same = jnp.where(one == two, 1.0, 0.0).astype(F32)
    return jnp.dot(rows, same, precision=lax.Precision.HIGHEST, preferred_element_type=F32)


def fold(value):
    return jnp.sum(value.reshape(value.shape[0] // 8, 8, value.shape[1]), axis=0)


def column(width):
    return lax.broadcasted_iota(jnp.int32, (STEP, width), 0) & (W - 1)


def four(*sums):
    return jnp.concatenate([jnp.sum(s, axis=0, keepdims=True) for s in sums] + [jnp.zeros((8 - len(sums), C), F32)])


def sigmoid(value):
    return 1.0 / (1.0 + jnp.exp(-value))


def forward_body(
    x_ref, far_w_ref, gain_ref, h0_ref, h1_ref, far_turned_ref, far_stat_ref, sums_ref,
    w_ref, wf, x3, y, turned, stat_ref, w_sem, turned_sem, stat_sem,
):
    fetch = pltpu.make_async_copy(far_w_ref, w_ref, w_sem)
    fetch.start()
    zero = jnp.zeros((8, C), F32)

    def moments(step, carry):
        value = x_ref[at(step), :].astype(F32)
        return carry[0] + fold(value), carry[1] + fold(value * value)

    half = PIX // STEP
    s0, q0 = lax.fori_loop(0, half, moments, (zero, zero))
    s1, q1 = lax.fori_loop(half, 2 * half, moments, (zero, zero))
    grouped = group_sum(four(s0, q0, s1, q1)) * (1.0 / (PIX * C // GROUPS))
    stats = []
    for f in range(2):
        mean = grouped[2 * f : 2 * f + 1]
        var = grouped[2 * f + 1 : 2 * f + 2] - mean * mean
        stats += [mean, lax.rsqrt(var + epsilon)]
    gain = gain_ref[...].reshape(1, C)
    stat_ref[...] = jnp.concatenate([*stats, gain, jnp.zeros((3, C), F32)])
    sends = [pltpu.make_async_copy(stat_ref, far_stat_ref, stat_sem)]
    sends[0].start()
    edge = column(C)

    def activate(step, mean, scale):
        value = x_ref[at(step), :].astype(F32)
        pre = (value - mean) * scale * gain
        act = pre / (1.0 + jnp.exp(-pre))
        low = act.astype(BF16)
        act = low.astype(F32)
        x3[at(step), 0:C] = jnp.where(edge == 0, 0.0, pltpu.roll(act, 1, 0)).astype(BF16)
        x3[at(step), C : 2 * C] = low
        x3[at(step), 2 * C : 3 * C] = jnp.where(
            edge == W - 1, 0.0, pltpu.roll(act, STEP - 1, 0)
        ).astype(BF16)

    def act_step(step, carry):
        activate(step, stats[0], stats[1])
        return carry

    lax.fori_loop(0, half, act_step, 0)
    fetch.wait()
    for i in range(3):
        for j in range(3):
            wf[C * j : C * (j + 1), PAD * i : PAD * i + C] = w_ref[3 * i + j]

    def product(f):
        y[f, 0:W, :] = jnp.zeros((W, 3 * PAD), F32)
        y[f, W + PIX : 2 * W + PIX, :] = jnp.zeros((W, 3 * PAD), F32)
        y[f, W : W + PIX, :] = jnp.dot(
            x3[f * PIX : (f + 1) * PIX, :], wf[...], preferred_element_type=F32
        )

    def turn_frame(f):
        turn(x3[f * PIX : (f + 1) * PIX, C : 2 * C], turned.at[f])
        send = pltpu.make_async_copy(
            turned.at[f], far_turned_ref.at[:, f * PIX : (f + 1) * PIX], turned_sem.at[f]
        )
        send.start()
        sends.append(send)

    def finish(f, h_ref, base, carry):
        conv = (
            y[f, pl.ds(base, STEP), 0:C]
            + y[f, pl.ds(base + W, STEP), PAD : PAD + C]
            + y[f, pl.ds(base + 2 * W, STEP), 2 * PAD : 2 * PAD + C]
        )
        value = x_ref[pl.ds(base + f * PIX, STEP), :].astype(F32)
        low = (value + conv).astype(BF16)
        h_ref[pl.ds(base, STEP), :] = low
        value = low.astype(F32)
        return carry[0] + fold(value), carry[1] + fold(value * value)

    product(0)
    for step in range(half, 2 * half):
        activate(step, stats[2], stats[3])
    turn_frame(0)
    product(1)
    total = (zero, zero)
    for step in range(half):
        total = finish(0, h0_ref, step * STEP, total)
    turn_frame(1)

    def last_step(step, carry):
        return finish(1, h1_ref, pl.multiple_of(step * STEP, STEP), carry)

    total = lax.fori_loop(0, half, last_step, total)
    spread(total, sums_ref)
    for send in sends:
        send.wait()


def spread(total, sums_ref):
    first = jnp.sum(total[0], axis=0, keepdims=True)
    second = jnp.sum(total[1], axis=0, keepdims=True)
    both = jnp.concatenate([first, second])
    for k in range(sums_ref.shape[0]):
        sums_ref[k] = both


def turn(acts, out_ref):
    rows = lax.broadcasted_iota(jnp.int32, (C, C), 0)
    same = jnp.where(rows == lax.broadcasted_iota(jnp.int32, (C, C), 1), 1.0, 0.0).astype(BF16)
    lane = lax.broadcasted_iota(jnp.int32, (C, STEP), 1) & (W - 1)
    moved = times_transposed(same, acts)
    for step in range(PIX // STEP):
        part = moved[:, step * STEP : (step + 1) * STEP]
        where = slice(step * STEP, (step + 1) * STEP)
        out_ref[0:C, where] = jnp.where(lane == 0, 0.0, pltpu.roll(part, 1, 1)).astype(BF16)
        out_ref[C : 2 * C, where] = part.astype(BF16)
        out_ref[2 * C : 3 * C, where] = jnp.where(
            lane == W - 1, 0.0, pltpu.roll(part, STEP - 1, 1)
        ).astype(BF16)


def forward(x, weight, gain, peers):
    return call(
        forward_body,
        (
            shape((PIX, C), BF16),
            shape((PIX, C), BF16),
            far((3 * C, ROWS), BF16),
            far((8, C), F32),
            shape((peers, 2, C), F32),
        ),
        (
            pltpu.VMEM((9, C, C), BF16),
            pltpu.VMEM((3 * C, 3 * PAD), BF16),
            pltpu.VMEM((ROWS, 3 * C), BF16),
            pltpu.VMEM((2, PIX + 2 * W, 3 * PAD), F32),
            pltpu.VMEM((2, 3 * C, PIX), BF16),
            pltpu.VMEM((8, C), F32),
            pltpu.SemaphoreType.DMA,
            pltpu.SemaphoreType.DMA((2,)),
            pltpu.SemaphoreType.DMA,
        ),
        flops=2_500_000_000,
        limit=24,
        ins=[VMEM, FAR, VMEM],
        outs=(VMEM, VMEM, FAR, FAR, VMEM),
    )(x, in_hbm(weight), gain)


def times_transposed(a, b):
    return lax.dot_general(a, b, (((1,), (1,)), ((), ())), preferred_element_type=F32)


def clip_stats(sums_ref, count):
    total = jnp.sum(sums_ref[...], axis=0)
    grouped = group_sum(jnp.concatenate([total, jnp.zeros((6, C), F32)])) * (1.0 / count)
    return grouped[0:1], grouped[1:2]


def mixed_grad_body(before_ref, cot_ref, after_ref, w_ref, far_ref, out_ref, sem):
    sends = []
    for f in range(2):
        here = slice(f * PIX, (f + 1) * PIX)
        last = cot_ref[0:PIX, :] if f else before_ref[...]
        later = after_ref[...] if f else cot_ref[PIX:ROWS, :]
        total = times_transposed(later, w_ref[0])
        total = total + times_transposed(cot_ref[here, :], w_ref[1])
        total = total + times_transposed(last, w_ref[2])
        out_ref[here, :] = total.astype(BF16)
        send = pltpu.make_async_copy(out_ref.at[here, :], far_ref.at[here, :], sem.at[f])
        send.start()
        sends.append(send)
    for send in sends:
        send.wait()


def mixed_gradient(before, cot, after, weight):
    return call(
        mixed_grad_body,
        far((ROWS, C), BF16),
        (pltpu.VMEM((ROWS, C), BF16), pltpu.SemaphoreType.DMA((2,))),
        flops=1_500_000_000,
        ins=[VMEM] * 4,
        outs=FAR,
    )(before, cot, after, weight)


def slope_body(
    count, sums_ref, h0_ref, h1_ref, far_grad_ref, cot_ref, gain_ref,
    part_ref, stat_ref, out_ref, far_stat_ref, grad_ref, sem, grad_sem,
):
    fetch = pltpu.make_async_copy(far_grad_ref, grad_ref, grad_sem)
    fetch.start()
    mean, square = clip_stats(sums_ref, count)
    scale = lax.rsqrt(square - mean * mean + epsilon)
    gain = gain_ref[...].reshape(1, C)
    stat_ref[...] = jnp.concatenate([mean, scale, gain, jnp.zeros((5, C), F32)])
    send = pltpu.make_async_copy(stat_ref, far_stat_ref, sem)
    send.start()
    fetch.wait()
    zero = jnp.zeros((8, C), F32)
    total = (zero, zero)
    for f, h_ref in enumerate((h0_ref, h1_ref)):

        def step_body(step, carry, f=f, h_ref=h_ref):
            base = pl.multiple_of(step * STEP, STEP)
            there = pl.ds(base + f * PIX, STEP)
            hat = (h_ref[pl.ds(base, STEP), :].astype(F32) - mean) * scale
            pre = hat * gain
            s = sigmoid(pre)
            slope = s * (1.0 + pre * (1.0 - s))
            dhat = grad_ref[there, :].astype(F32) * slope * gain
            part_ref[there, :] = cot_ref[there, :].astype(F32) + scale * dhat
            return carry[0] + fold(dhat), carry[1] + fold(dhat * hat)

        total = lax.fori_loop(0, PIX // STEP, step_body, total)
    spread(total, out_ref)
    send.wait()


def slopes(sums, h0, h1, grad, cot, gain, count):
    return call(
        functools.partial(slope_body, count),
        (shape((ROWS, C), F32), shape((8, C), F32), shape(sums.shape, F32), far((8, C), F32)),
        (pltpu.VMEM((ROWS, C), BF16), pltpu.SemaphoreType.DMA, pltpu.SemaphoreType.DMA),
        ins=[VMEM] * 3 + [FAR] + [VMEM] * 2,
        outs=(VMEM, VMEM, VMEM, FAR),
    )(sums, h0, h1, in_hbm(grad), cot, gain)


def mix(h_ref, base, mean, scale, gain):
    pre = (h_ref[pl.ds(base, STEP), :].astype(F32) - mean) * scale * gain
    return pre / (1.0 + jnp.exp(-pre))


def mixed_body(
    h0_ref, h1_ref, before_ref, cot_ref, after_ref, stat_ref,
    far_keep_ref, far_give_ref, turned, keep_ref, give_ref, sem,
):
    mean, scale, gain = stat_ref[0:1, :], stat_ref[1:2, :], stat_ref[2:3, :]
    for f, h_ref in enumerate((h0_ref, h1_ref)):
        for step in range(PIX // STEP):
            act = mix(h_ref, step * STEP, mean, scale, gain).astype(BF16)
            turned[:, f * PIX + step * STEP : f * PIX + (step + 1) * STEP] = act.T
    core = lax.axis_index("c")
    first, second = turned[:, 0:PIX], turned[:, PIX:ROWS]
    sends = []
    for k in range(3):
        if k == 1:
            part = jnp.dot(turned[...], cot_ref[...], preferred_element_type=F32)
        else:
            one = cot_ref[PIX:ROWS, :] if k == 0 else before_ref[...]
            two = after_ref[...] if k == 0 else cot_ref[0:PIX, :]
            part = jnp.dot(first, one, preferred_element_type=F32)
            part = part + jnp.dot(second, two, preferred_element_type=F32)
        left, right = part[:, 0:HALF], part[:, HALF:C]
        keep_ref[k * C : (k + 1) * C, 0:HALF] = jnp.where(core == 0, left, right)
        give_ref[k * C : (k + 1) * C, 0:HALF] = jnp.where(core == 0, right, left)
        here = slice(k * C, (k + 1) * C)
        sends += [
            pltpu.make_async_copy(give_ref.at[here, :], far_give_ref.at[here, :], sem.at[2 * k]),
            pltpu.make_async_copy(keep_ref.at[here, :], far_keep_ref.at[here, :], sem.at[2 * k + 1]),
        ]
        for send in sends[-2:]:
            send.start()
    for send in sends:
        send.wait()


def temporal_gradient(h0, h1, before, cot, after, stat):
    return call(
        mixed_body,
        (far((3 * C, 256), F32), far((3 * C, 256), F32)),
        (
            pltpu.VMEM((C, ROWS), BF16),
            pltpu.VMEM((3 * C, 256), F32),
            pltpu.VMEM((3 * C, 256), F32),
            pltpu.SemaphoreType.DMA((6,)),
        ),
        flops=1_500_000_000,
        ins=[VMEM] * 6,
        outs=(FAR, FAR),
    )(h0, h1, before, cot, after, stat)


def temporal_body(
    hb_ref, h0_ref, h1_ref, ha_ref, far_stat_ref, w_ref, out_ref, mx_ref, stat_ref, sem
):
    fetch = pltpu.make_async_copy(far_stat_ref, stat_ref, sem)
    fetch.start()
    fetch.wait()
    mean, scale, gain = stat_ref[0:1, :], stat_ref[1:2, :], stat_ref[2:3, :]
    place = lax.axis_index(FRAME)
    live = (place > 0, None, None, place < lax.axis_size(FRAME) - 1)
    for n, h_ref in enumerate((hb_ref, h0_ref, h1_ref, ha_ref)):

        def step_body(step, carry, n=n, h_ref=h_ref):
            base = pl.multiple_of(step * STEP, STEP)
            act = mix(h_ref, base, mean, scale, gain)
            if live[n] is not None:
                act = jnp.where(live[n], act, 0.0)
            mx_ref[pl.ds(base + n * PIX, STEP), :] = act.astype(BF16)
            return carry

        lax.fori_loop(0, PIX // STEP, step_body, 0)
    for f, h_ref in enumerate((h0_ref, h1_ref)):
        total = None
        for k in range(3):
            part = jnp.dot(
                mx_ref[(f + k) * PIX : (f + k + 1) * PIX, :],
                w_ref[k],
                preferred_element_type=F32,
            )
            total = part if total is None else total + part
        low = total.astype(BF16).astype(F32)
        out_ref[f * PIX : (f + 1) * PIX, :] = (h_ref[...].astype(F32) + low).astype(BF16)


def temporal(before, h0, h1, after, stat, weight):
    return call(
        temporal_body,
        shape((ROWS, C), BF16),
        (pltpu.VMEM((4 * PIX, C), BF16), pltpu.VMEM((8, C), F32), pltpu.SemaphoreType.DMA),
        flops=1_500_000_000,
        ins=[VMEM] * 4 + [FAR, VMEM],
        outs=VMEM,
    )(before, h0, h1, after, in_hbm(stat), weight)


def whole_grad(part_ref, h_ref, stat_ref, sums, base, f):
    mean, scale = stat_ref[0:1, :], stat_ref[1:2, :]
    hat = (h_ref[pl.ds(base, STEP), :].astype(F32) - mean) * scale
    return part_ref[pl.ds(base + f * PIX, STEP), :] - scale * (sums[0] + hat * sums[1])


def hidden_grad_body(
    count, sums_ref, stat_ref, part_ref, h0_ref, h1_ref,
    keep_ref, give_ref, far_total_ref, total_ref, sem,
):
    sums = clip_stats(sums_ref, count)
    total_ref[...] = jnp.concatenate([*sums, jnp.zeros((6, C), F32)])
    send = pltpu.make_async_copy(total_ref, far_total_ref, sem)
    send.start()
    core = lax.axis_index("c")
    for f, h_ref in enumerate((h0_ref, h1_ref)):

        def step_body(step, carry, f=f, h_ref=h_ref):
            base = pl.multiple_of(step * STEP, STEP)
            here = pl.ds(base + f * PIX, STEP)
            grad = whole_grad(part_ref, h_ref, stat_ref, sums, base, f)
            left, right = grad[:, 0:HALF], grad[:, HALF:C]
            keep_ref[here, :] = jnp.where(core == 0, left, right).astype(BF16)
            give_ref[here, :] = jnp.where(core == 0, right, left).astype(BF16)
            return carry

        lax.fori_loop(0, PIX // STEP, step_body, 0)
    send.wait()


def hidden_gradient(sums, stat, part, h0, h1, count):
    return call(
        functools.partial(hidden_grad_body, count),
        (shape((ROWS, HALF), BF16), shape((ROWS, HALF), BF16), far((8, C), F32)),
        (pltpu.VMEM((8, C), F32), pltpu.SemaphoreType.DMA),
        ins=[VMEM] * 5,
        outs=(VMEM, VMEM, FAR),
    )(sums, stat, part, h0, h1)


def row_taps(value):
    none = jnp.zeros((W, value.shape[1]), value.dtype)
    return (
        jnp.concatenate([value[W:], none]),
        value,
        jnp.concatenate([none, value[: PIX - W]]),
    )


def weight_grad_body(
    far_mine_ref, far_other_ref, mine_ref, other_ref, far_keep_ref, got_ref, far_ref,
    rhs, out, turned, keep_ref, sem, fetch_sem, keep_sem,
):
    fetches = []
    for j in range(3):
        here = slice(j * C, (j + 1) * C)
        for n, ref in enumerate((far_mine_ref, far_other_ref)):
            fetch = pltpu.make_async_copy(
                ref.at[here, :], turned.at[n, here, :], fetch_sem.at[2 * j + n]
            )
            fetch.start()
            fetches.append(fetch)
    keep_fetch = pltpu.make_async_copy(far_keep_ref, keep_ref, keep_sem)
    keep_fetch.start()
    for n, ref in enumerate((mine_ref, other_ref)):
        for f in range(2):
            where = slice(f * PIX, (f + 1) * PIX)
            for i, tap in enumerate(row_taps(ref[where, :])):
                rhs[n, where, i * HALF : (i + 1) * HALF] = tap
    keep_fetch.wait()
    sends = []
    for j in range(3):
        here = slice(j * C, (j + 1) * C)
        for fetch in fetches[2 * j : 2 * j + 2]:
            fetch.wait()
        total = jnp.dot(turned[0, here, :], rhs[0], preferred_element_type=F32)
        total = total + jnp.dot(turned[1, here, :], rhs[1], preferred_element_type=F32)
        out[here, 0 : 3 * HALF] = total.astype(BF16)
        kept = keep_ref[here, 0:HALF] + got_ref[here, 0:HALF]
        out[here, 3 * HALF : 4 * HALF] = kept.astype(BF16)
        if j == 2:
            out[3 * C :, :] = jnp.zeros((1024 - 3 * C, 4 * HALF), BF16)
            here = slice(j * C, 1024)
        send = pltpu.make_async_copy(out.at[here, :], far_ref.at[here, :], sem.at[j])
        send.start()
        sends.append(send)
    for send in sends:
        send.wait()


def weight_gradients(mine_turned, other_turned, mine, other, keep, got):
    return call(
        weight_grad_body,
        far((1024, 4 * HALF), BF16),
        (
            pltpu.VMEM((2, ROWS, 3 * HALF), BF16),
            pltpu.VMEM((1024, 4 * HALF), BF16),
            pltpu.VMEM((2, 3 * C, ROWS), BF16),
            pltpu.VMEM((3 * C, 256), F32),
            pltpu.SemaphoreType.DMA((3,)),
            pltpu.SemaphoreType.DMA((6,)),
            pltpu.SemaphoreType.DMA,
        ),
        flops=2_500_000_000,
        limit=16,
        ins=[FAR] * 2 + [VMEM] * 2 + [FAR, VMEM],
        outs=FAR,
    )(in_hbm(mine_turned), in_hbm(other_turned), mine, other, in_hbm(keep), got)


def input_grad_body(
    part_ref, h0_ref, h1_ref, far_clip_ref, far_total_ref, x_ref, far_stat_ref, far_w_ref,
    out_ref, wb, rows, z, dh, grads, lows, clip_ref, total_ref, stat_ref, w_ref, sem,
):
    pairs = (far_clip_ref, clip_ref), (far_total_ref, total_ref), (far_stat_ref, stat_ref)
    fetches = [
        pltpu.make_async_copy(one, two, sem.at[n])
        for n, (one, two) in enumerate((*pairs, (far_w_ref, w_ref)))
    ]
    for fetch in fetches:
        fetch.start()
    for fetch in fetches[:3]:
        fetch.wait()
    clip_sums = total_ref[0:1, :], total_ref[1:2, :]
    gain = stat_ref[4:5, :]
    edge = column(C)
    half = PIX // STEP
    for f in range(2):
        mean, scale = stat_ref[2 * f : 2 * f + 1, :], stat_ref[2 * f + 1 : 2 * f + 2, :]
        h_ref = (h0_ref, h1_ref)[f]

        def grad_body(step, carry, f=f, h_ref=h_ref):
            base = pl.multiple_of(step * STEP, STEP)
            grad = whole_grad(part_ref, h_ref, clip_ref, clip_sums, base, f)
            grads[pl.ds(base, STEP), :] = grad
            lows[pl.ds(base, STEP), :] = grad.astype(BF16)
            return carry

        lax.fori_loop(0, half, grad_body, 0)
        if f == 0:
            fetches[3].wait()
            for j in range(3):
                for i in range(3):
                    wb[PAD * j : PAD * j + C, C * i : C * (i + 1)] = w_ref[3 * i + j]
                wb[PAD * j + C : PAD * (j + 1), :] = jnp.zeros((PAD - C, 3 * C), BF16)
        for i, tap in enumerate(row_taps(lows[...])):
            rows[:, i * C : (i + 1) * C] = tap
        z[...] = times_transposed(rows[...], wb[...])

        def step_body(step, carry, f=f, mean=mean, scale=scale):
            base = pl.multiple_of(step * STEP, STEP)
            here = pl.ds(base, STEP)
            right = jnp.where(edge == W - 1, 0.0, pltpu.roll(z[here, 0:C], STEP - 1, 0))
            left = jnp.where(edge == 0, 0.0, pltpu.roll(z[here, 2 * PAD : 2 * PAD + C], 1, 0))
            acts_grad = right + z[here, PAD : PAD + C] + left
            hat = (x_ref[pl.ds(base + f * PIX, STEP), :].astype(F32) - mean) * scale
            pre = hat * gain
            s = sigmoid(pre)
            dhat = acts_grad * (s * (1.0 + pre * (1.0 - s))) * gain
            dh[here, :] = dhat
            return carry[0] + fold(dhat), carry[1] + fold(dhat * hat)

        zero = jnp.zeros((8, C), F32)
        sums = lax.fori_loop(0, half, step_body, (zero, zero))
        grouped = group_sum(four(*sums)) * (1.0 / (PIX * C // GROUPS))
        first, second = grouped[0:1], grouped[1:2]

        def last_body(step, carry, f=f, mean=mean, scale=scale, first=first, second=second):
            base = pl.multiple_of(step * STEP, STEP)
            there = pl.ds(base + f * PIX, STEP)
            hat = (x_ref[there, :].astype(F32) - mean) * scale
            here = pl.ds(base, STEP)
            value = grads[here, :] + scale * (dh[here, :] - first - hat * second)
            out_ref[there, :] = value.astype(BF16)
            return carry

        lax.fori_loop(0, half, last_body, 0)


def input_gradient(part, h0, h1, clip_stat, total, x, stat, weight):
    return call(
        input_grad_body,
        shape((ROWS, C), BF16),
        (
            pltpu.VMEM((3 * PAD, 3 * C), BF16),
            pltpu.VMEM((PIX, 3 * C), BF16),
            pltpu.VMEM((PIX, 3 * PAD), F32),
            pltpu.VMEM((PIX, C), F32),
            pltpu.VMEM((PIX, C), F32),
            pltpu.VMEM((PIX, C), BF16),
            pltpu.VMEM((8, C), F32),
            pltpu.VMEM((8, C), F32),
            pltpu.VMEM((8, C), F32),
            pltpu.VMEM((9, C, C), BF16),
            pltpu.SemaphoreType.DMA((4,)),
        ),
        flops=2_500_000_000,
        limit=18,
        ins=[VMEM] * 3 + [FAR] * 2 + [VMEM] + [FAR] * 2,
        outs=VMEM,
    )(part, h0, h1, in_hbm(clip_stat), in_hbm(total), x, in_hbm(stat), in_hbm(weight))


def unpack_body(mine_ref, other_ref, far_spatial_ref, far_temporal_ref, taps, sem):
    core = lax.axis_index("c")
    sends = []
    for j in range(3):
        here = slice(j * C, (j + 1) * C)
        mine, other = mine_ref[here, :], other_ref[here, :]
        left = jnp.where(core == 0, mine, other)
        right = jnp.where(core == 0, other, mine)
        for i in range(4):
            n = 3 * i + j
            lanes = slice(i * HALF, (i + 1) * HALF)
            taps[n, :, 0:HALF] = left[:, lanes]
            taps[n, :, HALF:C] = right[:, lanes]
            target = far_spatial_ref.at[n] if i < 3 else far_temporal_ref.at[j]
            send = pltpu.make_async_copy(taps.at[n], target, sem.at[n])
            send.start()
            sends.append(send)
    for send in sends:
        send.wait()


def unpack(mine, other):
    return call(
        unpack_body,
        (far((9, C, C), BF16), far((3, C, C), BF16)),
        (pltpu.VMEM((12, C, C), BF16), pltpu.SemaphoreType.DMA((12,))),
        ins=[VMEM] * 2,
        outs=(FAR, FAR),
    )(mine, other)


def neighbours(first, second):
    size = lax.axis_size(FRAME)
    before = lax.ppermute(second, FRAME, [(i, i + 1) for i in range(size - 1)])
    after = lax.ppermute(first, FRAME, [(i + 1, i) for i in range(size - 1)])
    return before, after


def swap_cores(value):
    return lax.ppermute(value, "c", [(0, 1), (1, 0)])


def everyone_total(value):
    plane = lax.axis_size(PLANE)
    value = value.reshape(plane, 1024 // plane, value.shape[1])
    return lax.all_to_all(value, PLANE, 0, 0)


def everyone_share(value, beside):
    plane, line = lax.axis_size(PLANE), lax.axis_size(LINE)
    width = value.shape[2]
    value = jnp.sum(value.astype(F32), axis=0)
    value = value.reshape(line, 1024 // plane // line, width)
    value = jnp.sum(lax.all_to_all(value, LINE, 0, 0), axis=0).astype(BF16)
    value, *beside = lax.optimization_barrier((value, *beside))
    value = jnp.broadcast_to(value[None], (line,) + value.shape)
    return beside, lax.all_to_all(value, LINE, 0, 0).reshape(1024 // plane, width)


def everyone_gets(value):
    plane = lax.axis_size(PLANE)
    value = jnp.broadcast_to(value[None], (plane,) + value.shape)
    return lax.all_to_all(value, PLANE, 0, 0).reshape(1024, value.shape[2])


def on_device(clips, cotangent, spatial_weight, temporal_weight, gain_one, gain_two):
    size = lax.axis_size(FRAME)
    count = float(size * ROWS * C // GROUPS)
    x = clips.reshape(ROWS, C)
    cot = cotangent.reshape(ROWS, C)
    spatial_weight = spatial_weight.reshape(9, C, C)
    barrier = lax.optimization_barrier
    cot_before, cot_after = neighbours(cot[:PIX], cot[PIX:])
    h0, h1, mine_turned, stat_one, sums = forward(x, spatial_weight, gain_one, size)
    sums = lax.all_to_all(sums, FRAME, 0, 0)
    mixed_grad = mixed_gradient(cot_before, cot, cot_after, temporal_weight)
    sums, mine_turned, mixed_grad = barrier((sums, mine_turned, mixed_grad))
    other_turned = swap_cores(mine_turned)
    part, clip_stat, sums, far_stat = slopes(sums, h0, h1, mixed_grad, cot, gain_two, count)
    sums = lax.all_to_all(sums, FRAME, 0, 0)
    temporal_keep, temporal_give = temporal_gradient(
        h0, h1, cot_before, cot, cot_after, clip_stat
    )
    sums, temporal_give = barrier((sums, temporal_give))
    temporal_got = swap_cores(temporal_give)
    low_keep, low_give, total = hidden_gradient(sums, clip_stat, part, h0, h1, count)
    low_got = swap_cores(low_give)
    packed = weight_gradients(
        mine_turned, other_turned, low_keep, low_got, temporal_keep, temporal_got
    )
    packed, total, edge0, edge1 = barrier((packed, total, h0, h1))
    shares = everyone_total(packed)
    before, after = neighbours(edge0, edge1)
    input_grad = input_gradient(
        part, h0, h1, far_stat, total, x, stat_one, spatial_weight
    )
    shares, input_grad = barrier((shares, input_grad))
    (before, after), mine = everyone_share(shares, (before, after))
    mine, before, after = barrier((mine, before, after))
    output = temporal(before, h0, h1, after, far_stat, temporal_weight)
    mine, output = barrier((everyone_gets(mine), output))
    other = swap_cores(mine)
    spatial_grad, temporal_grad = unpack(mine, other)
    return (
        output.reshape(clips.shape),
        input_grad.reshape(clips.shape),
        spatial_grad.reshape(3, 3, C, C),
        temporal_grad,
    )


def solution(mesh):
    fine = Mesh(mesh.devices.reshape(2, 4, 2, 4, 4), ("zl", "x", "c", "y", "zh"))
    return jax.shard_map(
        on_device,
        mesh=fine,
        in_specs=(P(DP, FRAME), P(DP, FRAME), P(), P(), P(), P()),
        out_specs=(P(DP, FRAME), P(DP, FRAME), P(), P()),
        check_vma=False,
    )
```

```python
import functools

import jax
import jax.numpy as jnp
from jax import lax
from jax.experimental import pallas as pl
from jax.experimental.pallas import tpu as pltpu
from jax.sharding import Mesh, PartitionSpec as P

epsilon = 1e-05

GROUPS = 32
DP = ("zl", "x", "c")
FRAME = ("y", "zh")
PLANE = ("x", "y")
LINE = ("zl", "zh")

C = 320
W = 32
PAD = 384
HALF = C // 2
PIX = 512
ROWS = 2 * PIX
STEP = 128
F32 = jnp.float32
BF16 = jnp.bfloat16

MIB = 1024 * 1024


VMEM = pl.BlockSpec(memory_space=pltpu.VMEM)
FAR = pl.BlockSpec(memory_space=pltpu.HBM)


def call(body, out, scratch=(), flops=0, limit=12, ins=None, outs=None):
    specs = {}
    if ins is not None:
        specs = {"in_specs": ins, "out_specs": outs}
    return pl.pallas_call(
        body,
        out_shape=out,
        scratch_shapes=list(scratch),
        compiler_params=pltpu.CompilerParams(vmem_limit_bytes=limit * MIB),
        cost_estimate=pl.CostEstimate(flops=flops, transcendentals=0, bytes_accessed=8_000_000),
        **specs,
    )


def shape(dims, kind):
    return jax.ShapeDtypeStruct(dims, kind)


def far(dims, kind):
    return pltpu.HBM(dims, kind)


def in_hbm(value):
    return pltpu.with_memory_space_constraint(value, pltpu.HBM)


def at(step, size=STEP):
    return pl.ds(pl.multiple_of(step * size, size), size)


def group_sum(rows):
    per = C // GROUPS
    one = lax.broadcasted_iota(jnp.int32, (C, C), 0) * 6554 >> 16
    two = lax.broadcasted_iota(jnp.int32, (C, C), 1) * 6554 >> 16
    assert per == 10
    same = jnp.where(one == two, 1.0, 0.0).astype(F32)
    return jnp.dot(rows, same, precision=lax.Precision.HIGHEST, preferred_element_type=F32)


def fold(value):
    return jnp.sum(value.reshape(value.shape[0] // 8, 8, value.shape[1]), axis=0)


def column(width):
    return lax.broadcasted_iota(jnp.int32, (STEP, width), 0) & (W - 1)


def four(*sums):
    return jnp.concatenate([jnp.sum(s, axis=0, keepdims=True) for s in sums] + [jnp.zeros((8 - len(sums), C), F32)])


def sigmoid(value):
    return 1.0 / (1.0 + jnp.exp(-value))


def forward_body(
    x_ref, far_w_ref, gain_ref, h0_ref, h1_ref, far_turned_ref, far_stat_ref, sums_ref,
    w_ref, wf, x3, y, turned, stat_ref, w_sem, turned_sem, stat_sem,
):
    fetch = pltpu.make_async_copy(far_w_ref, w_ref, w_sem)
    fetch.start()
    zero = jnp.zeros((8, C), F32)

    def moments(step, carry):
        value = x_ref[at(step), :].astype(F32)
        return carry[0] + fold(value), carry[1] + fold(value * value)

    half = PIX // STEP
    s0, q0 = lax.fori_loop(0, half, moments, (zero, zero))
    s1, q1 = lax.fori_loop(half, 2 * half, moments, (zero, zero))
    grouped = group_sum(four(s0, q0, s1, q1)) * (1.0 / (PIX * C // GROUPS))
    stats = []
    for f in range(2):
        mean = grouped[2 * f : 2 * f + 1]
        var = grouped[2 * f + 1 : 2 * f + 2] - mean * mean
        stats += [mean, lax.rsqrt(var + epsilon)]
    gain = gain_ref[...].reshape(1, C)
    stat_ref[...] = jnp.concatenate([*stats, gain, jnp.zeros((3, C), F32)])
    sends = [pltpu.make_async_copy(stat_ref, far_stat_ref, stat_sem)]
    sends[0].start()
    edge = column(C)

    def activate(step, mean, scale):
        value = x_ref[at(step), :].astype(F32)
        pre = (value - mean) * scale * gain
        act = pre / (1.0 + jnp.exp(-pre))
        low = act.astype(BF16)
        act = low.astype(F32)
        x3[at(step), 0:C] = jnp.where(edge == 0, 0.0, pltpu.roll(act, 1, 0)).astype(BF16)
        x3[at(step), C : 2 * C] = low
        x3[at(step), 2 * C : 3 * C] = jnp.where(
            edge == W - 1, 0.0, pltpu.roll(act, STEP - 1, 0)
        ).astype(BF16)

    def act_step(step, carry):
        activate(step, stats[0], stats[1])
        return carry

    lax.fori_loop(0, half, act_step, 0)
    fetch.wait()
    for i in range(3):
        for j in range(3):
            wf[C * j : C * (j + 1), PAD * i : PAD * i + C] = w_ref[3 * i + j]

    def product(f):
        y[f, 0:W, :] = jnp.zeros((W, 3 * PAD), F32)
        y[f, W + PIX : 2 * W + PIX, :] = jnp.zeros((W, 3 * PAD), F32)
        y[f, W : W + PIX, :] = jnp.dot(
            x3[f * PIX : (f + 1) * PIX, :], wf[...], preferred_element_type=F32
        )

    def turn_frame(f):
        turn(x3[f * PIX : (f + 1) * PIX, C : 2 * C], turned.at[f])
        send = pltpu.make_async_copy(
            turned.at[f], far_turned_ref.at[:, f * PIX : (f + 1) * PIX], turned_sem.at[f]
        )
        send.start()
        sends.append(send)

    def finish(f, h_ref, base, carry):
        conv = (
            y[f, pl.ds(base, STEP), 0:C]
            + y[f, pl.ds(base + W, STEP), PAD : PAD + C]
            + y[f, pl.ds(base + 2 * W, STEP), 2 * PAD : 2 * PAD + C]
        )
        value = x_ref[pl.ds(base + f * PIX, STEP), :].astype(F32)
        low = (value + conv).astype(BF16)
        h_ref[pl.ds(base, STEP), :] = low
        value = low.astype(F32)
        return carry[0] + fold(value), carry[1] + fold(value * value)

    product(0)
    for step in range(half, 2 * half):
        activate(step, stats[2], stats[3])
    turn_frame(0)
    product(1)
    total = (zero, zero)
    for step in range(half):
        total = finish(0, h0_ref, step * STEP, total)
    turn_frame(1)

    def last_step(step, carry):
        return finish(1, h1_ref, pl.multiple_of(step * STEP, STEP), carry)

    total = lax.fori_loop(0, half, last_step, total)
    spread(total, sums_ref)
    for send in sends:
        send.wait()


def spread(total, sums_ref):
    first = jnp.sum(total[0], axis=0, keepdims=True)
    second = jnp.sum(total[1], axis=0, keepdims=True)
    both = jnp.concatenate([first, second])
    for k in range(sums_ref.shape[0]):
        sums_ref[k] = both


def turn(acts, out_ref):
    rows = lax.broadcasted_iota(jnp.int32, (C, C), 0)
    same = jnp.where(rows == lax.broadcasted_iota(jnp.int32, (C, C), 1), 1.0, 0.0).astype(BF16)
    lane = lax.broadcasted_iota(jnp.int32, (C, STEP), 1) & (W - 1)
    moved = times_transposed(same, acts)
    for step in range(PIX // STEP):
        part = moved[:, step * STEP : (step + 1) * STEP]
        where = slice(step * STEP, (step + 1) * STEP)
        out_ref[0:C, where] = jnp.where(lane == 0, 0.0, pltpu.roll(part, 1, 1)).astype(BF16)
        out_ref[C : 2 * C, where] = part.astype(BF16)
        out_ref[2 * C : 3 * C, where] = jnp.where(
            lane == W - 1, 0.0, pltpu.roll(part, STEP - 1, 1)
        ).astype(BF16)


def forward(x, weight, gain, peers):
    return call(
        forward_body,
        (
            shape((PIX, C), BF16),
            shape((PIX, C), BF16),
            far((3 * C, ROWS), BF16),
            far((8, C), F32),
            shape((peers, 2, C), F32),
        ),
        (
            pltpu.VMEM((9, C, C), BF16),
            pltpu.VMEM((3 * C, 3 * PAD), BF16),
            pltpu.VMEM((ROWS, 3 * C), BF16),
            pltpu.VMEM((2, PIX + 2 * W, 3 * PAD), F32),
            pltpu.VMEM((2, 3 * C, PIX), BF16),
            pltpu.VMEM((8, C), F32),
            pltpu.SemaphoreType.DMA,
            pltpu.SemaphoreType.DMA((2,)),
            pltpu.SemaphoreType.DMA,
        ),
        flops=2_500_000_000,
        limit=24,
        ins=[VMEM, FAR, VMEM],
        outs=(VMEM, VMEM, FAR, FAR, VMEM),
    )(x, in_hbm(weight), gain)


def times_transposed(a, b):
    return lax.dot_general(a, b, (((1,), (1,)), ((), ())), preferred_element_type=F32)


def clip_stats(sums_ref, count):
    total = jnp.sum(sums_ref[...], axis=0)
    grouped = group_sum(jnp.concatenate([total, jnp.zeros((6, C), F32)])) * (1.0 / count)
    return grouped[0:1], grouped[1:2]


def mixed_grad_body(
    far_before_ref, cot_ref, far_after_ref, w_ref, far_ref, out_ref, sem, before_ref, after_ref, halo_sem
):
    fetches = [
        pltpu.make_async_copy(far_before_ref, before_ref, halo_sem.at[0]),
        pltpu.make_async_copy(far_after_ref, after_ref, halo_sem.at[1]),
    ]
    for fetch in fetches:
        fetch.start()
    for fetch in fetches:
        fetch.wait()
    sends = []
    for f in range(2):
        here = slice(f * PIX, (f + 1) * PIX)
        last = cot_ref[0:PIX, :] if f else before_ref[...]
        later = after_ref[...] if f else cot_ref[PIX:ROWS, :]
        total = times_transposed(later, w_ref[0])
        total = total + times_transposed(cot_ref[here, :], w_ref[1])
        total = total + times_transposed(last, w_ref[2])
        out_ref[here, :] = total.astype(BF16)
        send = pltpu.make_async_copy(out_ref.at[here, :], far_ref.at[here, :], sem.at[f])
        send.start()
        sends.append(send)
    for send in sends:
        send.wait()


def mixed_gradient(before, cot, after, weight):
    return call(
        mixed_grad_body,
        far((ROWS, C), BF16),
        (pltpu.VMEM((ROWS, C), BF16), pltpu.SemaphoreType.DMA((2,)), pltpu.VMEM((PIX, C), BF16), pltpu.VMEM((PIX, C), BF16), pltpu.SemaphoreType.DMA((2,))),
        flops=1_500_000_000,
        ins=[FAR, VMEM, FAR, VMEM],
        outs=FAR,
    )(in_hbm(before), cot, in_hbm(after), weight)


def slope_body(
    count, sums_ref, h0_ref, h1_ref, far_grad_ref, cot_ref, gain_ref,
    part_ref, stat_ref, out_ref, far_stat_ref, grad_ref, sem, grad_sem,
):
    fetch = pltpu.make_async_copy(far_grad_ref, grad_ref, grad_sem)
    fetch.start()
    mean, square = clip_stats(sums_ref, count)
    scale = lax.rsqrt(square - mean * mean + epsilon)
    gain = gain_ref[...].reshape(1, C)
    stat_ref[...] = jnp.concatenate([mean, scale, gain, jnp.zeros((5, C), F32)])
    send = pltpu.make_async_copy(stat_ref, far_stat_ref, sem)
    send.start()
    fetch.wait()
    zero = jnp.zeros((8, C), F32)
    total = (zero, zero)
    for f, h_ref in enumerate((h0_ref, h1_ref)):

        def step_body(step, carry, f=f, h_ref=h_ref):
            base = pl.multiple_of(step * STEP, STEP)
            there = pl.ds(base + f * PIX, STEP)
            hat = (h_ref[pl.ds(base, STEP), :].astype(F32) - mean) * scale
            pre = hat * gain
            s = sigmoid(pre)
            slope = s * (1.0 + pre * (1.0 - s))
            dhat = grad_ref[there, :].astype(F32) * slope * gain
            part_ref[there, :] = cot_ref[there, :].astype(F32) + scale * dhat
            return carry[0] + fold(dhat), carry[1] + fold(dhat * hat)

        total = lax.fori_loop(0, PIX // STEP, step_body, total)
    spread(total, out_ref)
    send.wait()


def slopes(sums, h0, h1, grad, cot, gain, count):
    return call(
        functools.partial(slope_body, count),
        (shape((ROWS, C), F32), shape((8, C), F32), shape(sums.shape, F32), far((8, C), F32)),
        (pltpu.VMEM((ROWS, C), BF16), pltpu.SemaphoreType.DMA, pltpu.SemaphoreType.DMA),
        ins=[VMEM] * 3 + [FAR] + [VMEM] * 2,
        outs=(VMEM, VMEM, VMEM, FAR),
    )(sums, h0, h1, in_hbm(grad), cot, gain)


def mix(h_ref, base, mean, scale, gain):
    pre = (h_ref[pl.ds(base, STEP), :].astype(F32) - mean) * scale * gain
    return pre / (1.0 + jnp.exp(-pre))


def mixed_body(
    h0_ref, h1_ref, far_before_ref, cot_ref, far_after_ref, stat_ref, sums_ref,
    keep_ref, give_ref, turned, before_ref, after_ref, halo_sem,
):
    fetches = [
        pltpu.make_async_copy(far_before_ref, before_ref, halo_sem.at[0]),
        pltpu.make_async_copy(far_after_ref, after_ref, halo_sem.at[1]),
    ]
    for fetch in fetches:
        fetch.start()
    mean, scale, gain = stat_ref[0:1, :], stat_ref[1:2, :], stat_ref[2:3, :]
    for f, h_ref in enumerate((h0_ref, h1_ref)):
        for step in range(PIX // STEP):
            act = mix(h_ref, step * STEP, mean, scale, gain).astype(BF16)
            turned[:, f * PIX + step * STEP : f * PIX + (step + 1) * STEP] = act.T
    core = lax.axis_index("c")
    for fetch in fetches:
        fetch.wait()
    first, second = turned[:, 0:PIX], turned[:, PIX:ROWS]
    for k in range(3):
        if k == 1:
            part = jnp.dot(turned[...], cot_ref[...], preferred_element_type=F32)
        else:
            one = cot_ref[PIX:ROWS, :] if k == 0 else before_ref[...]
            two = after_ref[...] if k == 0 else cot_ref[0:PIX, :]
            part = jnp.dot(first, one, preferred_element_type=F32)
            part = part + jnp.dot(second, two, preferred_element_type=F32)
        left, right = part[:, 0:HALF], part[:, HALF:C]
        keep_ref[k * C : (k + 1) * C, 0:HALF] = jnp.where(core == 0, left, right)
        give_ref[k * C : (k + 1) * C, 0:HALF] = jnp.where(core == 0, right, left)


def temporal_gradient(h0, h1, before, cot, after, stat, sums):
    return call(
        mixed_body,
        (shape((3 * C, 256), F32), shape((3 * C, 256), F32)),
        (pltpu.VMEM((C, ROWS), BF16), pltpu.VMEM((PIX, C), BF16), pltpu.VMEM((PIX, C), BF16), pltpu.SemaphoreType.DMA((2,))),
        flops=1_500_000_000,
        ins=[VMEM] * 2 + [FAR, VMEM, FAR] + [VMEM] * 2,
        outs=(VMEM, VMEM),
    )(h0, h1, in_hbm(before), cot, in_hbm(after), stat, sums)


def temporal_body(
    hb_ref, h0_ref, h1_ref, ha_ref, far_stat_ref, w_ref, out_ref, mx_ref, stat_ref, sem
):
    fetch = pltpu.make_async_copy(far_stat_ref, stat_ref, sem)
    fetch.start()
    fetch.wait()
    mean, scale, gain = stat_ref[0:1, :], stat_ref[1:2, :], stat_ref[2:3, :]
    place = lax.axis_index(FRAME)
    live = (place > 0, None, None, place < lax.axis_size(FRAME) - 1)
    for n, h_ref in enumerate((hb_ref, h0_ref, h1_ref, ha_ref)):

        def step_body(step, carry, n=n, h_ref=h_ref):
            base = pl.multiple_of(step * STEP, STEP)
            act = mix(h_ref, base, mean, scale, gain)
            if live[n] is not None:
                act = jnp.where(live[n], act, 0.0)
            mx_ref[pl.ds(base + n * PIX, STEP), :] = act.astype(BF16)
            return carry

        lax.fori_loop(0, PIX // STEP, step_body, 0)
    for f, h_ref in enumerate((h0_ref, h1_ref)):
        total = None
        for k in range(3):
            part = jnp.dot(
                mx_ref[(f + k) * PIX : (f + k + 1) * PIX, :],
                w_ref[k],
                preferred_element_type=F32,
            )
            total = part if total is None else total + part
        low = total.astype(BF16).astype(F32)
        out_ref[f * PIX : (f + 1) * PIX, :] = (h_ref[...].astype(F32) + low).astype(BF16)


def temporal(before, h0, h1, after, stat, weight):
    return call(
        temporal_body,
        shape((ROWS, C), BF16),
        (pltpu.VMEM((4 * PIX, C), BF16), pltpu.VMEM((8, C), F32), pltpu.SemaphoreType.DMA),
        flops=1_500_000_000,
        ins=[VMEM] * 4 + [FAR, VMEM],
        outs=VMEM,
    )(before, h0, h1, after, in_hbm(stat), weight)


def whole_grad(part_ref, h_ref, stat_ref, sums, base, f):
    mean, scale = stat_ref[0:1, :], stat_ref[1:2, :]
    hat = (h_ref[pl.ds(base, STEP), :].astype(F32) - mean) * scale
    return part_ref[pl.ds(base + f * PIX, STEP), :] - scale * (sums[0] + hat * sums[1])


def hidden_grad_body(
    count, sums_ref, stat_ref, part_ref, h0_ref, h1_ref,
    keep_ref, give_ref, far_total_ref, total_ref, sem,
):
    sums = clip_stats(sums_ref, count)
    total_ref[...] = jnp.concatenate([*sums, jnp.zeros((6, C), F32)])
    send = pltpu.make_async_copy(total_ref, far_total_ref, sem)
    send.start()
    core = lax.axis_index("c")
    for f, h_ref in enumerate((h0_ref, h1_ref)):

        def step_body(step, carry, f=f, h_ref=h_ref):
            base = pl.multiple_of(step * STEP, STEP)
            here = pl.ds(base + f * PIX, STEP)
            grad = whole_grad(part_ref, h_ref, stat_ref, sums, base, f)
            left, right = grad[:, 0:HALF], grad[:, HALF:C]
            keep_ref[here, :] = jnp.where(core == 0, left, right).astype(BF16)
            give_ref[here, :] = jnp.where(core == 0, right, left).astype(BF16)
            return carry

        lax.fori_loop(0, PIX // STEP, step_body, 0)
    send.wait()


def hidden_gradient(sums, stat, part, h0, h1, count):
    return call(
        functools.partial(hidden_grad_body, count),
        (shape((ROWS, HALF), BF16), shape((ROWS, HALF), BF16), far((8, C), F32)),
        (pltpu.VMEM((8, C), F32), pltpu.SemaphoreType.DMA),
        ins=[VMEM] * 5,
        outs=(VMEM, VMEM, FAR),
    )(sums, stat, part, h0, h1)


def row_taps(value):
    none = jnp.zeros((W, value.shape[1]), value.dtype)
    return (
        jnp.concatenate([value[W:], none]),
        value,
        jnp.concatenate([none, value[: PIX - W]]),
    )


def weight_grad_body(
    mine_turned_ref, other_turned_ref, mine_ref, other_ref, keep_ref, got_ref, far_ref, rhs, out, sem
):
    for n, ref in enumerate((mine_ref, other_ref)):
        for f in range(2):
            where = slice(f * PIX, (f + 1) * PIX)
            for i, tap in enumerate(row_taps(ref[where, :])):
                rhs[n, where, i * HALF : (i + 1) * HALF] = tap
    sends = []
    for j in range(3):
        here = slice(j * C, (j + 1) * C)
        total = jnp.dot(mine_turned_ref[here, :], rhs[0], preferred_element_type=F32)
        total = total + jnp.dot(other_turned_ref[here, :], rhs[1], preferred_element_type=F32)
        out[here, 0 : 3 * HALF] = total.astype(BF16)
        kept = keep_ref[here, 0:HALF] + got_ref[here, 0:HALF]
        out[here, 3 * HALF : 4 * HALF] = kept.astype(BF16)
        if j == 2:
            out[3 * C :, :] = jnp.zeros((1024 - 3 * C, 4 * HALF), BF16)
            here = slice(j * C, 1024)
        send = pltpu.make_async_copy(out.at[here, :], far_ref.at[here, :], sem.at[j])
        send.start()
        sends.append(send)
    for send in sends:
        send.wait()


def weight_gradients(mine_turned, other_turned, mine, other, keep, got):
    return call(
        weight_grad_body,
        far((1024, 4 * HALF), BF16),
        (
            pltpu.VMEM((2, ROWS, 3 * HALF), BF16),
            pltpu.VMEM((1024, 4 * HALF), BF16),
            pltpu.SemaphoreType.DMA((3,)),
        ),
        flops=2_500_000_000,
        ins=[VMEM] * 6,
        outs=FAR,
    )(mine_turned, other_turned, mine, other, keep, got)


def input_grad_body(
    part_ref, h0_ref, h1_ref, far_clip_ref, far_total_ref, x_ref, far_stat_ref, far_w_ref,
    out_ref, wb, rows, z, dh, grads, lows, clip_ref, total_ref, stat_ref, w_ref, sem,
):
    pairs = (far_clip_ref, clip_ref), (far_total_ref, total_ref), (far_stat_ref, stat_ref)
    fetches = [
        pltpu.make_async_copy(one, two, sem.at[n])
        for n, (one, two) in enumerate((*pairs, (far_w_ref, w_ref)))
    ]
    for fetch in fetches:
        fetch.start()
    for fetch in fetches[:3]:
        fetch.wait()
    clip_sums = total_ref[0:1, :], total_ref[1:2, :]
    gain = stat_ref[4:5, :]
    edge = column(C)
    half = PIX // STEP
    for f in range(2):
        mean, scale = stat_ref[2 * f : 2 * f + 1, :], stat_ref[2 * f + 1 : 2 * f + 2, :]
        h_ref = (h0_ref, h1_ref)[f]

        def grad_body(step, carry, f=f, h_ref=h_ref):
            base = pl.multiple_of(step * STEP, STEP)
            grad = whole_grad(part_ref, h_ref, clip_ref, clip_sums, base, f)
            grads[pl.ds(base, STEP), :] = grad
            lows[pl.ds(base, STEP), :] = grad.astype(BF16)
            return carry

        lax.fori_loop(0, half, grad_body, 0)
        if f == 0:
            fetches[3].wait()
            for j in range(3):
                for i in range(3):
                    wb[PAD * j : PAD * j + C, C * i : C * (i + 1)] = w_ref[3 * i + j]
                wb[PAD * j + C : PAD * (j + 1), :] = jnp.zeros((PAD - C, 3 * C), BF16)
        for i, tap in enumerate(row_taps(lows[...])):
            rows[:, i * C : (i + 1) * C] = tap
        z[...] = times_transposed(rows[...], wb[...])

        def step_body(step, carry, f=f, mean=mean, scale=scale):
            base = pl.multiple_of(step * STEP, STEP)
            here = pl.ds(base, STEP)
            right = jnp.where(edge == W - 1, 0.0, pltpu.roll(z[here, 0:C], STEP - 1, 0))
            left = jnp.where(edge == 0, 0.0, pltpu.roll(z[here, 2 * PAD : 2 * PAD + C], 1, 0))
            acts_grad = right + z[here, PAD : PAD + C] + left
            hat = (x_ref[pl.ds(base + f * PIX, STEP), :].astype(F32) - mean) * scale
            pre = hat * gain
            s = sigmoid(pre)
            dhat = acts_grad * (s * (1.0 + pre * (1.0 - s))) * gain
            dh[here, :] = dhat
            return carry[0] + fold(dhat), carry[1] + fold(dhat * hat)

        zero = jnp.zeros((8, C), F32)
        sums = lax.fori_loop(0, half, step_body, (zero, zero))
        grouped = group_sum(four(*sums)) * (1.0 / (PIX * C // GROUPS))
        first, second = grouped[0:1], grouped[1:2]

        def last_body(step, carry, f=f, mean=mean, scale=scale, first=first, second=second):
            base = pl.multiple_of(step * STEP, STEP)
            there = pl.ds(base + f * PIX, STEP)
            hat = (x_ref[there, :].astype(F32) - mean) * scale
            here = pl.ds(base, STEP)
            value = grads[here, :] + scale * (dh[here, :] - first - hat * second)
            out_ref[there, :] = value.astype(BF16)
            return carry

        lax.fori_loop(0, half, last_body, 0)


def input_gradient(part, h0, h1, clip_stat, total, x, stat, weight):
    return call(
        input_grad_body,
        shape((ROWS, C), BF16),
        (
            pltpu.VMEM((3 * PAD, 3 * C), BF16),
            pltpu.VMEM((PIX, 3 * C), BF16),
            pltpu.VMEM((PIX, 3 * PAD), F32),
            pltpu.VMEM((PIX, C), F32),
            pltpu.VMEM((PIX, C), F32),
            pltpu.VMEM((PIX, C), BF16),
            pltpu.VMEM((8, C), F32),
            pltpu.VMEM((8, C), F32),
            pltpu.VMEM((8, C), F32),
            pltpu.VMEM((9, C, C), BF16),
            pltpu.SemaphoreType.DMA((4,)),
        ),
        flops=2_500_000_000,
        limit=18,
        ins=[VMEM] * 3 + [FAR] * 2 + [VMEM] + [FAR] * 2,
        outs=VMEM,
    )(part, h0, h1, in_hbm(clip_stat), in_hbm(total), x, in_hbm(stat), in_hbm(weight))


def unpack_body(mine_ref, other_ref, far_spatial_ref, far_temporal_ref, taps, sem):
    core = lax.axis_index("c")
    sends = []
    for j in range(3):
        here = slice(j * C, (j + 1) * C)
        mine, other = mine_ref[here, :], other_ref[here, :]
        left = jnp.where(core == 0, mine, other)
        right = jnp.where(core == 0, other, mine)
        for i in range(4):
            n = 3 * i + j
            lanes = slice(i * HALF, (i + 1) * HALF)
            taps[n, :, 0:HALF] = left[:, lanes]
            taps[n, :, HALF:C] = right[:, lanes]
            target = far_spatial_ref.at[n] if i < 3 else far_temporal_ref.at[j]
            send = pltpu.make_async_copy(taps.at[n], target, sem.at[n])
            send.start()
            sends.append(send)
    for send in sends:
        send.wait()


def unpack(mine, other):
    return call(
        unpack_body,
        (far((9, C, C), BF16), far((3, C, C), BF16)),
        (pltpu.VMEM((12, C, C), BF16), pltpu.SemaphoreType.DMA((12,))),
        ins=[VMEM] * 2,
        outs=(FAR, FAR),
    )(mine, other)


def neighbours(first, second):
    size = lax.axis_size(FRAME)
    before = lax.ppermute(second, FRAME, [(i, i + 1) for i in range(size - 1)])
    after = lax.ppermute(first, FRAME, [(i + 1, i) for i in range(size - 1)])
    return before, after


def swap_cores(value):
    return lax.ppermute(value, "c", [(0, 1), (1, 0)])


def everyone_total(value):
    plane = lax.axis_size(PLANE)
    value = value.reshape(plane, 1024 // plane, value.shape[1])
    return lax.all_to_all(value, PLANE, 0, 0)


def everyone_share(value, beside):
    plane, line = lax.axis_size(PLANE), lax.axis_size(LINE)
    width = value.shape[2]
    value = jnp.sum(value.astype(F32), axis=0)
    value = value.reshape(line, 1024 // plane // line, width)
    value = jnp.sum(lax.all_to_all(value, LINE, 0, 0), axis=0).astype(BF16)
    value, *beside = lax.optimization_barrier((value, *beside))
    value = jnp.broadcast_to(value[None], (line,) + value.shape)
    return beside, lax.all_to_all(value, LINE, 0, 0).reshape(1024 // plane, width)


def everyone_gets(value):
    plane = lax.axis_size(PLANE)
    value = jnp.broadcast_to(value[None], (plane,) + value.shape)
    return lax.all_to_all(value, PLANE, 0, 0).reshape(1024, value.shape[2])


def on_device(clips, cotangent, spatial_weight, temporal_weight, gain_one, gain_two):
    size = lax.axis_size(FRAME)
    count = float(size * ROWS * C // GROUPS)
    x = clips.reshape(ROWS, C)
    cot = cotangent.reshape(ROWS, C)
    spatial_weight = spatial_weight.reshape(9, C, C)
    barrier = lax.optimization_barrier
    cot_before, cot_after = neighbours(cot[:PIX], cot[PIX:])
    h0, h1, mine_turned, stat_one, sums = forward(x, spatial_weight, gain_one, size)
    sums = lax.all_to_all(sums, FRAME, 0, 0)
    mixed_grad = mixed_gradient(cot_before, cot, cot_after, temporal_weight)
    sums, mine_turned, mixed_grad = barrier((sums, mine_turned, mixed_grad))
    other_turned = swap_cores(mine_turned)
    part, clip_stat, sums, far_stat = slopes(sums, h0, h1, mixed_grad, cot, gain_two, count)
    sums = lax.all_to_all(sums, FRAME, 0, 0)
    temporal_keep, temporal_give = temporal_gradient(
        h0, h1, cot_before, cot, cot_after, clip_stat, sums
    )
    temporal_got = swap_cores(temporal_give)
    low_keep, low_give, total = hidden_gradient(sums, clip_stat, part, h0, h1, count)
    low_got = swap_cores(low_give)
    packed = weight_gradients(
        mine_turned, other_turned, low_keep, low_got, temporal_keep, temporal_got
    )
    packed, total, edge0, edge1 = barrier((packed, total, h0, h1))
    shares = everyone_total(packed)
    before, after = neighbours(edge0, edge1)
    input_grad = input_gradient(
        part, h0, h1, far_stat, total, x, stat_one, spatial_weight
    )
    shares, input_grad = barrier((shares, input_grad))
    (before, after), mine = everyone_share(shares, (before, after))
    mine, before, after = barrier((mine, before, after))
    output = temporal(before, h0, h1, after, far_stat, temporal_weight)
    mine, output = barrier((everyone_gets(mine), output))
    other = swap_cores(mine)
    spatial_grad, temporal_grad = unpack(mine, other)
    return (
        output.reshape(clips.shape),
        input_grad.reshape(clips.shape),
        spatial_grad.reshape(3, 3, C, C),
        temporal_grad,
    )


def solution(mesh):
    fine = Mesh(mesh.devices.reshape(2, 4, 2, 4, 4), ("zl", "x", "c", "y", "zh"))
    return jax.shard_map(
        on_device,
        mesh=fine,
        in_specs=(P(DP, FRAME), P(DP, FRAME), P(), P(), P(), P()),
        out_specs=(P(DP, FRAME), P(DP, FRAME), P(), P()),
        check_vma=False,
    )
```
